32 devices in a mesh: gx: 8 (over z, x), gy: 4 (over y, core).
Axes of the slice: x: 2, y: 2, z: 4, core: 2. Of those that a mesh axis runs over, the one named last changes fastest.
Arguments:
- velocity: float32 [3, 64, 256, 128], P(None, 'gx', 'gy'), may hold values from -2 to 3, as said below
- counts: int32 [8, 4, 9], P('gx', 'gy'), may hold values from 1 to 1024, as said below
- src_cell: int32 [8, 4, 9, 1024], P('gx', 'gy'), may hold values from 0 to 65535
- weights: float32 [8, 4, 9, 1024], P('gx', 'gy'), may hold values from 0.05 to 0.35
- dst_cell: int32 [8, 4, 9, 1024], P('gx', 'gy'), may hold values from 0 to 65535
- blade_tile: int32 [20, 192], replicated, may hold values from 0 to 31, as said below
- blade_cell: int32 [20, 192], replicated, may hold values from 0 to 65535
- blade_coef: float32 [20, 192], replicated, may hold values from 0.5 to 2
Outputs:
- updated: float32 [3, 64, 256, 128], P(None, 'gx', 'gy')
- forcing: float32 [3, 64, 256, 128], P(None, 'gx', 'gy')
The draws below stay inside these ranges and needn't reach their ends.
Inputs may be any that keep to these rules, and one draw needn't show every extreme that they name: The velocity components, streamwise with a mean near 1. `counts`: some list is full, with 1024 used slots. `blade_tile`: turbines stand near one spanwise row of tiles; a turbine's points lie in at most three tiles.
All inputs are finite; a program needn't handle non-finite values.
Results may differ from the reference program's by a relative error of at most 0.00002.
Values sent between devices are 32-bit elements; how exact they have to be, the bound alone decides.
No kernel may reach another device: no remote copies, remote signals or barrier semaphores. Data moves between devices by JAX's collectives and lax.ppermute only.
A program may use at most 256 MiB of HBM per device.

```python
import math
import jax
import jax.numpy as jnp

CX = 8
CY = 64
NZ = 128
CAP = 1024
DIRS = 9
NT = 20
NP = 192
TILES_X = 8
TILES_Y = 4
NX = 64
NY = 256
CELLS = 65536


def draw_velocity(key, part):
    key_noise = jax.random.fold_in(jax.random.fold_in(key, 11), 0)
    noise = jax.random.normal(key_noise, (3, NX, NY, NZ), jnp.float32) * 0.4
    noise = jnp.clip(noise, -1.9, 1.9)
    stream_mean = jnp.array([1.0, 0.0, 0.0], jnp.float32)[:, None, None, None]
    return (stream_mean + noise).astype(jnp.float32)


def draw_counts(key, part):
    key_base, key_slot = jax.random.split(jax.random.fold_in(key, 23))
    total_lists = TILES_X * TILES_Y * DIRS
    drawn = jax.random.randint(key_base, (total_lists,), 1, CAP + 1)
    chosen_slot = jax.random.randint(key_slot, (), 0, total_lists)
    drawn = drawn.at[chosen_slot].set(CAP)
    return drawn.reshape(TILES_X, TILES_Y, DIRS).astype(jnp.int32)


def draw_blade_tile(key, part):
    key_ridge, key_home, key_side, key_cross = jax.random.split(jax.random.fold_in(key, 37), 4)
    ridge_row = jax.random.randint(key_ridge, (), 0, TILES_Y)
    home_x = jax.random.randint(key_home, (NT, 1), 0, TILES_X)
    home_y = (ridge_row + jax.random.randint(key_side, (NT, 1), 0, 2)) % TILES_Y
    outer_blade = (jnp.arange(NP, dtype=jnp.int32) >= 2 * NP // 3).astype(jnp.int32)[None, :]
    crossing = jax.random.randint(key_cross, (NT, NP), 0, 2) * outer_blade
    return (home_x * TILES_Y + (home_y + crossing) % TILES_Y).astype(jnp.int32)


def with_ends(values, rng, least, top_value):
    extent = values.shape
    place = [jax.random.randint(jax.random.fold_in(rng, axis), (), 0, extent[axis]) for axis in range(len(extent))]
    values = values.at[tuple(place)].set(least)
    longest = extent.index(max(extent))
    place[longest] = (place[longest] + 1) % extent[longest]
    return values.at[tuple(place)].set(top_value)


def steps_of(key, extent, pieces, least, largest):
    factor_of = 1.0
    for position, blocks in pieces:
        steps = jax.random.uniform(jax.random.fold_in(jax.random.fold_in(key, 6), position), (blocks,), jnp.float32, least / len(pieces), largest / len(pieces))
        factor_of = factor_of * jnp.repeat(jnp.exp(steps), extent[position] // blocks).reshape((-1,) + (1,) * (len(extent) - 1 - position))
    return factor_of


def setup_inputs(seed: int = 0) -> dict:
    key_list = jax.random.split(jax.random.key(seed), 9)
    return {
        "velocity": draw_velocity(jax.random.fold_in(key_list[8], 71), 0),
        "counts": draw_counts(jax.random.fold_in(key_list[8], 71), 0),
        "src_cell": with_ends(jax.random.randint(key_list[2], (TILES_X, TILES_Y, DIRS, CAP), 0, CELLS), jax.random.fold_in(key_list[2], 1), 0, CELLS - 1).astype(jnp.int32),
        "weights": jnp.clip(0.05 + 0.29999999 * jax.random.uniform(key_list[3], (TILES_X, TILES_Y, DIRS, CAP), jnp.float32) ** steps_of(key_list[3], (TILES_X, TILES_Y, DIRS, CAP), ((0, 8), (1, 4)), -0.2, 0.2), 0.05, 0.35),
        "dst_cell": with_ends(jax.random.randint(key_list[4], (TILES_X, TILES_Y, DIRS, CAP), 0, CELLS), jax.random.fold_in(key_list[4], 1), 0, CELLS - 1).astype(jnp.int32),
        "blade_tile": draw_blade_tile(jax.random.fold_in(key_list[8], 71), 0),
        "blade_cell": with_ends(jax.random.randint(key_list[6], (NT, NP), 0, CELLS), jax.random.fold_in(key_list[6], 1), 0, CELLS - 1).astype(jnp.int32),
        "blade_coef": jnp.clip(jnp.exp(jax.random.uniform(key_list[7], (NT, NP), jnp.float32, math.log(0.5), math.log(2.0))), 0.5, 2.0),
    }


def global_index(tile_x, tile_y, local):
    local_x = local // (CY * NZ)
    local_y = (local // NZ) % CY
    local_z = local % NZ
    return ((tile_x * CX + local_x) * NY + tile_y * CY + local_y) * NZ + local_z


def reference(velocity, counts, src_cell, weights, dst_cell, blade_tile, blade_cell, blade_coef):
    flat_vel = velocity.reshape(3, -1)
    tile_x = jnp.arange(TILES_X, dtype=jnp.int32)[:, None, None, None]
    tile_y = jnp.arange(TILES_Y, dtype=jnp.int32)[None, :, None, None]
    active = jnp.arange(CAP, dtype=jnp.int32)[None, None, None, :] < counts[..., None]
    masked_w = jnp.where(active, weights, jnp.zeros_like(weights))
    source = global_index(tile_x, tile_y, src_cell)
    picked = flat_vel[:, source]
    blocks = jnp.concatenate([picked * masked_w[None], masked_w[None]], axis=0)
    moved = []
    for direction in range(9):
        offset_x = direction // 3 - 1
        offset_y = direction % 3 - 1
        moved.append(jnp.roll(blocks[:, :, :, direction], (offset_x, offset_y), axis=(1, 2)))
    moved = jnp.stack(moved, axis=3)
    targets = global_index(tile_x, tile_y, dst_cell).reshape(-1)
    totals = jnp.zeros((4, flat_vel.shape[1]), jnp.float32).at[:, targets].add(moved.reshape(4, -1))
    corrected = (1.0 - totals[3]) * flat_vel - totals[:3]

    blade_x = blade_tile // TILES_Y
    blade_y = blade_tile % TILES_Y
    blade_index = global_index(blade_x, blade_y, blade_cell)
    sampled = flat_vel[:, blade_index]
    rotor_mean = jnp.sum(sampled[0], axis=1) / NP
    forces = -blade_coef[None] * rotor_mean[None, :, None] * sampled
    forcing = jnp.zeros((3, flat_vel.shape[1]), jnp.float32).at[:, blade_index.reshape(-1)].add(forces.reshape(3, -1))

    field_now = corrected.reshape(3, NX, NY, NZ)
    columns = [field_now[0], field_now[1], field_now[2]]
    outputs = []
    for component in range(3):
        current = columns[component]
        layer = jnp.zeros((NX, NY, 1), current.dtype)
        east_side = jnp.roll(current, -1, 0)
        west_side = jnp.roll(current, 1, 0)
        north_side = jnp.roll(current, -1, 1)
        south_side = jnp.roll(current, 1, 1)
        upper_side = jnp.concatenate([current[:, :, 1:], layer], axis=2)
        lower_side = jnp.concatenate([layer, current[:, :, :-1]], axis=2)
        laplace = east_side + west_side + north_side + south_side + upper_side + lower_side - 6.0 * current
        advection = columns[0] * (east_side - west_side) * 0.5 + columns[1] * (north_side - south_side) * 0.5 + columns[2] * (upper_side - lower_side) * 0.5
        outputs.append(current + 0.2 * (0.15 * laplace - advection + forcing[component].reshape(NX, NY, NZ)))
    return jnp.stack(outputs), forcing.reshape(3, NX, NY, NZ)
```

```python
import functools

import jax
import jax.numpy as jnp
from jax import lax
from jax.experimental import pallas as pl
from jax.experimental.pallas import tpu as pltpu
from jax.sharding import PartitionSpec as P

F32 = jnp.float32
BF16 = jnp.bfloat16
VMEM_SPEC = pl.BlockSpec(memory_space=pltpu.VMEM)
SMEM_SPEC = pl.BlockSpec(memory_space=pltpu.SMEM)
PARAMS = pltpu.CompilerParams(vmem_limit_bytes=48 << 20)


def halves(value):
    high = value.astype(BF16)
    low = (value - high.astype(F32)).astype(BF16)
    return high, low


def one_hot(extent, index):
    rows = lax.broadcasted_iota(jnp.int32, (extent, index.shape[1]), 0)
    return jnp.where(rows == index, 1.0, 0.0).astype(BF16)


def build_table(vel_ref, table):
    half = vel_ref.shape[1] // 2
    for c in range(3):
        for piece in range(2):
            high, low = halves(vel_ref[c, piece * half : (piece + 1) * half, :])
            table[c, :, piece * 128 : (piece + 1) * 128] = high
            table[c, :, 256 + piece * 128 : 256 + (piece + 1) * 128] = low


def pick(table, cell):
    key = (cell & 127) | (((cell >> 15) & 1) << 7)
    place = (cell >> 7) & 255
    hot = one_hot(256, key)
    hot = jnp.concatenate([hot, hot], axis=0)
    here = lax.broadcasted_iota(jnp.int32, (256, cell.shape[1]), 0) == place
    out = []
    for c in range(3):
        found = jnp.dot(table[c], hot, preferred_element_type=F32)
        out.append(jnp.sum(jnp.where(here, found, 0.0), axis=0, keepdims=True))
    return out


def spread(cell, values):
    row = (cell >> 7) & 511
    level = cell & 127
    hot = one_hot(512, row)
    at_level = lax.broadcasted_iota(jnp.int32, (128, cell.shape[1]), 0) == level
    high, low = [], []
    for value in values:
        vh = value.astype(BF16).astype(F32)
        vl = value - vh
        high.append(jnp.where(at_level, vh, 0.0).astype(BF16))
        low.append(jnp.where(at_level, vl, 0.0).astype(BF16))
    left = jnp.concatenate([hot, hot], axis=1)
    right = jnp.concatenate([jnp.concatenate(high, axis=0), jnp.concatenate(low, axis=0)], axis=1)
    return lax.dot_general(left, right, (((1,), (1,)), ((), ())), preferred_element_type=F32)


def active_turbines(tile_ref, mine, listed):
    turbines = tile_ref.shape[0]
    owned = jnp.where(tile_ref[...] == mine, 1.0, 0.0)
    found = jnp.max(owned, axis=1, keepdims=True)
    total = jnp.int32(0)
    for t in range(turbines):
        listed[total] = t
        total = total + jnp.where(found[t, 0] > 0.5, 1, 0)
    return total


def gather_kernel(mine_ref, cnt_ref, vel_ref, src_ref, w_ref, tile_ref, cell_ref, out_ref, pts_ref, rot_ref, table, listed, tlist):
    build_table(vel_ref, table)
    out_ref[...] = jnp.zeros_like(out_ref)
    pts_ref[...] = jnp.zeros_like(pts_ref)
    mine = mine_ref[0]
    n_turb = active_turbines(tile_ref, mine, tlist)
    points = tile_ref.shape[1]

    def turbine(i, carry):
        t = tlist[i]
        owned = tile_ref[pl.ds(t, 1), :] == mine
        rows = pick(table, cell_ref[pl.ds(t, 1), :])
        for c in range(3):
            pts_ref[c, pl.ds(t, 1), :] = jnp.where(owned, rows[c], 0.0)
        return carry

    lax.fori_loop(0, n_turb, turbine, 0)
    sums = jnp.sum(pts_ref[0], axis=1, keepdims=True)
    rot_ref[...] = jnp.broadcast_to(sums, rot_ref.shape)

    total = jnp.int32(0)
    for d in range(9):
        blocks = (cnt_ref[0, 0, d] + 127) >> 7

        def put(j, n, d=d):
            listed[n] = d * 8 + j
            return n + 1

        total = lax.fori_loop(0, blocks, put, total)
    listed[total] = listed[total - 1]

    def pair(i, carry):
        b0, b1 = listed[2 * i], listed[2 * i + 1]
        cell = jnp.concatenate([src_ref[pl.ds(b0, 1), :], src_ref[pl.ds(b1, 1), :]], axis=1)
        rows = pick(table, cell)
        lane = lax.broadcasted_iota(jnp.int32, (1, 128), 1)
        for s, b in enumerate((b0, b1)):
            d, j = b >> 3, b & 7
            weight = jnp.where(lane + j * 128 < cnt_ref[0, 0, d], w_ref[pl.ds(b, 1), :], 0.0)
            for c in range(3):
                out_ref[d, c, pl.ds(j, 1), :] = rows[c][:, s * 128 : (s + 1) * 128] * weight
            out_ref[d, 3, pl.ds(j, 1), :] = weight
        return carry

    lax.fori_loop(0, (total + 1) >> 1, pair, 0)


def scatter_kernel(val_ref, dst_ref, vel_ref, cor_ref, xlo_ref, xhi_ref, ylo_ref, yhi_ref, acc, listed):
    acc[...] = jnp.zeros_like(acc)
    total = jnp.int32(0)
    for d in range(9):
        used = jnp.sum(jnp.where(val_ref[d, 3] != 0.0, 1.0, 0.0)).astype(jnp.int32)
        blocks = (used + 127) >> 7

        def put(j, n, d=d):
            listed[n] = d * 8 + j
            return n + 1

        total = lax.fori_loop(0, blocks, put, total)
    for k in range(4):
        listed[total + k] = 0

    def chunk(i, carry):
        cells, vals = [], [[], [], [], []]
        for k in range(4):
            at = 4 * i + k
            b = listed[at]
            d, j = b >> 3, b & 7
            keep = jnp.where(at < total, 1.0, 0.0)
            cells.append(dst_ref[pl.ds(b, 1), :])
            for c in range(4):
                vals[c].append(val_ref[d, c, pl.ds(j, 1), :] * keep)
        cell = jnp.concatenate(cells, axis=1)
        vals = [jnp.concatenate(v, axis=1) for v in vals]
        acc[...] += spread(cell, vals)
        return carry

    lax.fori_loop(0, (total + 3) >> 2, chunk, 0)
    for c in range(3):
        cor = (1.0 - acc[:, 384:512]) * vel_ref[c] - acc[:, c * 128 : (c + 1) * 128]
        cor_ref[c] = cor
        xlo_ref[c] = cor[0:64]
        xhi_ref[c] = cor[448:512]
        for x in range(8):
            ylo_ref[c, x : x + 1, :] = cor[x * 64 : x * 64 + 1]
            yhi_ref[c, x : x + 1, :] = cor[x * 64 + 63 : x * 64 + 64]


def forcing_kernel(mine_ref, tile_ref, cell_ref, coef_ref, pts_ref, rot_ref, out_ref, tlist):
    out_ref[...] = jnp.zeros_like(out_ref)
    n_turb = active_turbines(tile_ref, mine_ref[0], tlist)
    points = tile_ref.shape[1]

    def turbine(i, carry):
        t = tlist[i]
        rotor = rot_ref[pl.ds(t, 1), 0:1] * (1.0 / 192)
        scale = -coef_ref[pl.ds(t, 1), :] * rotor
        force = [scale * pts_ref[c, pl.ds(t, 1), :] for c in range(3)]
        got = spread(cell_ref[pl.ds(t, 1), :], force)
        for c in range(3):
            out_ref[c] += got[:, c * 128 : (c + 1) * 128]
        return carry

    lax.fori_loop(0, n_turb, turbine, 0)


def stencil_kernel(cor_ref, frc_ref, west_ref, east_ref, south_ref, north_ref, out_ref):
    lane = lax.broadcasted_iota(jnp.int32, (64, 128), 1)
    for x in range(8):
        rows = slice(x * 64, x * 64 + 64)
        now = [cor_ref[c, rows, :] for c in range(3)]
        for c in range(3):
            u = now[c]
            west = cor_ref[c, (x - 1) * 64 : x * 64, :] if x > 0 else west_ref[c]
            east = cor_ref[c, (x + 1) * 64 : (x + 2) * 64, :] if x < 7 else east_ref[c]
            south = jnp.concatenate([south_ref[c, x : x + 1, :], u[:-1]], axis=0)
            north = jnp.concatenate([u[1:], north_ref[c, x : x + 1, :]], axis=0)
            upper = jnp.where(lane == 127, 0.0, pltpu.roll(u, 127, 1))
            lower = jnp.where(lane == 0, 0.0, pltpu.roll(u, 1, 1))
            laplace = east + west + north + south + upper + lower - 6.0 * u
            advect = (
                now[0] * (east - west) * 0.5
                + now[1] * (north - south) * 0.5
                + now[2] * (upper - lower) * 0.5
            )
            out_ref[c, rows, :] = u + 0.2 * (0.15 * laplace - advect + frc_ref[c, rows, :])


def shift(value, axis, step):
    count = lax.axis_size(axis)
    return lax.ppermute(value, axis, [(i, (i + step) % count) for i in range(count)])


def total_over(value, axis):
    count = lax.axis_size(axis)
    step = 1
    while step < count:
        value = value + lax.ppermute(value, axis, [(i, i ^ step) for i in range(count)])
        step *= 2
    return value


def body(velocity, counts, src_cell, weights, dst_cell, blade_tile, blade_cell, blade_coef):
    vel = velocity.reshape(3, 512, 128)
    src = src_cell.reshape(72, 128)
    weight = weights.reshape(72, 128)
    dst = dst_cell.reshape(72, 128)
    turbines, points = blade_cell.shape
    mine = (lax.axis_index("gx") * lax.axis_size("gy") + lax.axis_index("gy")).reshape(1).astype(jnp.int32)
    rows_t, lanes_t = turbines + -turbines % 8, points + -points % 128
    pad = ((0, rows_t - turbines), (0, lanes_t - points))
    tile = jnp.pad(blade_tile, pad, constant_values=-1)
    cell = jnp.pad(blade_cell, pad)
    coef = jnp.pad(blade_coef, pad)

    sent, pts, partial = pl.pallas_call(
        gather_kernel,
        out_shape=(
            jax.ShapeDtypeStruct((9, 4, 8, 128), F32),
            jax.ShapeDtypeStruct((3, rows_t, lanes_t), F32),
            jax.ShapeDtypeStruct((rows_t, 128), F32),
        ),
        in_specs=[SMEM_SPEC, SMEM_SPEC] + [VMEM_SPEC] * 5,
        out_specs=(VMEM_SPEC,) * 3,
        scratch_shapes=[pltpu.VMEM((3, 256, 512), BF16), pltpu.SMEM((80,), jnp.int32), pltpu.SMEM((32,), jnp.int32)],
        compiler_params=PARAMS,
        name="gather",
    )(mine, counts, vel, src, weight, tile, cell)

    rotor = total_over(total_over(partial, "gy"), "gx")

    low = shift(sent[0:3], "gx", -1)
    high = shift(sent[6:9], "gx", 1)
    grid = jnp.concatenate([low, sent[3:6], high], axis=0).reshape(3, 3, 4, 8, 128)
    low = shift(grid[:, 0], "gy", -1)
    high = shift(grid[:, 2], "gy", 1)
    arrived = jnp.stack([low, grid[:, 1], high], axis=1).reshape(9, 4, 8, 128)

    cor, xlo, xhi, ylo, yhi = pl.pallas_call(
        scatter_kernel,
        out_shape=(
            jax.ShapeDtypeStruct((3, 512, 128), F32),
            jax.ShapeDtypeStruct((3, 64, 128), F32),
            jax.ShapeDtypeStruct((3, 64, 128), F32),
            jax.ShapeDtypeStruct((3, 8, 128), F32),
            jax.ShapeDtypeStruct((3, 8, 128), F32),
        ),
        in_specs=[VMEM_SPEC] * 3,
        out_specs=(VMEM_SPEC,) * 5,
        scratch_shapes=[pltpu.VMEM((512, 512), F32), pltpu.SMEM((80,), jnp.int32)],
        compiler_params=PARAMS,
        name="scatter",
    )(arrived, dst, vel)

    west = shift(xhi, "gx", 1)
    east = shift(xlo, "gx", -1)
    south = shift(yhi, "gy", 1)
    north = shift(ylo, "gy", -1)

    forcing = pl.pallas_call(
        forcing_kernel,
        out_shape=jax.ShapeDtypeStruct((3, 512, 128), F32),
        in_specs=[SMEM_SPEC] + [VMEM_SPEC] * 5,
        out_specs=VMEM_SPEC,
        scratch_shapes=[pltpu.SMEM((32,), jnp.int32)],
        compiler_params=PARAMS,
        name="forcing",
    )(mine, tile, cell, coef, pts, rotor)

    updated = pl.pallas_call(
        stencil_kernel,
        out_shape=jax.ShapeDtypeStruct((3, 512, 128), F32),
        in_specs=[VMEM_SPEC] * 6,
        out_specs=VMEM_SPEC,
        compiler_params=PARAMS,
        name="stencil",
    )(cor, forcing, west, east, south, north)
    return updated.reshape(velocity.shape), forcing.reshape(velocity.shape)


def solution(mesh):
    grid = P("gx", "gy", None)
    lists = P("gx", "gy", None, None)
    field = P(None, "gx", "gy", None)
    return jax.shard_map(
        body,
        mesh=mesh,
        in_specs=(field, grid, lists, lists, lists, P(), P(), P()),
        out_specs=(field, field),
        check_vma=False,
    )
```

```python
import jax
import jax.numpy as jnp
from jax import lax
from jax.experimental import pallas as pl
from jax.experimental.pallas import tpu as pltpu
from jax.sharding import PartitionSpec as P

F32 = jnp.float32
BF16 = jnp.bfloat16
VMEM = pl.BlockSpec(memory_space=pltpu.VMEM)
SMEM = pl.BlockSpec(memory_space=pltpu.SMEM)
HBM = pl.BlockSpec(memory_space=pl.ANY)


def halves(value):
    high = value.astype(BF16)
    low = (value - high.astype(F32)).astype(BF16)
    return high, low


def one_hot(extent, index):
    rows = lax.broadcasted_iota(jnp.int32, (extent, index.shape[1]), 0)
    return jnp.where(rows == index, 1.0, 0.0).astype(BF16)


def pick(table, cell):
    key = (cell & 127) | (((cell >> 15) & 1) << 7)
    place = (cell >> 7) & 255
    hot = one_hot(256, key)
    hot = jnp.concatenate([hot, hot], axis=0)
    here = lax.broadcasted_iota(jnp.int32, (256, cell.shape[1]), 0) == place
    out = []
    for c in range(3):
        found = jnp.dot(table[c], hot, preferred_element_type=F32)
        out.append(jnp.sum(jnp.where(here, found, 0.0), axis=0, keepdims=True))
    return out


def spread(extent, row, level, values):
    hot = one_hot(extent, row)
    at_level = lax.broadcasted_iota(jnp.int32, (128, level.shape[1]), 0) == level
    high, low = [], []
    for value in values:
        vh = value.astype(BF16).astype(F32)
        high.append(jnp.where(at_level, vh, 0.0).astype(BF16))
        low.append(jnp.where(at_level, value - vh, 0.0).astype(BF16))
    left = jnp.concatenate([hot, hot], axis=1)
    right = jnp.concatenate([jnp.concatenate(high, axis=0), jnp.concatenate(low, axis=0)], axis=1)
    return lax.dot_general(left, right, (((1,), (1,)), ((), ())), preferred_element_type=F32)


def sides(mine_ref, count_y):
    mine = mine_ref[0]
    return 1 - 2 * ((mine // count_y) & 1), 1 - 2 * (mine & 1)


def list_blocks(lists, listed):
    total = jnp.int32(0)
    for used, tag in lists:

        def put(j, n, tag=tag):
            listed[n] = tag * 8 + j
            return n + 1

        total = lax.fori_loop(0, (used + 127) >> 7, put, total)
    return total


def gather_lists(table, total, width, listed, direction, cnt_ref, src_ref, w_ref, out_ref):
    for k in range(width - 1):
        listed[total + k] = listed[total - 1]

    def step(i, carry):
        blocks = [listed[width * i + k] for k in range(width)]
        rows = [direction[b >> 3] * 8 + (b & 7) for b in blocks]
        cell = jnp.concatenate([src_ref[pl.ds(r, 1), :] for r in rows], axis=1)
        found = pick(table, cell)
        lane = lax.broadcasted_iota(jnp.int32, (1, 128), 1)
        for k, (b, r) in enumerate(zip(blocks, rows)):
            used = cnt_ref[0, 0, r >> 3]
            j = b & 7
            weight = jnp.where(lane + j * 128 < used, w_ref[pl.ds(r, 1), :], 0.0)
            for c in range(3):
                out_ref[b >> 3, c, pl.ds(j, 1), :] = found[c][:, k * 128 : (k + 1) * 128] * weight
            out_ref[b >> 3, 3, pl.ds(j, 1), :] = weight
        return carry

    lax.fori_loop(0, (total + width - 1) // width, step, 0)


def make_far_gather(count_y, width):
    def kernel(mine_ref, cnt_ref, vel_hbm, src_ref, w_ref, out_ref, table, vel_ref, sem, listed, direction):
        half = vel_ref.shape[1] // 2
        copies = []
        for c in range(3):
            copies.append(pltpu.make_async_copy(vel_hbm.at[c], vel_ref.at[c], sem.at[c]))
            copies[-1].start()
        out_ref[...] = jnp.zeros_like(out_ref)
        side_x, side_y = sides(mine_ref, count_y)
        lists = []
        for s in range(2):
            for t in range(3):
                d = 3 * (side_x * (1 - 2 * s) + 1) + side_y * (1 - t) + 1
                direction[3 * s + t] = d
                lists.append((cnt_ref[0, 0, d], 3 * s + t))
        total = list_blocks(lists, listed)
        for c in range(3):
            copies[c].wait()
            for piece in range(2):
                high, low = halves(vel_ref[c, piece * half : (piece + 1) * half, :])
                table[c, :, piece * 128 : (piece + 1) * 128] = high
                table[c, :, 256 + piece * 128 : 256 + (piece + 1) * 128] = low
        gather_lists(table, total, width, listed, direction, cnt_ref, src_ref, w_ref, out_ref)

    return kernel


def active_turbines(tile_ref, mine, listed):
    turbines = tile_ref.shape[0]
    owned = jnp.where(tile_ref[...] == mine, 1.0, 0.0)
    found = jnp.max(owned, axis=1, keepdims=True)
    total = jnp.int32(0)
    for t in range(turbines):
        listed[total] = t
        total = total + jnp.where(found[t, 0] > 0.5, 1, 0)
    listed[total] = 0
    return total


def make_near_gather(count_y, width):
    def kernel(mine_ref, cnt_ref, table, src_ref, w_ref, tile_ref, cell_ref, out_ref, pts_ref, rot_ref, listed, direction, tlist):
        turbines, points = tile_ref.shape
        out_ref[...] = jnp.zeros_like(out_ref)
        pts_ref[...] = jnp.zeros_like(pts_ref)
        mine = mine_ref[0]
        n_turb = active_turbines(tile_ref, mine, tlist)

        def turbine(i, carry):
            pair = [tlist[2 * i], tlist[2 * i + 1]]
            cell = jnp.concatenate([cell_ref[pl.ds(t, 1), :] for t in pair], axis=1)
            found = pick(table, cell)
            for k, t in enumerate(pair):
                owned = tile_ref[pl.ds(t, 1), :] == mine
                for c in range(3):
                    pts_ref[c, pl.ds(t, 1), :] = jnp.where(owned, found[c][:, k * points : (k + 1) * points], 0.0)
            return carry

        lax.fori_loop(0, (n_turb + 1) >> 1, turbine, 0)
        rot_ref[...] = jnp.zeros_like(rot_ref)
        sums = jnp.sum(pts_ref[0], axis=1, keepdims=True)
        rot_ref[0:turbines, :] = jnp.broadcast_to(sums, (turbines, 128))

        _, side_y = sides(mine_ref, count_y)
        lists = []
        for t in range(3):
            d = 3 + side_y * (1 - t) + 1
            direction[t] = d
            lists.append((cnt_ref[0, 0, d], t))
        total = list_blocks(lists, listed)
        gather_lists(table, total, width, listed, direction, cnt_ref, src_ref, w_ref, out_ref)

    return kernel


def scatter_lists(val, n_lists, direction, dst_ref, listed, acc, extent, place):
    lists = []
    for q in range(n_lists):
        used = jnp.sum(jnp.where(val[q, 3] != 0.0, 1.0, 0.0)).astype(jnp.int32)
        lists.append((used, q))
    total = list_blocks(lists, listed)
    for k in range(3):
        listed[total + k] = 0

    def chunk(i, carry):
        cells, vals = [], [[], [], [], []]
        for k in range(4):
            at = 4 * i + k
            b = listed[at]
            q, j = b >> 3, b & 7
            keep = jnp.where(at < total, 1.0, 0.0)
            cells.append(dst_ref[pl.ds(direction[q] * 8 + j, 1), :])
            for c in range(4):
                vals[c].append(val[q, c, pl.ds(j, 1), :] * keep)
        cell = jnp.concatenate(cells, axis=1)
        vals = [jnp.concatenate(v, axis=1) for v in vals]
        acc[...] += spread(extent, place((cell >> 7) & 511), cell & 127, vals)
        return carry

    lax.fori_loop(0, (total + 3) >> 2, chunk, 0)


def make_first_scatter(count_y):
    def kernel(mine_ref, low_ref, own_ref, high_ref, dst_ref, acc, val, listed, direction):
        side_x, _ = sides(mine_ref, count_y)
        for q, ref in enumerate((low_ref, own_ref, high_ref)):
            val[q] = ref[1]
            direction[q] = 3 * (side_x * (q - 1) + 1) + 1
        acc[...] = jnp.zeros_like(acc)
        scatter_lists(val, 3, direction, dst_ref, listed, acc, 512, lambda row: row)

    return kernel


def load_later_lists(mine_ref, count_y, first_ref, second_ref, val, direction):
    side_x, side_y = sides(mine_ref, count_y)
    for t, ref in enumerate((first_ref, second_ref)):
        for s in range(3):
            q = 3 * t + s
            for c in range(4):
                at = (s * 4 + c) * 8
                val[q, c] = ref[at : at + 8, :]
            direction[q] = 3 * (side_x * (s - 1) + 1) + side_y * (2 * t - 1) + 1


def corrected(acc, vel, c):
    return (1.0 - acc[:, 384:512]) * vel - acc[:, c * 128 : (c + 1) * 128]


def make_outer_scatter(count_y):
    def kernel(mine_ref, base_ref, first_ref, second_ref, dst_ref, vel_ref, cor_ref, fa_ref, fb_ref, acc, val, listed, direction):
        load_later_lists(mine_ref, count_y, first_ref, second_ref, val, direction)
        acc[0:128, :] = base_ref[0:128, :]
        acc[128:256, :] = base_ref[384:512, :]
        place = lambda row: jnp.where(row < 128, row, jnp.where(row >= 384, row - 256, 512))
        scatter_lists(val, 6, direction, dst_ref, listed, acc, 256, place)
        side_x, _ = sides(mine_ref, count_y)
        for c in range(3):
            vel = jnp.concatenate([vel_ref[c, 0:128, :], vel_ref[c, 384:512, :]], axis=0)
            cor = corrected(acc, vel, c)
            cor_ref[c] = cor
            fa_ref[c] = jnp.where(side_x > 0, cor[192:256], cor[0:64])
            fb_ref[c] = jnp.where(side_x > 0, cor[0:64], cor[192:256])

    return kernel


def make_inner_scatter(count_y):
    def kernel(mine_ref, base_ref, first_ref, second_ref, dst_ref, vel_ref, outer_ref, cor_ref, fa_ref, fb_ref, acc, val, listed, direction):
        load_later_lists(mine_ref, count_y, first_ref, second_ref, val, direction)
        acc[...] = base_ref[128:384, :]
        scatter_lists(val, 6, direction, dst_ref, listed, acc, 256, lambda row: row - 128)
        _, side_y = sides(mine_ref, count_y)
        for c in range(3):
            cor_ref[c] = corrected(acc, vel_ref[c, 128:384, :], c)
            for x in range(8):
                ref, at = (cor_ref, x - 2) if 2 <= x < 6 else (outer_ref, x if x < 2 else x - 4)
                low = ref[c, at * 64 : at * 64 + 1, :]
                high = ref[c, at * 64 + 63 : at * 64 + 64, :]
                fa_ref[c, x : x + 1, :] = jnp.where(side_y > 0, high, low)
                fb_ref[c, x : x + 1, :] = jnp.where(side_y > 0, low, high)

    return kernel


def forcing_kernel(mine_ref, tile_ref, cell_ref, coef_ref, pts_ref, rot_ref, out_ref, tlist):
    out_ref[...] = jnp.zeros_like(out_ref)
    n_turb = active_turbines(tile_ref, mine_ref[0], tlist)
    points = tile_ref.shape[1]

    def turbine(i, carry):
        pair = [tlist[2 * i], tlist[2 * i + 1]]
        cell = jnp.concatenate([cell_ref[pl.ds(t, 1), :] for t in pair], axis=1)
        force = [[], [], []]
        for k, t in enumerate(pair):
            keep = jnp.where(2 * i + k < n_turb, 1.0 / points, 0.0)
            scale = -coef_ref[pl.ds(t, 1), :] * (rot_ref[pl.ds(t, 1), 0:1] * keep)
            for c in range(3):
                force[c].append(scale * pts_ref[c, pl.ds(t, 1), :])
        force = [jnp.concatenate(f, axis=1) for f in force]
        got = spread(512, (cell >> 7) & 511, cell & 127, force)
        for c in range(3):
            out_ref[c] += got[:, c * 128 : (c + 1) * 128]
        return carry

    lax.fori_loop(0, (n_turb + 1) >> 1, turbine, 0)


def make_stencil(count_y):
    def kernel(mine_ref, outer_ref, inner_ref, frc_ref, xa_ref, xb_ref, ya_ref, yb_ref, out_hbm, frc_hbm, out_ref, sem):
        side_x, side_y = sides(mine_ref, count_y)
        given = pltpu.make_async_copy(frc_ref, frc_hbm, sem.at[8])
        given.start()
        lane = lax.broadcasted_iota(jnp.int32, (64, 128), 1)

        def slab(c, x):
            if x < 0:
                return jnp.where(side_x > 0, xb_ref[c * 64 : c * 64 + 64, :], xa_ref[c * 64 : c * 64 + 64, :])
            if x > 7:
                return jnp.where(side_x > 0, xa_ref[c * 64 : c * 64 + 64, :], xb_ref[c * 64 : c * 64 + 64, :])
            ref, at = (inner_ref, x - 2) if 2 <= x < 6 else (outer_ref, x if x < 2 else x - 4)
            return ref[c, at * 64 : at * 64 + 64, :]

        copies = []
        for x in range(8):
            now = [slab(c, x) for c in range(3)]
            for c in range(3):
                u = now[c]
                west, east = slab(c, x - 1), slab(c, x + 1)
                ya, yb = ya_ref[c, x : x + 1, :], yb_ref[c, x : x + 1, :]
                south = jnp.concatenate([jnp.where(side_y > 0, yb, ya), u[:-1]], axis=0)
                north = jnp.concatenate([u[1:], jnp.where(side_y > 0, ya, yb)], axis=0)
                upper = jnp.where(lane == 127, 0.0, pltpu.roll(u, 127, 1))
                lower = jnp.where(lane == 0, 0.0, pltpu.roll(u, 1, 1))
                laplace = east + west + north + south + upper + lower - 6.0 * u
                advect = (
                    now[0] * (east - west) * 0.5
                    + now[1] * (north - south) * 0.5
                    + now[2] * (upper - lower) * 0.5
                )
                out_ref[c, x] = u + 0.2 * (0.15 * laplace - advect + frc_ref[c, x * 64 : x * 64 + 64, :])
            copies.append(pltpu.make_async_copy(out_ref.at[:, x], out_hbm.at[:, x], sem.at[x]))
            copies[-1].start()
        for copy in copies:
            copy.wait()
        given.wait()

    return kernel


def swap(value, axis, step):
    count = lax.axis_size(axis)
    return lax.ppermute(value, axis, [(i, i ^ step) for i in range(count)])


def swap_next(value, axis):
    count = lax.axis_size(axis)
    return lax.ppermute(value, axis, [(i, (i - 1 if i % 2 == 0 else i + 1) % count) for i in range(count)])


def call(kernel, name, outs, ins, args, scratch=(), flops=10**9, limit=32):
    return pl.pallas_call(
        kernel,
        out_shape=tuple(jax.ShapeDtypeStruct(shape, dtype) for shape, dtype, _ in outs),
        in_specs=ins,
        out_specs=tuple(spec for _, _, spec in outs),
        scratch_shapes=list(scratch),
        compiler_params=pltpu.CompilerParams(vmem_limit_bytes=limit << 20),
        cost_estimate=pl.CostEstimate(flops=flops, bytes_accessed=10**5, transcendentals=0),
        name=name,
    )(*args)


def body(velocity, counts, src_cell, weights, dst_cell, blade_tile, blade_cell, blade_coef):
    vel = velocity.reshape(3, 512, 128)
    src = src_cell.reshape(72, 128)
    weight = weights.reshape(72, 128)
    dst = dst_cell.reshape(72, 128)
    turbines, points = blade_cell.shape
    count_x, count_y = lax.axis_size("gx"), lax.axis_size("gy")
    mine = (lax.axis_index("gx") * count_y + lax.axis_index("gy")).reshape(1).astype(jnp.int32)
    rows_t = turbines + -turbines % 8
    ints = lambda n: pltpu.SMEM((n,), jnp.int32)

    far, table = call(
        make_far_gather(count_y, 6),
        "far_gather",
        [((6, 4, 8, 128), F32, VMEM), ((3, 256, 512), BF16, VMEM)],
        [SMEM, SMEM, HBM, VMEM, VMEM],
        (mine, counts, vel, src, weight),
        [pltpu.VMEM((3, 512, 128), F32), pltpu.SemaphoreType.DMA((3,)), ints(64), ints(8)],
        flops=5 * 10**9,
    )
    low = swap(far[0:3], "gx", 1)
    high = swap_next(far[3:6], "gx")
    own, pts, rotor = call(
        make_near_gather(count_y, 4),
        "near_gather",
        [((3, 4, 8, 128), F32, VMEM), ((3, turbines, points), F32, VMEM), ((rows_t, 128), F32, VMEM)],
        [SMEM, SMEM] + [VMEM] * 5,
        (mine, counts, table, src, weight, blade_tile, blade_cell),
        [ints(40), ints(8), ints(32)],
        flops=4 * 10**9,
    )
    for axis, count in (("gx", count_x), ("gy", count_y)):
        step = 4
        while step < count:
            rotor = rotor + swap(rotor, axis, step)
            step *= 2

    def y_payload(t):
        parts = [part[t].reshape(32, 128) for part in (low, own, high)]
        return jnp.concatenate(parts + [rotor], axis=0)

    first = swap(y_payload(0), "gy", 1)
    rotor = rotor + first[96:]
    second = swap_next(y_payload(2), "gy")
    (acc,) = call(
        make_first_scatter(count_y),
        "first_scatter",
        [((512, 512), F32, VMEM)],
        [SMEM] + [VMEM] * 4,
        (mine, low, own, high, dst),
        [pltpu.VMEM((3, 4, 8, 128), F32), ints(40), ints(8)],
        flops=4 * 10**9,
    )
    rotor = rotor + second[96:]
    rotor = rotor + swap(rotor, "gx", 2)
    half_scratch = [pltpu.VMEM((256, 512), F32), pltpu.VMEM((6, 4, 8, 128), F32), ints(64), ints(8)]
    outer, fa, fb = call(
        make_outer_scatter(count_y),
        "outer_scatter",
        [((3, 256, 128), F32, VMEM), ((3, 64, 128), F32, VMEM), ((3, 64, 128), F32, VMEM)],
        [SMEM] + [VMEM] * 5,
        (mine, acc, first, second, dst, vel),
        half_scratch,
        flops=4 * 10**9,
    )
    xa = swap(jnp.concatenate([fa.reshape(192, 128), rotor], axis=0), "gx", 1)
    xb = swap_next(fb.reshape(192, 128), "gx")
    inner, fa, fb = call(
        make_inner_scatter(count_y),
        "inner_scatter",
        [((3, 256, 128), F32, VMEM), ((3, 8, 128), F32, VMEM), ((3, 8, 128), F32, VMEM)],
        [SMEM] + [VMEM] * 6,
        (mine, acc, first, second, dst, vel, outer),
        half_scratch,
        flops=4 * 10**9,
    )
    ya = swap(fa, "gy", 1)
    yb = swap_next(fb, "gy")
    rotor = rotor + xa[192:]
    (force,) = call(
        forcing_kernel,
        "forcing",
        [((3, 512, 128), F32, VMEM)],
        [SMEM] + [VMEM] * 5,
        (mine, blade_tile, blade_cell, blade_coef, pts, rotor),
        [ints(32)],
        flops=10**6,
    )
    updated, forcing = call(
        make_stencil(count_y),
        "stencil",
        [((3, 8, 64, 128), F32, HBM), ((3, 512, 128), F32, HBM)],
        [SMEM] + [VMEM] * 7,
        (mine, outer, inner, force, xa, xb, ya, yb),
        [pltpu.VMEM((3, 8, 64, 128), F32), pltpu.SemaphoreType.DMA((9,))],
    )
    return updated, forcing.reshape(velocity.shape)


def solution(mesh):
    grid = P("gx", "gy", None)
    lists = P("gx", "gy", None, None)
    field = P(None, "gx", "gy", None)
    return jax.shard_map(
        body,
        mesh=mesh,
        in_specs=(field, grid, lists, lists, lists, P(), P(), P()),
        out_specs=(field, field),
        check_vma=False,
    )
```

```python
import jax
import jax.numpy as jnp
from jax import lax
from jax.experimental import pallas as pl
from jax.experimental.pallas import tpu as pltpu
from jax.sharding import PartitionSpec as P

F32 = jnp.float32
BF16 = jnp.bfloat16
VMEM = pl.BlockSpec(memory_space=pltpu.VMEM)
SMEM = pl.BlockSpec(memory_space=pltpu.SMEM)
HBM = pl.BlockSpec(memory_space=pltpu.HBM)


def halves(value):
    high = value.astype(BF16)
    low = (value - high.astype(F32)).astype(BF16)
    return high, low


def one_hot(extent, index):
    rows = lax.broadcasted_iota(jnp.int32, (extent, index.shape[1]), 0)
    return jnp.where(rows == index, 1.0, 0.0).astype(BF16)


def pick(table, cell):
    key = (cell & 127) | (((cell >> 15) & 1) << 7)
    place = (cell >> 7) & 255
    hot = one_hot(256, key)
    hot = jnp.concatenate([hot, hot], axis=0)
    here = lax.broadcasted_iota(jnp.int32, (256, cell.shape[1]), 0) == place
    out = []
    for c in range(3):
        found = jnp.dot(table[c], hot, preferred_element_type=F32)
        out.append(jnp.sum(jnp.where(here, found, 0.0), axis=0, keepdims=True))
    return out


def spread(extent, row, level, values):
    hot = one_hot(extent, row)
    at_level = lax.broadcasted_iota(jnp.int32, (128, level.shape[1]), 0) == level
    high, low = [], []
    for value in values:
        vh = value.astype(BF16).astype(F32)
        high.append(jnp.where(at_level, vh, 0.0).astype(BF16))
        low.append(jnp.where(at_level, value - vh, 0.0).astype(BF16))
    left = jnp.concatenate([hot, hot], axis=1)
    right = jnp.concatenate([jnp.concatenate(high, axis=0), jnp.concatenate(low, axis=0)], axis=1)
    return lax.dot_general(left, right, (((1,), (1,)), ((), ())), preferred_element_type=F32)


def sides(mine_ref, count_y):
    mine = mine_ref[0]
    return 1 - 2 * ((mine // count_y) & 1), 1 - 2 * (mine & 1)


def list_blocks(lists, listed):
    total = jnp.int32(0)
    for used, tag in lists:

        def put(j, n, tag=tag):
            listed[n] = tag * 8 + j
            return n + 1

        total = lax.fori_loop(0, (used + 127) >> 7, put, total)
    return total


def gather_lists(table, total, width, listed, direction, cnt_ref, src_ref, w_ref, out_ref):
    for k in range(width - 1):
        listed[total + k] = listed[total - 1]

    def step(i, carry):
        blocks = [listed[width * i + k] for k in range(width)]
        rows = [direction[b >> 3] * 8 + (b & 7) for b in blocks]
        cell = jnp.concatenate([src_ref[pl.ds(r, 1), :] for r in rows], axis=1)
        found = pick(table, cell)
        lane = lax.broadcasted_iota(jnp.int32, (1, 128), 1)
        for k, (b, r) in enumerate(zip(blocks, rows)):
            used = cnt_ref[0, 0, r >> 3]
            j = b & 7
            weight = jnp.where(lane + j * 128 < used, w_ref[pl.ds(r, 1), :], 0.0)
            for c in range(3):
                out_ref[b >> 3, c, pl.ds(j, 1), :] = found[c][:, k * 128 : (k + 1) * 128] * weight
            out_ref[b >> 3, 3, pl.ds(j, 1), :] = weight
        return carry

    lax.fori_loop(0, (total + width - 1) // width, step, 0)


def make_far_gather(count_y, width):
    def kernel(mine_ref, cnt_hbm, vel_hbm, src_hbm, w_hbm, dst_hbm, out_ref, table, vel_ref, src_ref, w_ref, dst_ref, sem, cnt_ref, listed, direction):
        half = vel_ref.shape[1] // 2
        pairs = [(cnt_hbm, cnt_ref), (src_hbm, src_ref)]
        pairs += [(vel_hbm.at[c], vel_ref.at[c]) for c in range(3)]
        pairs += [(w_hbm, w_ref), (dst_hbm, dst_ref)]
        copies = [pltpu.make_async_copy(a, b, sem.at[k]) for k, (a, b) in enumerate(pairs)]
        for copy in copies:
            copy.start()
        out_ref[...] = jnp.zeros_like(out_ref)
        copies[0].wait()
        side_x, side_y = sides(mine_ref, count_y)
        lists = []
        for s in range(2):
            for t in range(3):
                d = 3 * (side_x * (1 - 2 * s) + 1) + side_y * (1 - t) + 1
                direction[3 * s + t] = d
                lists.append((cnt_ref[0, 0, d], 3 * s + t))
        total = list_blocks(lists, listed)
        copies[1].wait()
        for c in range(3):
            copies[2 + c].wait()
            for piece in range(2):
                high, low = halves(vel_ref[c, piece * half : (piece + 1) * half, :])
                table[c, :, piece * 128 : (piece + 1) * 128] = high
                table[c, :, 256 + piece * 128 : 256 + (piece + 1) * 128] = low
        copies[5].wait()
        gather_lists(table, total, width, listed, direction, cnt_ref, src_ref, w_ref, out_ref)
        copies[6].wait()

    return kernel


def active_turbines(tile_ref, mine, listed):
    turbines = tile_ref.shape[0]
    owned = jnp.where(tile_ref[...] == mine, 1.0, 0.0)
    found = jnp.max(owned, axis=1, keepdims=True)
    total = jnp.int32(0)
    for t in range(turbines):
        listed[total] = t
        total = total + jnp.where(found[t, 0] > 0.5, 1, 0)
    listed[total] = 0
    return total


def points_kernel(mine_ref, table, tile_ref, cell_ref, pts_ref, rot_ref, tlist):
    turbines, points = tile_ref.shape
    pts_ref[...] = jnp.zeros_like(pts_ref)
    mine = mine_ref[0]
    n_turb = active_turbines(tile_ref, mine, tlist)

    def turbine(i, carry):
        pair = [tlist[2 * i], tlist[2 * i + 1]]
        cell = jnp.concatenate([cell_ref[pl.ds(t, 1), :] for t in pair], axis=1)
        found = pick(table, cell)
        for k, t in enumerate(pair):
            owned = tile_ref[pl.ds(t, 1), :] == mine
            for c in range(3):
                pts_ref[c, pl.ds(t, 1), :] = jnp.where(owned, found[c][:, k * points : (k + 1) * points], 0.0)
        return carry

    lax.fori_loop(0, (n_turb + 1) >> 1, turbine, 0)
    rot_ref[...] = jnp.zeros_like(rot_ref)
    sums = jnp.sum(pts_ref[0], axis=1, keepdims=True)
    rot_ref[0:turbines, :] = jnp.broadcast_to(sums, (turbines, 128))


def make_near_gather(count_y, width):
    def kernel(mine_ref, cnt_ref, table, src_ref, w_ref, out_ref, listed, direction):
        out_ref[...] = jnp.zeros_like(out_ref)
        _, side_y = sides(mine_ref, count_y)
        lists = []
        for t in range(3):
            d = 3 + side_y * (1 - t) + 1
            direction[t] = d
            lists.append((cnt_ref[0, 0, d], t))
        total = list_blocks(lists, listed)
        gather_lists(table, total, width, listed, direction, cnt_ref, src_ref, w_ref, out_ref)

    return kernel


def scatter_lists(val, n_lists, direction, dst_ref, listed, acc, extent, place):
    lists = []
    for q in range(n_lists):
        used = jnp.sum(jnp.where(val[q, 3] != 0.0, 1.0, 0.0)).astype(jnp.int32)
        lists.append((used, q))
    total = list_blocks(lists, listed)
    for k in range(3):
        listed[total + k] = 0

    def chunk(i, carry):
        cells, vals = [], [[], [], [], []]
        for k in range(4):
            at = 4 * i + k
            b = listed[at]
            q, j = b >> 3, b & 7
            keep = jnp.where(at < total, 1.0, 0.0)
            cells.append(dst_ref[pl.ds(direction[q] * 8 + j, 1), :])
            for c in range(4):
                vals[c].append(val[q, c, pl.ds(j, 1), :] * keep)
        cell = jnp.concatenate(cells, axis=1)
        vals = [jnp.concatenate(v, axis=1) for v in vals]
        acc[...] += spread(extent, place((cell >> 7) & 511), cell & 127, vals)
        return carry

    lax.fori_loop(0, (total + 3) >> 2, chunk, 0)


def make_first_scatter(count_y):
    def kernel(mine_ref, low_ref, own_ref, high_ref, dst_ref, acc, val, listed, direction):
        side_x, _ = sides(mine_ref, count_y)
        for q, ref in enumerate((low_ref, own_ref, high_ref)):
            val[q] = ref[1]
            direction[q] = 3 * (side_x * (q - 1) + 1) + 1
        acc[...] = jnp.zeros_like(acc)
        scatter_lists(val, 3, direction, dst_ref, listed, acc, 512, lambda row: row)

    return kernel


def load_later_lists(mine_ref, count_y, first_ref, second_ref, val, direction):
    side_x, side_y = sides(mine_ref, count_y)
    for t, ref in enumerate((first_ref, second_ref)):
        for s in range(3):
            q = 3 * t + s
            for c in range(4):
                at = (s * 4 + c) * 8
                val[q, c] = ref[at : at + 8, :]
            direction[q] = 3 * (side_x * (s - 1) + 1) + side_y * (2 * t - 1) + 1


def corrected(acc, vel, c):
    return (1.0 - acc[:, 384:512]) * vel - acc[:, c * 128 : (c + 1) * 128]


def make_outer_scatter(count_y):
    def kernel(mine_ref, base_ref, first_ref, second_ref, dst_ref, vel_ref, cor_ref, fa_ref, fb_ref, acc, val, listed, direction):
        load_later_lists(mine_ref, count_y, first_ref, second_ref, val, direction)
        acc[0:128, :] = base_ref[0:128, :]
        acc[128:256, :] = base_ref[384:512, :]
        place = lambda row: jnp.where(row < 128, row, jnp.where(row >= 384, row - 256, 512))
        scatter_lists(val, 6, direction, dst_ref, listed, acc, 256, place)
        side_x, _ = sides(mine_ref, count_y)
        for c in range(3):
            vel = jnp.concatenate([vel_ref[c, 0:128, :], vel_ref[c, 384:512, :]], axis=0)
            cor = corrected(acc, vel, c)
            cor_ref[c] = cor
            fa_ref[c] = jnp.where(side_x > 0, cor[192:256], cor[0:64])
            fb_ref[c] = jnp.where(side_x > 0, cor[0:64], cor[192:256])

    return kernel


def make_inner_scatter(count_y):
    def kernel(mine_ref, base_ref, first_ref, second_ref, dst_ref, vel_ref, outer_ref, cor_ref, fa_ref, fb_ref, acc, val, listed, direction):
        load_later_lists(mine_ref, count_y, first_ref, second_ref, val, direction)
        acc[...] = base_ref[128:384, :]
        scatter_lists(val, 6, direction, dst_ref, listed, acc, 256, lambda row: row - 128)
        _, side_y = sides(mine_ref, count_y)
        for c in range(3):
            cor_ref[c] = corrected(acc, vel_ref[c, 128:384, :], c)
            for x in range(8):
                ref, at = (cor_ref, x - 2) if 2 <= x < 6 else (outer_ref, x if x < 2 else x - 4)
                low = ref[c, at * 64 : at * 64 + 1, :]
                high = ref[c, at * 64 + 63 : at * 64 + 64, :]
                fa_ref[c, x : x + 1, :] = jnp.where(side_y > 0, high, low)
                fb_ref[c, x : x + 1, :] = jnp.where(side_y > 0, low, high)

    return kernel


def forcing_kernel(mine_ref, tile_ref, cell_ref, coef_ref, pts_ref, rot_ref, out_ref, tlist):
    out_ref[...] = jnp.zeros_like(out_ref)
    n_turb = active_turbines(tile_ref, mine_ref[0], tlist)
    points = tile_ref.shape[1]

    def turbine(i, carry):
        pair = [tlist[2 * i], tlist[2 * i + 1]]
        cell = jnp.concatenate([cell_ref[pl.ds(t, 1), :] for t in pair], axis=1)
        force = [[], [], []]
        for k, t in enumerate(pair):
            keep = jnp.where(2 * i + k < n_turb, 1.0 / points, 0.0)
            scale = -coef_ref[pl.ds(t, 1), :] * (rot_ref[pl.ds(t, 1), 0:1] * keep)
            for c in range(3):
                force[c].append(scale * pts_ref[c, pl.ds(t, 1), :])
        force = [jnp.concatenate(f, axis=1) for f in force]
        got = spread(512, (cell >> 7) & 511, cell & 127, force)
        for c in range(3):
            out_ref[c] += got[:, c * 128 : (c + 1) * 128]
        return carry

    lax.fori_loop(0, (n_turb + 1) >> 1, turbine, 0)


def make_stencil(count_y):
    def kernel(mine_ref, outer_ref, inner_ref, frc_ref, xa_ref, xb_ref, ya_ref, yb_ref, out_hbm, frc_hbm, out_ref, sem):
        side_x, side_y = sides(mine_ref, count_y)
        given = pltpu.make_async_copy(frc_ref, frc_hbm, sem.at[8])
        given.start()
        lane = lax.broadcasted_iota(jnp.int32, (64, 128), 1)

        def slab(c, x):
            if x < 0:
                return jnp.where(side_x > 0, xb_ref[c * 64 : c * 64 + 64, :], xa_ref[c * 64 : c * 64 + 64, :])
            if x > 7:
                return jnp.where(side_x > 0, xa_ref[c * 64 : c * 64 + 64, :], xb_ref[c * 64 : c * 64 + 64, :])
            ref, at = (inner_ref, x - 2) if 2 <= x < 6 else (outer_ref, x if x < 2 else x - 4)
            return ref[c, at * 64 : at * 64 + 64, :]

        copies = []
        for x in range(8):
            now = [slab(c, x) for c in range(3)]
            for c in range(3):
                u = now[c]
                west, east = slab(c, x - 1), slab(c, x + 1)
                ya, yb = ya_ref[c, x : x + 1, :], yb_ref[c, x : x + 1, :]
                south = jnp.concatenate([jnp.where(side_y > 0, yb, ya), u[:-1]], axis=0)
                north = jnp.concatenate([u[1:], jnp.where(side_y > 0, ya, yb)], axis=0)
                upper = jnp.where(lane == 127, 0.0, pltpu.roll(u, 127, 1))
                lower = jnp.where(lane == 0, 0.0, pltpu.roll(u, 1, 1))
                laplace = east + west + north + south + upper + lower - 6.0 * u
                advect = (
                    now[0] * (east - west) * 0.5
                    + now[1] * (north - south) * 0.5
                    + now[2] * (upper - lower) * 0.5
                )
                out_ref[c, x] = u + 0.2 * (0.15 * laplace - advect + frc_ref[c, x * 64 : x * 64 + 64, :])
            copies.append(pltpu.make_async_copy(out_ref.at[:, x], out_hbm.at[:, x], sem.at[x]))
            copies[-1].start()
        for copy in copies:
            copy.wait()
        given.wait()

    return kernel


def swap(value, axis, step):
    count = lax.axis_size(axis)
    return lax.ppermute(value, axis, [(i, i ^ step) for i in range(count)])


def swap_next(value, axis):
    count = lax.axis_size(axis)
    return lax.ppermute(value, axis, [(i, (i - 1 if i % 2 == 0 else i + 1) % count) for i in range(count)])


def call(kernel, name, outs, ins, args, scratch=(), flops=10**9, limit=32):
    return pl.pallas_call(
        kernel,
        out_shape=tuple(jax.ShapeDtypeStruct(shape, dtype) for shape, dtype, _ in outs),
        in_specs=ins,
        out_specs=tuple(spec for _, _, spec in outs),
        scratch_shapes=list(scratch),
        compiler_params=pltpu.CompilerParams(vmem_limit_bytes=limit << 20),
        cost_estimate=pl.CostEstimate(flops=flops, bytes_accessed=10**5, transcendentals=0),
        name=name,
    )(*args)


def body(velocity, counts, src_cell, weights, dst_cell, blade_tile, blade_cell, blade_coef):
    vel = velocity.reshape(3, 512, 128)
    src = src_cell.reshape(72, 128)
    weight = weights.reshape(72, 128)
    dst = dst_cell.reshape(72, 128)
    turbines, points = blade_cell.shape
    count_x, count_y = lax.axis_size("gx"), lax.axis_size("gy")
    mine = (lax.axis_index("gx") * count_y + lax.axis_index("gy")).reshape(1).astype(jnp.int32)
    rows_t = turbines + -turbines % 8
    ints = lambda n: pltpu.SMEM((n,), jnp.int32)

    whole = ((72, 128), jnp.int32, VMEM)
    far, table, vel, src, weight, dst = call(
        make_far_gather(count_y, 6),
        "far_gather",
        [((6, 4, 8, 128), F32, VMEM), ((3, 256, 512), BF16, VMEM), ((3, 512, 128), F32, VMEM), whole, ((72, 128), F32, VMEM), whole],
        [SMEM] + [HBM] * 5,
        (mine, counts, vel, src, weight, dst),
        [pltpu.SemaphoreType.DMA((7,)), pltpu.SMEM((1, 1, 9), jnp.int32), ints(64), ints(8)],
        flops=5 * 10**9,
    )
    low = swap(far[0:3], "gx", 1)
    high = swap_next(far[3:6], "gx")
    pts, rotor = call(
        points_kernel,
        "points",
        [((3, turbines, points), F32, VMEM), ((rows_t, 128), F32, VMEM)],
        [SMEM] + [VMEM] * 3,
        (mine, table, blade_tile, blade_cell),
        [ints(32)],
        flops=10**9,
    )
    (own,) = call(
        make_near_gather(count_y, 4),
        "near_gather",
        [((3, 4, 8, 128), F32, VMEM)],
        [SMEM, SMEM] + [VMEM] * 3,
        (mine, counts, table, src, weight),
        [ints(40), ints(8)],
        flops=4 * 10**9,
    )
    for axis, count in (("gx", count_x), ("gy", count_y)):
        step = 4
        while step < count:
            rotor = rotor + swap(rotor, axis, step)
            step *= 2

    def y_payload(t):
        parts = [part[t].reshape(32, 128) for part in (low, own, high)]
        return jnp.concatenate(parts + [rotor], axis=0)

    first = swap(y_payload(0), "gy", 1)
    rotor = rotor + first[96:]
    second = swap_next(y_payload(2), "gy")
    (acc,) = call(
        make_first_scatter(count_y),
        "first_scatter",
        [((512, 512), F32, VMEM)],
        [SMEM] + [VMEM] * 4,
        (mine, low, own, high, dst),
        [pltpu.VMEM((3, 4, 8, 128), F32), ints(40), ints(8)],
        flops=4 * 10**9,
    )
    rotor = rotor + second[96:]
    rotor = rotor + swap(rotor, "gx", 2)
    half_scratch = [pltpu.VMEM((256, 512), F32), pltpu.VMEM((6, 4, 8, 128), F32), ints(64), ints(8)]
    outer, fa, fb = call(
        make_outer_scatter(count_y),
        "outer_scatter",
        [((3, 256, 128), F32, VMEM), ((3, 64, 128), F32, VMEM), ((3, 64, 128), F32, VMEM)],
        [SMEM] + [VMEM] * 5,
        (mine, acc, first, second, dst, vel),
        half_scratch,
        flops=4 * 10**9,
    )
    xa = swap(jnp.concatenate([fa.reshape(192, 128), rotor], axis=0), "gx", 1)
    xb = swap_next(fb.reshape(192, 128), "gx")
    inner, fa, fb = call(
        make_inner_scatter(count_y),
        "inner_scatter",
        [((3, 256, 128), F32, VMEM), ((3, 8, 128), F32, VMEM), ((3, 8, 128), F32, VMEM)],
        [SMEM] + [VMEM] * 6,
        (mine, acc, first, second, dst, vel, outer),
        half_scratch,
        flops=4 * 10**9,
    )
    rotor, xb, fa, fb = lax.optimization_barrier((rotor + xa[192:], xb, fa, fb))
    ya = swap(fa, "gy", 1)
    yb = swap_next(fb, "gy")
    (force,) = call(
        forcing_kernel,
        "forcing",
        [((3, 512, 128), F32, VMEM)],
        [SMEM] + [VMEM] * 5,
        (mine, blade_tile, blade_cell, blade_coef, pts, rotor),
        [ints(32)],
        flops=10**6,
    )
    updated, forcing = call(
        make_stencil(count_y),
        "stencil",
        [((3, 8, 64, 128), F32, HBM), ((3, 512, 128), F32, HBM)],
        [SMEM] + [VMEM] * 7,
        (mine, outer, inner, force, xa, xb, ya, yb),
        [pltpu.VMEM((3, 8, 64, 128), F32), pltpu.SemaphoreType.DMA((9,))],
    )
    return updated, forcing.reshape(velocity.shape)


def solution(mesh):
    grid = P("gx", "gy", None)
    lists = P("gx", "gy", None, None)
    field = P(None, "gx", "gy", None)
    return jax.shard_map(
        body,
        mesh=mesh,
        in_specs=(field, grid, lists, lists, lists, P(), P(), P()),
        out_specs=(field, field),
        check_vma=False,
    )
```

```python
import jax
import jax.numpy as jnp
from jax import lax
from jax.experimental import pallas as pl
from jax.experimental.pallas import tpu as pltpu
from jax.sharding import PartitionSpec as P

F32 = jnp.float32
BF16 = jnp.bfloat16
VMEM = pl.BlockSpec(memory_space=pltpu.VMEM)
SMEM = pl.BlockSpec(memory_space=pltpu.SMEM)
HBM = pl.BlockSpec(memory_space=pltpu.HBM)


def halves(value):
    high = value.astype(BF16)
    low = (value - high.astype(F32)).astype(BF16)
    return high, low


def one_hot(extent, index):
    rows = lax.broadcasted_iota(jnp.int32, (extent, index.shape[1]), 0)
    return jnp.where(rows == index, 1.0, 0.0).astype(BF16)


def pick(table, cell):
    key = (cell & 127) | (((cell >> 15) & 1) << 7)
    place = (cell >> 7) & 255
    hot = one_hot(256, key)
    hot = jnp.concatenate([hot, hot], axis=0)
    here = lax.broadcasted_iota(jnp.int32, (256, cell.shape[1]), 0) == place
    out = []
    for c in range(3):
        found = jnp.dot(table[c], hot, preferred_element_type=F32)
        out.append(jnp.sum(jnp.where(here, found, 0.0), axis=0, keepdims=True))
    return out


def spread(extent, row, level, values):
    hot = one_hot(extent, row)
    at_level = lax.broadcasted_iota(jnp.int32, (128, level.shape[1]), 0) == level
    high, low = [], []
    for value in values:
        vh = value.astype(BF16).astype(F32)
        high.append(jnp.where(at_level, vh, 0.0).astype(BF16))
        low.append(jnp.where(at_level, value - vh, 0.0).astype(BF16))
    left = jnp.concatenate([hot, hot], axis=1)
    right = jnp.concatenate([jnp.concatenate(high, axis=0), jnp.concatenate(low, axis=0)], axis=1)
    return lax.dot_general(left, right, (((1,), (1,)), ((), ())), preferred_element_type=F32)


def sides(mine_ref, count_y):
    mine = mine_ref[0]
    return 1 - 2 * ((mine // count_y) & 1), 1 - 2 * (mine & 1)


def list_blocks(lists, listed):
    total = jnp.int32(0)
    for used, tag in lists:

        def put(j, n, tag=tag):
            listed[n] = tag * 8 + j
            return n + 1

        total = lax.fori_loop(0, (used + 127) >> 7, put, total)
    return total


def gather_lists(table, total, width, listed, direction, cnt_ref, src_ref, w_ref, out_ref):
    for k in range(width - 1):
        listed[total + k] = listed[total - 1]

    def step(i, carry):
        blocks = [listed[width * i + k] for k in range(width)]
        rows = [direction[b >> 3] * 8 + (b & 7) for b in blocks]
        cell = jnp.concatenate([src_ref[pl.ds(r, 1), :] for r in rows], axis=1)
        found = pick(table, cell)
        lane = lax.broadcasted_iota(jnp.int32, (1, 128), 1)
        for k, (b, r) in enumerate(zip(blocks, rows)):
            used = cnt_ref[0, 0, r >> 3]
            j = b & 7
            weight = jnp.where(lane + j * 128 < used, w_ref[pl.ds(r, 1), :], 0.0)
            for c in range(3):
                out_ref[b >> 3, c, pl.ds(j, 1), :] = found[c][:, k * 128 : (k + 1) * 128] * weight
            out_ref[b >> 3, 3, pl.ds(j, 1), :] = weight
        return carry

    lax.fori_loop(0, (total + width - 1) // width, step, 0)


def make_far_gather(count_y, width):
    def kernel(mine_ref, cnt_hbm, vel_hbm, src_hbm, w_hbm, dst_hbm, out_ref, table, vel_ref, src_ref, w_ref, dst_ref, sem, cnt_ref, listed, direction):
        half = vel_ref.shape[1] // 2
        pairs = [(cnt_hbm, cnt_ref), (src_hbm, src_ref)]
        pairs += [(vel_hbm.at[c], vel_ref.at[c]) for c in range(3)]
        pairs += [(w_hbm, w_ref), (dst_hbm, dst_ref)]
        copies = [pltpu.make_async_copy(a, b, sem.at[k]) for k, (a, b) in enumerate(pairs)]
        for copy in copies:
            copy.start()
        out_ref[...] = jnp.zeros_like(out_ref)
        copies[0].wait()
        side_x, side_y = sides(mine_ref, count_y)
        lists = []
        for s in range(2):
            for t in range(3):
                d = 3 * (side_x * (1 - 2 * s) + 1) + side_y * (1 - t) + 1
                direction[3 * s + t] = d
                lists.append((cnt_ref[0, 0, d], 3 * s + t))
        total = list_blocks(lists, listed)
        copies[1].wait()
        for c in range(3):
            copies[2 + c].wait()
            for piece in range(2):
                high, low = halves(vel_ref[c, piece * half : (piece + 1) * half, :])
                table[c, :, piece * 128 : (piece + 1) * 128] = high
                table[c, :, 256 + piece * 128 : 256 + (piece + 1) * 128] = low
        copies[5].wait()
        gather_lists(table, total, width, listed, direction, cnt_ref, src_ref, w_ref, out_ref)
        copies[6].wait()

    return kernel


def active_turbines(tile_ref, mine, listed):
    turbines = tile_ref.shape[0]
    owned = jnp.where(tile_ref[...] == mine, 1.0, 0.0)
    found = jnp.max(owned, axis=1, keepdims=True)
    total = jnp.int32(0)
    for t in range(turbines):
        listed[total] = t
        total = total + jnp.where(found[t, 0] > 0.5, 1, 0)
    listed[total] = 0
    return total


def points_kernel(mine_ref, table, tile_ref, cell_ref, pts_ref, rot_ref, tlist):
    turbines, points = tile_ref.shape
    pts_ref[...] = jnp.zeros_like(pts_ref)
    mine = mine_ref[0]
    n_turb = active_turbines(tile_ref, mine, tlist)

    def turbine(i, carry):
        pair = [tlist[2 * i], tlist[2 * i + 1]]
        cell = jnp.concatenate([cell_ref[pl.ds(t, 1), :] for t in pair], axis=1)
        found = pick(table, cell)
        for k, t in enumerate(pair):
            owned = tile_ref[pl.ds(t, 1), :] == mine
            for c in range(3):
                pts_ref[c, pl.ds(t, 1), :] = jnp.where(owned, found[c][:, k * points : (k + 1) * points], 0.0)
        return carry

    lax.fori_loop(0, (n_turb + 1) >> 1, turbine, 0)
    rot_ref[...] = jnp.zeros_like(rot_ref)
    sums = jnp.sum(pts_ref[0], axis=1, keepdims=True)
    rot_ref[0:turbines, :] = jnp.broadcast_to(sums, (turbines, 128))


def make_near_gather(count_y, width):
    def kernel(mine_ref, cnt_ref, table, src_ref, w_ref, out_ref, listed, direction):
        out_ref[...] = jnp.zeros_like(out_ref)
        _, side_y = sides(mine_ref, count_y)
        lists = []
        for t in range(3):
            d = 3 + side_y * (1 - t) + 1
            direction[t] = d
            lists.append((cnt_ref[0, 0, d], t))
        total = list_blocks(lists, listed)
        gather_lists(table, total, width, listed, direction, cnt_ref, src_ref, w_ref, out_ref)

    return kernel


def scatter_lists(val, n_lists, direction, dst_ref, listed, acc, extent, place, width=4):
    lists = []
    for q in range(n_lists):
        used = jnp.sum(jnp.where(val[q, 3] != 0.0, 1.0, 0.0)).astype(jnp.int32)
        lists.append((used, q))
    total = list_blocks(lists, listed)
    for k in range(width - 1):
        listed[total + k] = 0

    def chunk(i, carry):
        cells, vals = [], [[], [], [], []]
        for k in range(width):
            at = width * i + k
            b = listed[at]
            q, j = b >> 3, b & 7
            keep = jnp.where(at < total, 1.0, 0.0)
            cells.append(dst_ref[pl.ds(direction[q] * 8 + j, 1), :])
            for c in range(4):
                vals[c].append(val[q, c, pl.ds(j, 1), :] * keep)
        cell = jnp.concatenate(cells, axis=1)
        vals = [jnp.concatenate(v, axis=1) for v in vals]
        acc[...] += spread(extent, place((cell >> 7) & 511), cell & 127, vals)
        return carry

    lax.fori_loop(0, (total + width - 1) // width, chunk, 0)


def make_first_scatter(count_y):
    def kernel(mine_ref, low_ref, own_ref, high_ref, dst_ref, acc, val, listed, direction):
        side_x, _ = sides(mine_ref, count_y)
        for q, ref in enumerate((low_ref, own_ref, high_ref)):
            val[q] = ref[1]
            direction[q] = 3 * (side_x * (q - 1) + 1) + 1
        acc[...] = jnp.zeros_like(acc)
        scatter_lists(val, 3, direction, dst_ref, listed, acc, 512, lambda row: row)

    return kernel


def load_later_lists(mine_ref, count_y, first_ref, second_ref, val, direction):
    side_x, side_y = sides(mine_ref, count_y)
    for t, ref in enumerate((first_ref, second_ref)):
        for s in range(3):
            q = 3 * t + s
            for c in range(4):
                at = (s * 4 + c) * 8
                val[q, c] = ref[at : at + 8, :]
            direction[q] = 3 * (side_x * (s - 1) + 1) + side_y * (2 * t - 1) + 1


def corrected(acc, vel, c):
    return (1.0 - acc[:, 384:512]) * vel - acc[:, c * 128 : (c + 1) * 128]


def make_outer_scatter(count_y):
    def kernel(mine_ref, base_ref, first_ref, second_ref, dst_ref, vel_ref, cor_ref, fa_ref, fb_ref, acc, val, listed, direction):
        load_later_lists(mine_ref, count_y, first_ref, second_ref, val, direction)
        acc[0:128, :] = base_ref[0:128, :]
        acc[128:256, :] = base_ref[384:512, :]
        place = lambda row: jnp.where(row < 128, row, jnp.where(row >= 384, row - 256, 512))
        scatter_lists(val, 6, direction, dst_ref, listed, acc, 256, place, 6)
        side_x, _ = sides(mine_ref, count_y)
        for c in range(3):
            vel = jnp.concatenate([vel_ref[c, 0:128, :], vel_ref[c, 384:512, :]], axis=0)
            cor = corrected(acc, vel, c)
            cor_ref[c] = cor
            fa_ref[c] = jnp.where(side_x > 0, cor[192:256], cor[0:64])
            fb_ref[c] = jnp.where(side_x > 0, cor[0:64], cor[192:256])

    return kernel


def make_inner_scatter(count_y):
    def kernel(mine_ref, base_ref, first_ref, second_ref, dst_ref, vel_ref, outer_ref, cor_ref, fa_ref, fb_ref, acc, val, listed, direction):
        load_later_lists(mine_ref, count_y, first_ref, second_ref, val, direction)
        acc[...] = base_ref[128:384, :]
        scatter_lists(val, 6, direction, dst_ref, listed, acc, 256, lambda row: row - 128, 6)
        _, side_y = sides(mine_ref, count_y)
        for c in range(3):
            cor_ref[c] = corrected(acc, vel_ref[c, 128:384, :], c)
            for x in range(8):
                ref, at = (cor_ref, x - 2) if 2 <= x < 6 else (outer_ref, x if x < 2 else x - 4)
                low = ref[c, at * 64 : at * 64 + 1, :]
                high = ref[c, at * 64 + 63 : at * 64 + 64, :]
                fa_ref[c, x : x + 1, :] = jnp.where(side_y > 0, high, low)
                fb_ref[c, x : x + 1, :] = jnp.where(side_y > 0, low, high)

    return kernel


def forcing_kernel(mine_ref, tile_ref, cell_ref, coef_ref, pts_ref, rot_ref, out_ref, tlist):
    out_ref[...] = jnp.zeros_like(out_ref)
    n_turb = active_turbines(tile_ref, mine_ref[0], tlist)
    points = tile_ref.shape[1]

    def turbine(i, carry):
        pair = [tlist[2 * i], tlist[2 * i + 1]]
        cell = jnp.concatenate([cell_ref[pl.ds(t, 1), :] for t in pair], axis=1)
        force = [[], [], []]
        for k, t in enumerate(pair):
            keep = jnp.where(2 * i + k < n_turb, 1.0 / points, 0.0)
            scale = -coef_ref[pl.ds(t, 1), :] * (rot_ref[pl.ds(t, 1), 0:1] * keep)
            for c in range(3):
                force[c].append(scale * pts_ref[c, pl.ds(t, 1), :])
        force = [jnp.concatenate(f, axis=1) for f in force]
        got = spread(512, (cell >> 7) & 511, cell & 127, force)
        for c in range(3):
            out_ref[c] += got[:, c * 128 : (c + 1) * 128]
        return carry

    lax.fori_loop(0, (n_turb + 1) >> 1, turbine, 0)


def make_stencil(count_y):
    def kernel(mine_ref, outer_ref, inner_ref, frc_ref, xa_ref, xb_ref, ya_ref, yb_ref, out_hbm, frc_hbm, out_ref, sem):
        side_x, side_y = sides(mine_ref, count_y)
        given = pltpu.make_async_copy(frc_ref, frc_hbm, sem.at[8])
        given.start()
        lane = lax.broadcasted_iota(jnp.int32, (64, 128), 1)

        def slab(c, x):
            if x < 0:
                return jnp.where(side_x > 0, xb_ref[c * 64 : c * 64 + 64, :], xa_ref[c * 64 : c * 64 + 64, :])
            if x > 7:
                return jnp.where(side_x > 0, xa_ref[c * 64 : c * 64 + 64, :], xb_ref[c * 64 : c * 64 + 64, :])
            ref, at = (inner_ref, x - 2) if 2 <= x < 6 else (outer_ref, x if x < 2 else x - 4)
            return ref[c, at * 64 : at * 64 + 64, :]

        copies = []
        for x in range(8):
            now = [slab(c, x) for c in range(3)]
            for c in range(3):
                u = now[c]
                west, east = slab(c, x - 1), slab(c, x + 1)
                ya, yb = ya_ref[c, x : x + 1, :], yb_ref[c, x : x + 1, :]
                south = jnp.concatenate([jnp.where(side_y > 0, yb, ya), u[:-1]], axis=0)
                north = jnp.concatenate([u[1:], jnp.where(side_y > 0, ya, yb)], axis=0)
                upper = jnp.where(lane == 127, 0.0, pltpu.roll(u, 127, 1))
                lower = jnp.where(lane == 0, 0.0, pltpu.roll(u, 1, 1))
                laplace = east + west + north + south + upper + lower - 6.0 * u
                advect = (
                    now[0] * (east - west) * 0.5
                    + now[1] * (north - south) * 0.5
                    + now[2] * (upper - lower) * 0.5
                )
                out_ref[c, x] = u + 0.2 * (0.15 * laplace - advect + frc_ref[c, x * 64 : x * 64 + 64, :])
            copies.append(pltpu.make_async_copy(out_ref.at[:, x], out_hbm.at[:, x], sem.at[x]))
            copies[-1].start()
        for copy in copies:
            copy.wait()
        given.wait()

    return kernel


def swap(value, axis, step):
    count = lax.axis_size(axis)
    return lax.ppermute(value, axis, [(i, i ^ step) for i in range(count)])


def swap_next(value, axis):
    count = lax.axis_size(axis)
    return lax.ppermute(value, axis, [(i, (i - 1 if i % 2 == 0 else i + 1) % count) for i in range(count)])


def call(kernel, name, outs, ins, args, scratch=(), flops=10**9, limit=32):
    return pl.pallas_call(
        kernel,
        out_shape=tuple(jax.ShapeDtypeStruct(shape, dtype) for shape, dtype, _ in outs),
        in_specs=ins,
        out_specs=tuple(spec for _, _, spec in outs),
        scratch_shapes=list(scratch),
        compiler_params=pltpu.CompilerParams(vmem_limit_bytes=limit << 20),
        cost_estimate=pl.CostEstimate(flops=flops, bytes_accessed=10**5, transcendentals=0),
        name=name,
    )(*args)


def body(velocity, counts, src_cell, weights, dst_cell, blade_tile, blade_cell, blade_coef):
    vel = velocity.reshape(3, 512, 128)
    src = src_cell.reshape(72, 128)
    weight = weights.reshape(72, 128)
    dst = dst_cell.reshape(72, 128)
    turbines, points = blade_cell.shape
    count_x, count_y = lax.axis_size("gx"), lax.axis_size("gy")
    mine = (lax.axis_index("gx") * count_y + lax.axis_index("gy")).reshape(1).astype(jnp.int32)
    rows_t = turbines + -turbines % 8
    ints = lambda n: pltpu.SMEM((n,), jnp.int32)

    whole = ((72, 128), jnp.int32, VMEM)
    far, table, vel, src, weight, dst = call(
        make_far_gather(count_y, 6),
        "far_gather",
        [((6, 4, 8, 128), F32, VMEM), ((3, 256, 512), BF16, VMEM), ((3, 512, 128), F32, VMEM), whole, ((72, 128), F32, VMEM), whole],
        [SMEM] + [HBM] * 5,
        (mine,) + tuple(pltpu.with_memory_space_constraint(v, pltpu.HBM) for v in (counts, vel, src, weight, dst)),
        [pltpu.SemaphoreType.DMA((7,)), pltpu.SMEM((1, 1, 9), jnp.int32), ints(64), ints(8)],
        flops=5 * 10**9,
    )
    low = swap(far[0:3], "gx", 1)
    high = swap_next(far[3:6], "gx")
    pts, rotor = call(
        points_kernel,
        "points",
        [((3, turbines, points), F32, VMEM), ((rows_t, 128), F32, VMEM)],
        [SMEM] + [VMEM] * 3,
        (mine, table, blade_tile, blade_cell),
        [ints(32)],
        flops=10**9,
    )
    (own,) = call(
        make_near_gather(count_y, 4),
        "near_gather",
        [((3, 4, 8, 128), F32, VMEM)],
        [SMEM, SMEM] + [VMEM] * 3,
        (mine, counts, table, src, weight),
        [ints(40), ints(8)],
        flops=4 * 10**9,
    )
    for axis, count in (("gx", count_x), ("gy", count_y)):
        step = 4
        while step < count:
            rotor = rotor + swap(rotor, axis, step)
            step *= 2

    def y_payload(t):
        parts = [part[t].reshape(32, 128) for part in (low, own, high)]
        return jnp.concatenate(parts + [rotor], axis=0)

    first = swap(y_payload(0), "gy", 1)
    rotor = rotor + first[96:]
    second = swap_next(y_payload(2), "gy")
    (acc,) = call(
        make_first_scatter(count_y),
        "first_scatter",
        [((512, 512), F32, VMEM)],
        [SMEM] + [VMEM] * 4,
        (mine, low, own, high, dst),
        [pltpu.VMEM((3, 4, 8, 128), F32), ints(40), ints(8)],
        flops=4 * 10**9,
    )
    rotor = rotor + second[96:]
    rotor = rotor + swap(rotor, "gx", 2)
    half_scratch = [pltpu.VMEM((256, 512), F32), pltpu.VMEM((6, 4, 8, 128), F32), ints(64), ints(8)]
    outer, fa, fb = call(
        make_outer_scatter(count_y),
        "outer_scatter",
        [((3, 256, 128), F32, VMEM), ((3, 64, 128), F32, VMEM), ((3, 64, 128), F32, VMEM)],
        [SMEM] + [VMEM] * 5,
        (mine, acc, first, second, dst, vel),
        half_scratch,
        flops=4 * 10**9,
    )
    xa = swap(jnp.concatenate([fa.reshape(192, 128), rotor], axis=0), "gx", 1)
    xb = swap_next(fb.reshape(192, 128), "gx")
    inner, fa, fb = call(
        make_inner_scatter(count_y),
        "inner_scatter",
        [((3, 256, 128), F32, VMEM), ((3, 8, 128), F32, VMEM), ((3, 8, 128), F32, VMEM)],
        [SMEM] + [VMEM] * 6,
        (mine, acc, first, second, dst, vel, outer),
        half_scratch,
        flops=4 * 10**9,
    )
    rotor, xb, fa, fb = lax.optimization_barrier((rotor + xa[192:], xb, fa, fb))
    ya = swap(fa, "gy", 1)
    yb = swap_next(fb, "gy")
    (force,) = call(
        forcing_kernel,
        "forcing",
        [((3, 512, 128), F32, VMEM)],
        [SMEM] + [VMEM] * 5,
        (mine, blade_tile, blade_cell, blade_coef, pts, rotor),
        [ints(32)],
        flops=10**6,
    )
    updated, forcing = call(
        make_stencil(count_y),
        "stencil",
        [((3, 8, 64, 128), F32, HBM), ((3, 512, 128), F32, HBM)],
        [SMEM] + [VMEM] * 7,
        (mine, outer, inner, force, xa, xb, ya, yb),
        [pltpu.VMEM((3, 8, 64, 128), F32), pltpu.SemaphoreType.DMA((9,))],
    )
    return updated, forcing.reshape(velocity.shape)


def solution(mesh):
    grid = P("gx", "gy", None)
    lists = P("gx", "gy", None, None)
    field = P(None, "gx", "gy", None)
    return jax.shard_map(
        body,
        mesh=mesh,
        in_specs=(field, grid, lists, lists, lists, P(), P(), P()),
        out_specs=(field, field),
        check_vma=False,
    )
```

```python
import jax
import jax.numpy as jnp
from jax import lax
from jax.experimental import pallas as pl
from jax.experimental.pallas import tpu as pltpu
from jax.sharding import PartitionSpec as P

F32 = jnp.float32
BF16 = jnp.bfloat16
VMEM = pl.BlockSpec(memory_space=pltpu.VMEM)
SMEM = pl.BlockSpec(memory_space=pltpu.SMEM)
HBM = pl.BlockSpec(memory_space=pltpu.HBM)


def halves(value):
    high = value.astype(BF16)
    low = (value - high.astype(F32)).astype(BF16)
    return high, low


def one_hot(extent, index):
    rows = lax.broadcasted_iota(jnp.int32, (extent, index.shape[1]), 0)
    return jnp.where(rows == index, 1.0, 0.0).astype(BF16)


def pick(table, cell):
    key = (cell & 127) | (((cell >> 15) & 1) << 7)
    place = (cell >> 7) & 255
    hot = one_hot(256, key)
    hot = jnp.concatenate([hot, hot], axis=0)
    here = lax.broadcasted_iota(jnp.int32, (256, cell.shape[1]), 0) == place
    out = []
    for c in range(3):
        found = jnp.dot(table[c], hot, preferred_element_type=F32)
        out.append(jnp.sum(jnp.where(here, found, 0.0), axis=0, keepdims=True))
    return out


def spread(extent, row, level, values):
    hot = one_hot(extent, row)
    at_level = lax.broadcasted_iota(jnp.int32, (128, level.shape[1]), 0) == level
    high, low = [], []
    for value in values:
        vh = value.astype(BF16).astype(F32)
        high.append(jnp.where(at_level, vh, 0.0).astype(BF16))
        low.append(jnp.where(at_level, value - vh, 0.0).astype(BF16))
    left = jnp.concatenate([hot, hot], axis=1)
    right = jnp.concatenate([jnp.concatenate(high, axis=0), jnp.concatenate(low, axis=0)], axis=1)
    return lax.dot_general(left, right, (((1,), (1,)), ((), ())), preferred_element_type=F32)


def sides(mine_ref, count_y):
    mine = mine_ref[0]
    return 1 - 2 * ((mine // count_y) & 1), 1 - 2 * (mine & 1)


def list_blocks(lists, listed):
    total = jnp.int32(0)
    for used, tag in lists:
        for j in range(8):
            listed[total + j] = tag * 8 + j
        total = total + ((used + 127) >> 7)
    return total


def run_chunks(total, large, small, chunk):
    many = (total + small - 1) // large

    def big(i, carry):
        chunk(i * large, large)
        return carry

    lax.fori_loop(0, many, big, 0)

    def rest(i, carry):
        chunk(many * large + i * small, small)
        return carry

    lax.fori_loop(0, jnp.maximum(total - many * large + small - 1, 0) // small, rest, 0)


def gather_lists(table, total, large, small, listed, direction, cnt_ref, src_ref, w_ref, out_ref):
    for k in range(large):
        listed[total + k] = listed[total - 1]

    def chunk(first, width):
        blocks = [listed[first + k] for k in range(width)]
        rows = [direction[b >> 3] * 8 + (b & 7) for b in blocks]
        cell = jnp.concatenate([src_ref[pl.ds(r, 1), :] for r in rows], axis=1)
        found = pick(table, cell)
        lane = lax.broadcasted_iota(jnp.int32, (1, 128), 1)
        for k, (b, r) in enumerate(zip(blocks, rows)):
            used = cnt_ref[0, 0, r >> 3]
            j = b & 7
            weight = jnp.where(lane + j * 128 < used, w_ref[pl.ds(r, 1), :], 0.0)
            for c in range(3):
                out_ref[b >> 3, c, pl.ds(j, 1), :] = found[c][:, k * 128 : (k + 1) * 128] * weight
            out_ref[b >> 3, 3, pl.ds(j, 1), :] = weight

    run_chunks(total, large, small, chunk)


def make_far_gather(count_y, large, small):
    def kernel(mine_ref, cnt_hbm, vel_hbm, src_hbm, w_hbm, dst_hbm, out_ref, table, vel_ref, src_ref, w_ref, dst_ref, sem, cnt_ref, listed, direction):
        half = vel_ref.shape[1] // 2
        pairs = [(cnt_hbm, cnt_ref), (src_hbm, src_ref)]
        pairs += [(vel_hbm.at[c], vel_ref.at[c]) for c in range(3)]
        pairs += [(w_hbm, w_ref), (dst_hbm, dst_ref)]
        copies = [pltpu.make_async_copy(a, b, sem.at[k]) for k, (a, b) in enumerate(pairs)]
        for copy in copies:
            copy.start()
        out_ref[...] = jnp.zeros_like(out_ref)
        copies[0].wait()
        side_x, side_y = sides(mine_ref, count_y)
        lists = []
        for s in range(2):
            for t in range(3):
                d = 3 * (side_x * (1 - 2 * s) + 1) + side_y * (1 - t) + 1
                direction[3 * s + t] = d
                lists.append((cnt_ref[0, 0, d], 3 * s + t))
        total = list_blocks(lists, listed)
        copies[1].wait()
        for c in range(3):
            copies[2 + c].wait()
            for piece in range(2):
                high, low = halves(vel_ref[c, piece * half : (piece + 1) * half, :])
                table[c, :, piece * 128 : (piece + 1) * 128] = high
                table[c, :, 256 + piece * 128 : 256 + (piece + 1) * 128] = low
        copies[5].wait()
        gather_lists(table, total, large, small, listed, direction, cnt_ref, src_ref, w_ref, out_ref)
        copies[6].wait()

    return kernel


def active_turbines(tile_ref, mine, listed):
    turbines = tile_ref.shape[0]
    owned = jnp.where(tile_ref[...] == mine, 1.0, 0.0)
    found = jnp.max(owned, axis=1, keepdims=True)
    total = jnp.int32(0)
    for t in range(turbines):
        listed[total] = t
        total = total + jnp.where(found[t, 0] > 0.5, 1, 0)
    listed[total] = 0
    return total


def points_kernel(mine_ref, table, tile_ref, cell_ref, pts_ref, rot_ref, tlist):
    turbines, points = tile_ref.shape
    pts_ref[...] = jnp.zeros_like(pts_ref)
    mine = mine_ref[0]
    n_turb = active_turbines(tile_ref, mine, tlist)

    def turbine(i, carry):
        pair = [tlist[2 * i], tlist[2 * i + 1]]
        cell = jnp.concatenate([cell_ref[pl.ds(t, 1), :] for t in pair], axis=1)
        found = pick(table, cell)
        for k, t in enumerate(pair):
            owned = tile_ref[pl.ds(t, 1), :] == mine
            for c in range(3):
                pts_ref[c, pl.ds(t, 1), :] = jnp.where(owned, found[c][:, k * points : (k + 1) * points], 0.0)
        return carry

    lax.fori_loop(0, (n_turb + 1) >> 1, turbine, 0)
    rot_ref[...] = jnp.zeros_like(rot_ref)
    sums = jnp.sum(pts_ref[0], axis=1, keepdims=True)
    rot_ref[0:turbines, :] = jnp.broadcast_to(sums, (turbines, 128))


def make_near_gather(count_y, large, small):
    def kernel(mine_ref, cnt_ref, table, src_ref, w_ref, out_ref, listed, direction):
        out_ref[...] = jnp.zeros_like(out_ref)
        _, side_y = sides(mine_ref, count_y)
        lists = []
        for t in range(3):
            d = 3 + side_y * (1 - t) + 1
            direction[t] = d
            lists.append((cnt_ref[0, 0, d], t))
        total = list_blocks(lists, listed)
        gather_lists(table, total, large, small, listed, direction, cnt_ref, src_ref, w_ref, out_ref)

    return kernel


def scatter_lists(val, n_lists, direction, dst_ref, listed, acc, extent, place, large, small):
    lists = []
    for q in range(n_lists):
        used = jnp.sum(jnp.where(val[q, 3] != 0.0, 1.0, 0.0)).astype(jnp.int32)
        lists.append((used, q))
    total = list_blocks(lists, listed)
    for k in range(large):
        listed[total + k] = 0

    def chunk(first, width):
        cells, vals = [], [[], [], [], []]
        for k in range(width):
            b = listed[first + k]
            q, j = b >> 3, b & 7
            keep = jnp.where(first + k < total, 1.0, 0.0)
            cells.append(dst_ref[pl.ds(direction[q] * 8 + j, 1), :])
            for c in range(4):
                vals[c].append(val[q, c, pl.ds(j, 1), :] * keep)
        cell = jnp.concatenate(cells, axis=1)
        vals = [jnp.concatenate(v, axis=1) for v in vals]
        acc[...] += spread(extent, place((cell >> 7) & 511), cell & 127, vals)

    run_chunks(total, large, small, chunk)


def make_first_scatter(count_y):
    def kernel(mine_ref, low_ref, own_ref, high_ref, dst_ref, acc, val, listed, direction):
        side_x, _ = sides(mine_ref, count_y)
        for q, ref in enumerate((low_ref, own_ref, high_ref)):
            val[q] = ref[1]
            direction[q] = 3 * (side_x * (q - 1) + 1) + 1
        acc[...] = jnp.zeros_like(acc)
        scatter_lists(val, 3, direction, dst_ref, listed, acc, 512, lambda row: row, 12, 4)

    return kernel


def load_later_lists(mine_ref, count_y, first_ref, second_ref, val, direction):
    side_x, side_y = sides(mine_ref, count_y)
    for t, ref in enumerate((first_ref, second_ref)):
        for s in range(3):
            q = 3 * t + s
            for c in range(4):
                at = (s * 4 + c) * 8
                val[q, c] = ref[at : at + 8, :]
            direction[q] = 3 * (side_x * (s - 1) + 1) + side_y * (2 * t - 1) + 1


def corrected(acc, vel, c):
    return (1.0 - acc[:, 384:512]) * vel - acc[:, c * 128 : (c + 1) * 128]


def make_outer_scatter(count_y):
    def kernel(mine_ref, base_ref, first_ref, second_ref, dst_ref, vel_ref, cor_ref, fa_ref, fb_ref, acc, val, listed, direction):
        load_later_lists(mine_ref, count_y, first_ref, second_ref, val, direction)
        acc[0:128, :] = base_ref[0:128, :]
        acc[128:256, :] = base_ref[384:512, :]
        place = lambda row: jnp.where(row < 128, row, jnp.where(row >= 384, row - 256, 512))
        scatter_lists(val, 6, direction, dst_ref, listed, acc, 256, place, 12, 4)
        side_x, _ = sides(mine_ref, count_y)
        for c in range(3):
            vel = jnp.concatenate([vel_ref[c, 0:128, :], vel_ref[c, 384:512, :]], axis=0)
            cor = corrected(acc, vel, c)
            cor_ref[c] = cor
            fa_ref[c] = jnp.where(side_x > 0, cor[192:256], cor[0:64])
            fb_ref[c] = jnp.where(side_x > 0, cor[0:64], cor[192:256])

    return kernel


def make_inner_scatter(count_y):
    def kernel(mine_ref, base_ref, first_ref, second_ref, dst_ref, vel_ref, outer_ref, cor_ref, fa_ref, fb_ref, acc, val, listed, direction):
        load_later_lists(mine_ref, count_y, first_ref, second_ref, val, direction)
        acc[...] = base_ref[128:384, :]
        scatter_lists(val, 6, direction, dst_ref, listed, acc, 256, lambda row: row - 128, 12, 4)
        _, side_y = sides(mine_ref, count_y)
        for c in range(3):
            cor_ref[c] = corrected(acc, vel_ref[c, 128:384, :], c)
            for x in range(8):
                ref, at = (cor_ref, x - 2) if 2 <= x < 6 else (outer_ref, x if x < 2 else x - 4)
                low = ref[c, at * 64 : at * 64 + 1, :]
                high = ref[c, at * 64 + 63 : at * 64 + 64, :]
                fa_ref[c, x : x + 1, :] = jnp.where(side_y > 0, high, low)
                fb_ref[c, x : x + 1, :] = jnp.where(side_y > 0, low, high)

    return kernel


def forcing_kernel(mine_ref, tile_ref, cell_ref, coef_ref, pts_ref, rot_ref, out_ref, tlist):
    out_ref[...] = jnp.zeros_like(out_ref)
    n_turb = active_turbines(tile_ref, mine_ref[0], tlist)
    points = tile_ref.shape[1]

    def turbine(i, carry):
        pair = [tlist[2 * i], tlist[2 * i + 1]]
        cell = jnp.concatenate([cell_ref[pl.ds(t, 1), :] for t in pair], axis=1)
        force = [[], [], []]
        for k, t in enumerate(pair):
            keep = jnp.where(2 * i + k < n_turb, 1.0 / points, 0.0)
            scale = -coef_ref[pl.ds(t, 1), :] * (rot_ref[pl.ds(t, 1), 0:1] * keep)
            for c in range(3):
                force[c].append(scale * pts_ref[c, pl.ds(t, 1), :])
        force = [jnp.concatenate(f, axis=1) for f in force]
        got = spread(512, (cell >> 7) & 511, cell & 127, force)
        for c in range(3):
            out_ref[c] += got[:, c * 128 : (c + 1) * 128]
        return carry

    lax.fori_loop(0, (n_turb + 1) >> 1, turbine, 0)


def make_stencil(count_y):
    def kernel(mine_ref, outer_ref, inner_ref, frc_ref, xa_ref, xb_ref, ya_ref, yb_ref, out_hbm, frc_hbm, out_ref, sem):
        side_x, side_y = sides(mine_ref, count_y)
        given = pltpu.make_async_copy(frc_ref, frc_hbm, sem.at[8])
        given.start()
        lane = lax.broadcasted_iota(jnp.int32, (64, 128), 1)

        def slab(c, x):
            if x < 0:
                return jnp.where(side_x > 0, xb_ref[c * 64 : c * 64 + 64, :], xa_ref[c * 64 : c * 64 + 64, :])
            if x > 7:
                return jnp.where(side_x > 0, xa_ref[c * 64 : c * 64 + 64, :], xb_ref[c * 64 : c * 64 + 64, :])
            ref, at = (inner_ref, x - 2) if 2 <= x < 6 else (outer_ref, x if x < 2 else x - 4)
            return ref[c, at * 64 : at * 64 + 64, :]

        copies = []
        for x in range(8):
            now = [slab(c, x) for c in range(3)]
            for c in range(3):
                u = now[c]
                west, east = slab(c, x - 1), slab(c, x + 1)
                ya, yb = ya_ref[c, x : x + 1, :], yb_ref[c, x : x + 1, :]
                south = jnp.concatenate([jnp.where(side_y > 0, yb, ya), u[:-1]], axis=0)
                north = jnp.concatenate([u[1:], jnp.where(side_y > 0, ya, yb)], axis=0)
                upper = jnp.where(lane == 127, 0.0, pltpu.roll(u, 127, 1))
                lower = jnp.where(lane == 0, 0.0, pltpu.roll(u, 1, 1))
                laplace = east + west + north + south + upper + lower - 6.0 * u
                advect = (
                    now[0] * (east - west) * 0.5
                    + now[1] * (north - south) * 0.5
                    + now[2] * (upper - lower) * 0.5
                )
                out_ref[c, x] = u + 0.2 * (0.15 * laplace - advect + frc_ref[c, x * 64 : x * 64 + 64, :])
            copies.append(pltpu.make_async_copy(out_ref.at[:, x], out_hbm.at[:, x], sem.at[x]))
            copies[-1].start()
        for copy in copies:
            copy.wait()
        given.wait()

    return kernel


def swap(value, axis, step):
    count = lax.axis_size(axis)
    return lax.ppermute(value, axis, [(i, i ^ step) for i in range(count)])


def swap_next(value, axis):
    count = lax.axis_size(axis)
    return lax.ppermute(value, axis, [(i, (i - 1 if i % 2 == 0 else i + 1) % count) for i in range(count)])


def call(kernel, name, outs, ins, args, scratch=(), flops=10**9, limit=32):
    return pl.pallas_call(
        kernel,
        out_shape=tuple(jax.ShapeDtypeStruct(shape, dtype) for shape, dtype, _ in outs),
        in_specs=ins,
        out_specs=tuple(spec for _, _, spec in outs),
        scratch_shapes=list(scratch),
        compiler_params=pltpu.CompilerParams(vmem_limit_bytes=limit << 20),
        cost_estimate=pl.CostEstimate(flops=flops, bytes_accessed=10**5, transcendentals=0),
        name=name,
    )(*args)


def body(velocity, counts, src_cell, weights, dst_cell, blade_tile, blade_cell, blade_coef):
    vel = velocity.reshape(3, 512, 128)
    src = src_cell.reshape(72, 128)
    weight = weights.reshape(72, 128)
    dst = dst_cell.reshape(72, 128)
    turbines, points = blade_cell.shape
    count_x, count_y = lax.axis_size("gx"), lax.axis_size("gy")
    mine = (lax.axis_index("gx") * count_y + lax.axis_index("gy")).reshape(1).astype(jnp.int32)
    rows_t = turbines + -turbines % 8
    ints = lambda n: pltpu.SMEM((n,), jnp.int32)

    whole = ((72, 128), jnp.int32, VMEM)
    far, table, vel, src, weight, dst = call(
        make_far_gather(count_y, 12, 4),
        "far_gather",
        [((6, 4, 8, 128), F32, VMEM), ((3, 256, 512), BF16, VMEM), ((3, 512, 128), F32, VMEM), whole, ((72, 128), F32, VMEM), whole],
        [SMEM] + [HBM] * 5,
        (mine,) + tuple(pltpu.with_memory_space_constraint(v, pltpu.HBM) for v in (counts, vel, src, weight, dst)),
        [pltpu.SemaphoreType.DMA((7,)), pltpu.SMEM((1, 1, 9), jnp.int32), ints(72), ints(8)],
        flops=5 * 10**9,
    )
    low = swap(far[0:3], "gx", 1)
    high = swap_next(far[3:6], "gx")
    pts, rotor = call(
        points_kernel,
        "points",
        [((3, turbines, points), F32, VMEM), ((rows_t, 128), F32, VMEM)],
        [SMEM] + [VMEM] * 3,
        (mine, table, blade_tile, blade_cell),
        [ints(32)],
        flops=10**9,
    )
    (own,) = call(
        make_near_gather(count_y, 8, 4),
        "near_gather",
        [((3, 4, 8, 128), F32, VMEM)],
        [SMEM, SMEM] + [VMEM] * 3,
        (mine, counts, table, src, weight),
        [ints(48), ints(8)],
        flops=4 * 10**9,
    )
    for axis, count in (("gx", count_x), ("gy", count_y)):
        step = 4
        while step < count:
            rotor = rotor + swap(rotor, axis, step)
            step *= 2

    def y_payload(t):
        parts = [part[t].reshape(32, 128) for part in (low, own, high)]
        return jnp.concatenate(parts + [rotor], axis=0)

    first = swap(y_payload(0), "gy", 1)
    rotor = rotor + first[96:]
    second = swap_next(y_payload(2), "gy")
    (acc,) = call(
        make_first_scatter(count_y),
        "first_scatter",
        [((512, 512), F32, VMEM)],
        [SMEM] + [VMEM] * 4,
        (mine, low, own, high, dst),
        [pltpu.VMEM((3, 4, 8, 128), F32), ints(48), ints(8)],
        flops=4 * 10**9,
    )
    rotor = rotor + second[96:]
    rotor = rotor + swap(rotor, "gx", 2)
    half_scratch = [pltpu.VMEM((256, 512), F32), pltpu.VMEM((6, 4, 8, 128), F32), ints(72), ints(8)]
    outer, fa, fb = call(
        make_outer_scatter(count_y),
        "outer_scatter",
        [((3, 256, 128), F32, VMEM), ((3, 64, 128), F32, VMEM), ((3, 64, 128), F32, VMEM)],
        [SMEM] + [VMEM] * 5,
        (mine, acc, first, second, dst, vel),
        half_scratch,
        flops=4 * 10**9,
    )
    xa = swap(jnp.concatenate([fa.reshape(192, 128), rotor], axis=0), "gx", 1)
    xb = swap_next(fb.reshape(192, 128), "gx")
    inner, fa, fb = call(
        make_inner_scatter(count_y),
        "inner_scatter",
        [((3, 256, 128), F32, VMEM), ((3, 8, 128), F32, VMEM), ((3, 8, 128), F32, VMEM)],
        [SMEM] + [VMEM] * 6,
        (mine, acc, first, second, dst, vel, outer),
        half_scratch,
        flops=4 * 10**9,
    )
    rotor, xb, fa, fb = lax.optimization_barrier((rotor + xa[192:], xb, fa, fb))
    ya = swap(fa, "gy", 1)
    yb = swap_next(fb, "gy")
    (force,) = call(
        forcing_kernel,
        "forcing",
        [((3, 512, 128), F32, VMEM)],
        [SMEM] + [VMEM] * 5,
        (mine, blade_tile, blade_cell, blade_coef, pts, rotor),
        [ints(32)],
        flops=10**6,
    )
    updated, forcing = call(
        make_stencil(count_y),
        "stencil",
        [((3, 8, 64, 128), F32, HBM), ((3, 512, 128), F32, HBM)],
        [SMEM] + [VMEM] * 7,
        (mine, outer, inner, force, xa, xb, ya, yb),
        [pltpu.VMEM((3, 8, 64, 128), F32), pltpu.SemaphoreType.DMA((9,))],
    )
    return updated, forcing.reshape(velocity.shape)


def solution(mesh):
    grid = P("gx", "gy", None)
    lists = P("gx", "gy", None, None)
    field = P(None, "gx", "gy", None)
    return jax.shard_map(
        body,
        mesh=mesh,
        in_specs=(field, grid, lists, lists, lists, P(), P(), P()),
        out_specs=(field, field),
        check_vma=False,
    )
```

```python
import jax
import jax.numpy as jnp
from jax import lax
from jax.experimental import pallas as pl
from jax.experimental.pallas import tpu as pltpu
from jax.sharding import PartitionSpec as P

F32 = jnp.float32
BF16 = jnp.bfloat16
VMEM = pl.BlockSpec(memory_space=pltpu.VMEM)
SMEM = pl.BlockSpec(memory_space=pltpu.SMEM)
HBM = pl.BlockSpec(memory_space=pltpu.HBM)


def halves(value):
    high = value.astype(BF16)
    low = (value - high.astype(F32)).astype(BF16)
    return high, low


def one_hot(extent, index):
    rows = lax.broadcasted_iota(jnp.int32, (extent, index.shape[1]), 0)
    return jnp.where(rows == index, 1.0, 0.0).astype(BF16)


def pick(table, cell):
    key = (cell & 127) | (((cell >> 15) & 1) << 7)
    place = (cell >> 7) & 255
    hot = one_hot(256, key)
    hot = jnp.concatenate([hot, hot], axis=0)
    here = lax.broadcasted_iota(jnp.int32, (256, cell.shape[1]), 0) == place
    out = []
    for c in range(3):
        found = jnp.dot(table[c], hot, preferred_element_type=F32)
        out.append(jnp.sum(jnp.where(here, found, 0.0), axis=0, keepdims=True))
    return out


def spread(extent, row, level, values):
    hot = one_hot(extent, row)
    at_level = lax.broadcasted_iota(jnp.int32, (128, level.shape[1]), 0) == level
    high, low = [], []
    for value in values:
        vh = value.astype(BF16).astype(F32)
        high.append(jnp.where(at_level, vh, 0.0).astype(BF16))
        low.append(jnp.where(at_level, value - vh, 0.0).astype(BF16))
    left = jnp.concatenate([hot, hot], axis=1)
    right = jnp.concatenate([jnp.concatenate(high, axis=0), jnp.concatenate(low, axis=0)], axis=1)
    return lax.dot_general(left, right, (((1,), (1,)), ((), ())), preferred_element_type=F32)


def sides(mine_ref, count_y):
    mine = mine_ref[0]
    return 1 - 2 * ((mine // count_y) & 1), 1 - 2 * (mine & 1)


def list_blocks(lists, listed):
    total = jnp.int32(0)
    for used, tag in lists:
        for j in range(8):
            listed[total + j] = tag * 8 + j
        total = total + ((used + 127) >> 7)
    return total


def run_chunks(total, large, small, chunk):
    many = (total + small - 1) // large

    def big(i, carry):
        chunk(i * large, large)
        return carry

    lax.fori_loop(0, many, big, 0)

    def rest(i, carry):
        chunk(many * large + i * small, small)
        return carry

    lax.fori_loop(0, jnp.maximum(total - many * large + small - 1, 0) // small, rest, 0)


def gather_lists(table, total, large, small, listed, direction, src_ref, w_ref, out_ref):
    for k in range(large):
        listed[total + k] = listed[total - 1]

    def chunk(first, width):
        blocks = [listed[first + k] for k in range(width)]
        rows = [direction[b >> 3] * 8 + (b & 7) for b in blocks]
        cell = jnp.concatenate([src_ref[pl.ds(r, 1), :] for r in rows], axis=1)
        found = pick(table, cell)
        for k, (b, r) in enumerate(zip(blocks, rows)):
            j = b & 7
            weight = w_ref[pl.ds(r, 1), :]
            for c in range(3):
                out_ref[b >> 3, c, pl.ds(j, 1), :] = found[c][:, k * 128 : (k + 1) * 128] * weight
            out_ref[b >> 3, 3, pl.ds(j, 1), :] = weight

    run_chunks(total, large, small, chunk)


def make_far_gather(count_y, large, small):
    def kernel(
        mine_ref, cnt_hbm, vel_hbm, src_hbm, w_hbm, dst_hbm, tile_hbm, cell_hbm,
        out_ref, table, vel_ref, src_ref, w_ref, dst_ref, tile_ref, cell_ref, pts_ref, rot_ref,
        sem, cnt_ref, listed, direction, tlist,
    ):
        half = vel_ref.shape[1] // 2
        pairs = [(cnt_hbm, cnt_ref), (src_hbm, src_ref), (w_hbm, w_ref)]
        pairs += [(vel_hbm.at[c], vel_ref.at[c]) for c in range(3)]
        pairs += [(tile_hbm, tile_ref), (cell_hbm, cell_ref), (dst_hbm, dst_ref)]
        copies = [pltpu.make_async_copy(a, b, sem.at[k]) for k, (a, b) in enumerate(pairs)]
        for copy in copies:
            copy.start()
        out_ref[...] = jnp.zeros_like(out_ref)
        pts_ref[...] = jnp.zeros_like(pts_ref)
        rot_ref[...] = jnp.zeros_like(rot_ref)
        for copy in copies[:3]:
            copy.wait()
        slot = lax.broadcasted_iota(jnp.int32, (8, 128), 0) * 128 + lax.broadcasted_iota(jnp.int32, (8, 128), 1)
        for d in range(9):
            part = slice(d * 8, d * 8 + 8)
            w_ref[part, :] = jnp.where(slot < cnt_ref[0, 0, d], w_ref[part, :], 0.0)
        side_x, side_y = sides(mine_ref, count_y)
        lists = []
        for s in range(2):
            for t in range(3):
                d = 3 * (side_x * (1 - 2 * s) + 1) + side_y * (1 - t) + 1
                direction[3 * s + t] = d
                lists.append((cnt_ref[0, 0, d], 3 * s + t))
        total = list_blocks(lists, listed)
        for c in range(3):
            copies[3 + c].wait()
            for piece in range(2):
                high, low = halves(vel_ref[c, piece * half : (piece + 1) * half, :])
                table[c, :, piece * 128 : (piece + 1) * 128] = high
                table[c, :, 256 + piece * 128 : 256 + (piece + 1) * 128] = low
        for copy in copies[6:]:
            copy.wait()
        gather_lists(table, total, large, small, listed, direction, src_ref, w_ref, out_ref)
        gather_points(mine_ref[0], table, tile_ref, cell_ref, pts_ref, rot_ref, tlist)

    return kernel


def active_turbines(tile_ref, mine, listed):
    turbines = tile_ref.shape[0]
    owned = jnp.where(tile_ref[...] == mine, 1.0, 0.0)
    found = jnp.max(owned, axis=1, keepdims=True)
    total = jnp.int32(0)
    for t in range(turbines):
        listed[total] = t
        total = total + jnp.where(found[t, 0] > 0.5, 1, 0)
    listed[total] = 0
    return total


def gather_points(mine, table, tile_ref, cell_ref, pts_ref, rot_ref, tlist):
    turbines, points = tile_ref.shape
    n_turb = active_turbines(tile_ref, mine, tlist)

    def turbine(i, carry):
        pair = [tlist[2 * i], tlist[2 * i + 1]]
        cell = jnp.concatenate([cell_ref[pl.ds(t, 1), :] for t in pair], axis=1)
        found = pick(table, cell)
        for k, t in enumerate(pair):
            owned = tile_ref[pl.ds(t, 1), :] == mine
            for c in range(3):
                pts_ref[c, pl.ds(t, 1), :] = jnp.where(owned, found[c][:, k * points : (k + 1) * points], 0.0)
        return carry

    lax.fori_loop(0, (n_turb + 1) >> 1, turbine, 0)
    sums = jnp.sum(pts_ref[0], axis=1, keepdims=True)
    rot_ref[0:turbines, :] = jnp.broadcast_to(sums, (turbines, 128))


def used_slots(weight):
    return jnp.sum(jnp.where(weight != 0.0, 1.0, 0.0)).astype(jnp.int32)


def make_near_gather(count_y, large, small):
    def kernel(mine_ref, table, src_ref, w_ref, out_ref, listed, direction):
        out_ref[...] = jnp.zeros_like(out_ref)
        _, side_y = sides(mine_ref, count_y)
        used = [used_slots(w_ref[d * 8 : d * 8 + 8, :]) for d in (3, 4, 5)]
        last = jnp.where(side_y > 0, used[0], used[2])
        lists = [(jnp.where(side_y > 0, used[2], used[0]), 0), (used[1], 1), (last, 2)]
        for t in range(3):
            direction[t] = 3 + side_y * (1 - t) + 1
        total = list_blocks(lists, listed)
        gather_lists(table, total, large, small, listed, direction, src_ref, w_ref, out_ref)

    return kernel


def scatter_lists(val, n_lists, direction, dst_ref, listed, acc, extent, place, large, small):
    lists = []
    for q in range(n_lists):
        lists.append((used_slots(val[q, 3]), q))
    total = list_blocks(lists, listed)
    for k in range(large):
        listed[total + k] = 0

    def chunk(first, width):
        cells, vals = [], [[], [], [], []]
        for k in range(width):
            b = listed[first + k]
            q, j = b >> 3, b & 7
            keep = jnp.where(first + k < total, 1.0, 0.0)
            cells.append(dst_ref[pl.ds(direction[q] * 8 + j, 1), :])
            for c in range(4):
                vals[c].append(val[q, c, pl.ds(j, 1), :] * keep)
        cell = jnp.concatenate(cells, axis=1)
        vals = [jnp.concatenate(v, axis=1) for v in vals]
        acc[...] += spread(extent, place((cell >> 7) & 511), cell & 127, vals)

    run_chunks(total, large, small, chunk)


def make_first_scatter(count_y):
    def kernel(mine_ref, low_ref, own_ref, high_ref, dst_ref, acc, val, listed, direction):
        side_x, _ = sides(mine_ref, count_y)
        for q, ref in enumerate((low_ref, own_ref, high_ref)):
            for c in range(4):
                val[q, c] = ref[32 + c * 8 : 40 + c * 8, :]
            direction[q] = 3 * (side_x * (q - 1) + 1) + 1
        acc[...] = jnp.zeros_like(acc)
        scatter_lists(val, 3, direction, dst_ref, listed, acc, 512, lambda row: row, 12, 4)

    return kernel


def load_later_lists(mine_ref, count_y, first_ref, second_ref, val, direction):
    side_x, side_y = sides(mine_ref, count_y)
    for t, ref in enumerate((first_ref, second_ref)):
        for s in range(3):
            q = 3 * t + s
            for c in range(4):
                at = (s * 4 + c) * 8
                val[q, c] = ref[at : at + 8, :]
            direction[q] = 3 * (side_x * (s - 1) + 1) + side_y * (2 * t - 1) + 1


def corrected(acc, vel, c):
    return (1.0 - acc[:, 384:512]) * vel - acc[:, c * 128 : (c + 1) * 128]


def edge_rows(ref, c, columns):
    at = (lambda r: ref[r, columns]) if c is None else (lambda r: ref[c, r, columns])
    spare = [at(slice(0, 2))]
    low = [at(slice(x * 64, x * 64 + 1)) for x in range(1, 7)]
    high = [at(slice(x * 64 + 63, x * 64 + 64)) for x in range(1, 7)]
    return jnp.concatenate([at(slice(0, 64)), at(slice(448, 512))] + low + spare + high + spare, axis=0)


def edge_place(row):
    x, y = row >> 6, row & 63
    inside = jnp.where(y == 0, 127 + x, jnp.where(y == 63, 135 + x, 1024))
    return jnp.where(x == 0, y, jnp.where(x == 7, 64 + y, inside))


def make_edge_scatter(count_y):
    def kernel(
        mine_ref, base_ref, first_ref, second_ref, dst_ref, vel_ref,
        cor_ref, xa_ref, xb_ref, ya_ref, yb_ref, acc, val, listed, direction,
    ):
        load_later_lists(mine_ref, count_y, first_ref, second_ref, val, direction)
        acc[...] = edge_rows(base_ref, None, slice(None))
        scatter_lists(val, 6, direction, dst_ref, listed, acc, 144, edge_place, 12, 4)
        side_x, side_y = sides(mine_ref, count_y)
        for c in range(3):
            cor = corrected(acc, edge_rows(vel_ref, c, slice(None)), c)
            cor_ref[c] = cor[0:128]
            xa_ref[c] = jnp.where(side_x > 0, cor[64:128], cor[0:64])
            xb_ref[c] = jnp.where(side_x > 0, cor[0:64], cor[64:128])
            low = jnp.concatenate([cor[0:1], cor[128:134], cor[64:65]], axis=0)
            high = jnp.concatenate([cor[63:64], cor[136:142], cor[127:128]], axis=0)
            ya_ref[c] = jnp.where(side_y > 0, high, low)
            yb_ref[c] = jnp.where(side_y > 0, low, high)

    return kernel


def make_inner_scatter(count_y):
    def kernel(mine_ref, base_ref, first_ref, second_ref, dst_ref, vel_ref, cor_ref, acc, val, listed, direction):
        load_later_lists(mine_ref, count_y, first_ref, second_ref, val, direction)
        acc[...] = base_ref[64:448, :]
        scatter_lists(val, 6, direction, dst_ref, listed, acc, 384, lambda row: row - 64, 12, 4)
        for c in range(3):
            cor_ref[c] = corrected(acc, vel_ref[c, 64:448, :], c)

    return kernel


def add_forces(mine, tile_ref, cell_ref, coef_ref, pts_ref, rot_ref, out_ref, tlist):
    out_ref[...] = jnp.zeros_like(out_ref)
    n_turb = active_turbines(tile_ref, mine, tlist)
    points = tile_ref.shape[1]

    def turbine(i, carry):
        pair = [tlist[2 * i], tlist[2 * i + 1]]
        cell = jnp.concatenate([cell_ref[pl.ds(t, 1), :] for t in pair], axis=1)
        force = [[], [], []]
        for k, t in enumerate(pair):
            keep = jnp.where(2 * i + k < n_turb, 1.0 / points, 0.0)
            scale = -coef_ref[pl.ds(t, 1), :] * (rot_ref[pl.ds(t, 1), 0:1] * keep)
            for c in range(3):
                force[c].append(scale * pts_ref[c, pl.ds(t, 1), :])
        force = [jnp.concatenate(f, axis=1) for f in force]
        got = spread(512, (cell >> 7) & 511, cell & 127, force)
        for c in range(3):
            out_ref[c] += got[:, c * 128 : (c + 1) * 128]
        return carry

    lax.fori_loop(0, (n_turb + 1) >> 1, turbine, 0)


def make_stencil(count_y):
    def kernel(
        mine_ref, edge_ref, inner_ref, tile_ref, cell_ref, coef_ref, pts_ref, rot_ref, xa_ref, xb_ref, ya_ref, yb_ref,
        out_hbm, frc_hbm, out_ref, frc_ref, sem, tlist,
    ):
        add_forces(mine_ref[0], tile_ref, cell_ref, coef_ref, pts_ref, rot_ref, frc_ref, tlist)
        given = pltpu.make_async_copy(frc_ref, frc_hbm, sem.at[8])
        given.start()
        side_x, side_y = sides(mine_ref, count_y)
        lane = lax.broadcasted_iota(jnp.int32, (64, 128), 1)

        def slab(c, x):
            if x < 0:
                return jnp.where(side_x > 0, xb_ref[c * 64 : c * 64 + 64, :], xa_ref[c * 64 : c * 64 + 64, :])
            if x > 7:
                return jnp.where(side_x > 0, xa_ref[c * 64 : c * 64 + 64, :], xb_ref[c * 64 : c * 64 + 64, :])
            ref, at = (inner_ref, x - 1) if 1 <= x < 7 else (edge_ref, 0 if x == 0 else 1)
            return ref[c, at * 64 : at * 64 + 64, :]

        copies = []
        for x in range(8):
            now = [slab(c, x) for c in range(3)]
            for c in range(3):
                u = now[c]
                west, east = slab(c, x - 1), slab(c, x + 1)
                ya, yb = ya_ref[c, x : x + 1, :], yb_ref[c, x : x + 1, :]
                south = jnp.concatenate([jnp.where(side_y > 0, yb, ya), u[:-1]], axis=0)
                north = jnp.concatenate([u[1:], jnp.where(side_y > 0, ya, yb)], axis=0)
                upper = jnp.where(lane == 127, 0.0, pltpu.roll(u, 127, 1))
                lower = jnp.where(lane == 0, 0.0, pltpu.roll(u, 1, 1))
                laplace = east + west + north + south + upper + lower - 6.0 * u
                advect = (
                    now[0] * (east - west) * 0.5
                    + now[1] * (north - south) * 0.5
                    + now[2] * (upper - lower) * 0.5
                )
                out_ref[c, x] = u + 0.2 * (0.15 * laplace - advect + frc_ref[c, x * 64 : x * 64 + 64, :])
            copies.append(pltpu.make_async_copy(out_ref.at[:, x], out_hbm.at[:, x], sem.at[x]))
            copies[-1].start()
        for copy in copies:
            copy.wait()
        given.wait()

    return kernel


def swap(value, axis, step):
    count = lax.axis_size(axis)
    return lax.ppermute(value, axis, [(i, i ^ step) for i in range(count)])


def swap_next(value, axis):
    count = lax.axis_size(axis)
    return lax.ppermute(value, axis, [(i, (i - 1 if i % 2 == 0 else i + 1) % count) for i in range(count)])


def call(kernel, name, outs, ins, args, scratch=(), flops=10**9, limit=32):
    return pl.pallas_call(
        kernel,
        out_shape=tuple(jax.ShapeDtypeStruct(shape, dtype) for shape, dtype, _ in outs),
        in_specs=ins,
        out_specs=tuple(spec for _, _, spec in outs),
        scratch_shapes=list(scratch),
        compiler_params=pltpu.CompilerParams(vmem_limit_bytes=limit << 20),
        cost_estimate=pl.CostEstimate(flops=flops, bytes_accessed=10**5, transcendentals=0),
        name=name,
    )(*args)


def body(velocity, counts, src_cell, weights, dst_cell, blade_tile, blade_cell, blade_coef):
    vel = velocity.reshape(3, 512, 128)
    src = src_cell.reshape(72, 128)
    weight = weights.reshape(72, 128)
    dst = dst_cell.reshape(72, 128)
    turbines, points = blade_cell.shape
    count_x, count_y = lax.axis_size("gx"), lax.axis_size("gy")
    mine = (lax.axis_index("gx") * count_y + lax.axis_index("gy")).reshape(1).astype(jnp.int32)
    rows_t = turbines + -turbines % 8
    ints = lambda n: pltpu.SMEM((n,), jnp.int32)

    whole = ((72, 128), jnp.int32, VMEM)
    ints_t = (blade_tile.shape, jnp.int32, VMEM)
    given = (counts, vel, src, weight, dst, blade_tile, blade_cell)
    far, table, vel, src, weight, dst, tile, cell, pts, rotor = call(
        make_far_gather(count_y, 12, 4),
        "far_gather",
        [((6, 4, 8, 128), F32, VMEM), ((3, 256, 512), BF16, VMEM), ((3, 512, 128), F32, VMEM), whole]
        + [((72, 128), F32, VMEM), whole, ints_t, ints_t]
        + [((3, turbines, points), F32, VMEM), ((rows_t, 128), F32, VMEM)],
        [SMEM] + [HBM] * 7,
        (mine,) + tuple(pltpu.with_memory_space_constraint(v, pltpu.HBM) for v in given),
        [pltpu.SemaphoreType.DMA((9,)), pltpu.SMEM((1, 1, 9), jnp.int32), ints(72), ints(8), ints(32)],
        flops=5 * 10**9,
    )
    low = swap(jnp.concatenate([far[0:3].reshape(96, 128), rotor], axis=0), "gx", 1)
    high = swap_next(far[3:6].reshape(96, 128), "gx")
    (own,) = call(
        make_near_gather(count_y, 8, 4),
        "near_gather",
        [((3, 4, 8, 128), F32, VMEM)],
        [SMEM] + [VMEM] * 3,
        (mine, table, src, weight),
        [ints(48), ints(8)],
        flops=4 * 10**9,
    )
    rotor = rotor + low[96:]
    own = own.reshape(96, 128)

    def y_payload(t):
        return jnp.concatenate([part[t * 32 : t * 32 + 32] for part in (low, own, high)] + [rotor], axis=0)

    first = swap(y_payload(0), "gy", 1)
    rotor = rotor + first[96:]
    second = swap_next(y_payload(2), "gy")
    (acc,) = call(
        make_first_scatter(count_y),
        "first_scatter",
        [((512, 512), F32, VMEM)],
        [SMEM] + [VMEM] * 4,
        (mine, low, own, high, dst),
        [pltpu.VMEM((3, 4, 8, 128), F32), ints(48), ints(8)],
        flops=4 * 10**9,
    )
    rotor = rotor + second[96:]
    for axis, count in (("gx", count_x), ("gy", count_y)):
        step = 4
        while step < count:
            rotor = rotor + swap(rotor, axis, step)
            step *= 2
    lists = pltpu.VMEM((6, 4, 8, 128), F32)
    face_x, face_y = ((3, 64, 128), F32, VMEM), ((3, 8, 128), F32, VMEM)
    edge, xa, xb, ya, yb = call(
        make_edge_scatter(count_y),
        "edge_scatter",
        [((3, 128, 128), F32, VMEM), face_x, face_x, face_y, face_y],
        [SMEM] + [VMEM] * 5,
        (mine, acc, first, second, dst, vel),
        [pltpu.VMEM((144, 512), F32), lists, ints(72), ints(8)],
        flops=4 * 10**9,
    )
    xb = swap_next(jnp.concatenate([xb.reshape(192, 128), rotor], axis=0), "gx")
    xa = swap(xa.reshape(192, 128), "gx", 1)
    ya = swap(ya, "gy", 1)
    yb = swap_next(yb, "gy")
    (inner,) = call(
        make_inner_scatter(count_y),
        "inner_scatter",
        [((3, 384, 128), F32, VMEM)],
        [SMEM] + [VMEM] * 5,
        (mine, acc, first, second, dst, vel),
        [pltpu.VMEM((384, 512), F32), lists, ints(72), ints(8)],
        flops=6 * 10**9,
    )
    rotor = rotor + xb[192:]
    updated, forcing = call(
        make_stencil(count_y),
        "stencil",
        [((3, 8, 64, 128), F32, HBM), ((3, 512, 128), F32, HBM)],
        [SMEM] + [VMEM] * 11,
        (mine, edge, inner, tile, cell, blade_coef, pts, rotor, xa, xb, ya, yb),
        [pltpu.VMEM((3, 8, 64, 128), F32), pltpu.VMEM((3, 512, 128), F32), pltpu.SemaphoreType.DMA((9,)), ints(32)],
    )
    return updated, forcing.reshape(velocity.shape)


def solution(mesh):
    grid = P("gx", "gy", None)
    lists = P("gx", "gy", None, None)
    field = P(None, "gx", "gy", None)
    return jax.shard_map(
        body,
        mesh=mesh,
        in_specs=(field, grid, lists, lists, lists, P(), P(), P()),
        out_specs=(field, field),
        check_vma=False,
    )
```

```python
import jax
import jax.numpy as jnp
from jax import lax
from jax.experimental import pallas as pl
from jax.experimental.pallas import tpu as pltpu
from jax.sharding import PartitionSpec as P

F32 = jnp.float32
BF16 = jnp.bfloat16
VMEM = pl.BlockSpec(memory_space=pltpu.VMEM)
SMEM = pl.BlockSpec(memory_space=pltpu.SMEM)
HBM = pl.BlockSpec(memory_space=pltpu.HBM)


def halves(value):
    high = value.astype(BF16)
    low = (value - high.astype(F32)).astype(BF16)
    return high, low


def one_hot(extent, index):
    rows = lax.broadcasted_iota(jnp.int32, (extent, index.shape[1]), 0)
    return jnp.where(rows == index, 1.0, 0.0).astype(BF16)


def pick(table, cell):
    key = (cell & 127) | (((cell >> 15) & 1) << 7)
    place = (cell >> 7) & 255
    hot = one_hot(256, key)
    hot = jnp.concatenate([hot, hot], axis=0)
    here = lax.broadcasted_iota(jnp.int32, (256, cell.shape[1]), 0) == place
    out = []
    for c in range(3):
        found = jnp.dot(table[c], hot, preferred_element_type=F32)
        out.append(jnp.sum(jnp.where(here, found, 0.0), axis=0, keepdims=True))
    return out


def spread(extent, row, level, values):
    hot = one_hot(extent, row)
    at_level = lax.broadcasted_iota(jnp.int32, (128, level.shape[1]), 0) == level
    high, low = [], []
    for value in values:
        vh = value.astype(BF16).astype(F32)
        high.append(jnp.where(at_level, vh, 0.0).astype(BF16))
        low.append(jnp.where(at_level, value - vh, 0.0).astype(BF16))
    left = jnp.concatenate([hot, hot], axis=1)
    right = jnp.concatenate([jnp.concatenate(high, axis=0), jnp.concatenate(low, axis=0)], axis=1)
    return lax.dot_general(left, right, (((1,), (1,)), ((), ())), preferred_element_type=F32)


def sides(mine_ref, count_y):
    mine = mine_ref[0]
    return 1 - 2 * ((mine // count_y) & 1), 1 - 2 * (mine & 1)


def list_blocks(lists, listed):
    total = jnp.int32(0)
    for used, tag in lists:
        for j in range(8):
            listed[total + j] = tag * 8 + j
        total = total + ((used + 127) >> 7)
    return total


def run_chunks(total, large, small, chunk):
    many = (total + small - 1) // large

    def big(i, carry):
        chunk(i * large, large)
        return carry

    lax.fori_loop(0, many, big, 0)

    def rest(i, carry):
        chunk(many * large + i * small, small)
        return carry

    lax.fori_loop(0, jnp.maximum(total - many * large + small - 1, 0) // small, rest, 0)


def gather_lists(table, total, large, small, listed, direction, src_ref, w_ref, out_ref):
    for k in range(large):
        listed[total + k] = listed[total - 1]

    def chunk(first, width):
        blocks = [listed[first + k] for k in range(width)]
        rows = [direction[b >> 3] * 8 + (b & 7) for b in blocks]
        cell = jnp.concatenate([src_ref[pl.ds(r, 1), :] for r in rows], axis=1)
        found = pick(table, cell)
        for k, (b, r) in enumerate(zip(blocks, rows)):
            j = b & 7
            weight = w_ref[pl.ds(r, 1), :]
            for c in range(3):
                out_ref[b >> 3, c, pl.ds(j, 1), :] = found[c][:, k * 128 : (k + 1) * 128] * weight
            out_ref[b >> 3, 3, pl.ds(j, 1), :] = weight

    run_chunks(total, large, small, chunk)


def make_far_gather(count_y, large, small):
    def kernel(
        mine_ref, cnt_hbm, vel_hbm, src_hbm, w_hbm, dst_hbm, tile_hbm, cell_hbm, coef_hbm,
        out_ref, table, vel_ref, src_ref, w_ref, dst_ref, tile_ref, cell_ref, coef_ref, pts_ref, rot_ref,
        sem, cnt_ref, listed, direction, tlist,
    ):
        half = vel_ref.shape[1] // 2
        pairs = [(cnt_hbm, cnt_ref), (src_hbm, src_ref), (w_hbm, w_ref)]
        pairs += [(vel_hbm.at[c], vel_ref.at[c]) for c in range(3)]
        pairs += [(tile_hbm, tile_ref), (cell_hbm, cell_ref), (coef_hbm, coef_ref), (dst_hbm, dst_ref)]
        copies = [pltpu.make_async_copy(a, b, sem.at[k]) for k, (a, b) in enumerate(pairs)]
        for copy in copies:
            copy.start()
        out_ref[...] = jnp.zeros_like(out_ref)
        pts_ref[...] = jnp.zeros_like(pts_ref)
        rot_ref[...] = jnp.zeros_like(rot_ref)
        for copy in copies[:3]:
            copy.wait()
        slot = lax.broadcasted_iota(jnp.int32, (8, 128), 0) * 128 + lax.broadcasted_iota(jnp.int32, (8, 128), 1)
        for d in range(9):
            part = slice(d * 8, d * 8 + 8)
            w_ref[part, :] = jnp.where(slot < cnt_ref[0, 0, d], w_ref[part, :], 0.0)
        side_x, side_y = sides(mine_ref, count_y)
        lists = []
        for s in range(2):
            for t in range(3):
                d = 3 * (side_x * (1 - 2 * s) + 1) + side_y * (1 - t) + 1
                direction[3 * s + t] = d
                lists.append((cnt_ref[0, 0, d], 3 * s + t))
        total = list_blocks(lists, listed)
        for c in range(3):
            copies[3 + c].wait()
            for piece in range(2):
                high, low = halves(vel_ref[c, piece * half : (piece + 1) * half, :])
                table[c, :, piece * 128 : (piece + 1) * 128] = high
                table[c, :, 256 + piece * 128 : 256 + (piece + 1) * 128] = low
        for copy in copies[6:]:
            copy.wait()
        gather_lists(table, total, large, small, listed, direction, src_ref, w_ref, out_ref)
        gather_points(mine_ref[0], table, tile_ref, cell_ref, pts_ref, rot_ref, tlist)

    return kernel


def active_turbines(tile_ref, mine, listed):
    turbines = tile_ref.shape[0]
    owned = jnp.where(tile_ref[...] == mine, 1.0, 0.0)
    found = jnp.max(owned, axis=1, keepdims=True)
    total = jnp.int32(0)
    for t in range(turbines):
        listed[total] = t
        total = total + jnp.where(found[t, 0] > 0.5, 1, 0)
    listed[total] = 0
    return total


def gather_points(mine, table, tile_ref, cell_ref, pts_ref, rot_ref, tlist):
    turbines, points = tile_ref.shape
    n_turb = active_turbines(tile_ref, mine, tlist)

    def turbine(i, carry):
        pair = [tlist[2 * i], tlist[2 * i + 1]]
        cell = jnp.concatenate([cell_ref[pl.ds(t, 1), :] for t in pair], axis=1)
        found = pick(table, cell)
        for k, t in enumerate(pair):
            owned = tile_ref[pl.ds(t, 1), :] == mine
            for c in range(3):
                pts_ref[c, pl.ds(t, 1), :] = jnp.where(owned, found[c][:, k * points : (k + 1) * points], 0.0)
        return carry

    lax.fori_loop(0, (n_turb + 1) >> 1, turbine, 0)
    sums = jnp.sum(pts_ref[0], axis=1, keepdims=True)
    rot_ref[0:turbines, :] = jnp.broadcast_to(sums, (turbines, 128))


def used_slots(weight):
    return jnp.sum(jnp.where(weight != 0.0, 1.0, 0.0)).astype(jnp.int32)


def make_near_gather(count_y, large, small):
    def kernel(mine_ref, table, src_ref, w_ref, out_ref, listed, direction):
        out_ref[...] = jnp.zeros_like(out_ref)
        _, side_y = sides(mine_ref, count_y)
        used = [used_slots(w_ref[d * 8 : d * 8 + 8, :]) for d in (3, 4, 5)]
        last = jnp.where(side_y > 0, used[0], used[2])
        lists = [(jnp.where(side_y > 0, used[2], used[0]), 0), (used[1], 1), (last, 2)]
        for t in range(3):
            direction[t] = 3 + side_y * (1 - t) + 1
        total = list_blocks(lists, listed)
        gather_lists(table, total, large, small, listed, direction, src_ref, w_ref, out_ref)

    return kernel


def scatter_lists(val, n_lists, direction, dst_ref, listed, acc, extent, place, large, small):
    lists = []
    for q in range(n_lists):
        lists.append((used_slots(val[q, 3]), q))
    total = list_blocks(lists, listed)
    for k in range(large):
        listed[total + k] = 0

    def chunk(first, width):
        cells, vals = [], [[], [], [], []]
        for k in range(width):
            b = listed[first + k]
            q, j = b >> 3, b & 7
            keep = jnp.where(first + k < total, 1.0, 0.0)
            cells.append(dst_ref[pl.ds(direction[q] * 8 + j, 1), :])
            for c in range(4):
                vals[c].append(val[q, c, pl.ds(j, 1), :] * keep)
        cell = jnp.concatenate(cells, axis=1)
        vals = [jnp.concatenate(v, axis=1) for v in vals]
        acc[...] += spread(extent, place((cell >> 7) & 511), cell & 127, vals)

    run_chunks(total, large, small, chunk)


def make_first_scatter(count_y):
    def kernel(mine_ref, low_ref, own_ref, high_ref, dst_ref, acc, val, listed, direction):
        side_x, _ = sides(mine_ref, count_y)
        for q, ref in enumerate((low_ref, own_ref, high_ref)):
            for c in range(4):
                val[q, c] = ref[32 + c * 8 : 40 + c * 8, :]
            direction[q] = 3 * (side_x * (q - 1) + 1) + 1
        acc[...] = jnp.zeros_like(acc)
        scatter_lists(val, 3, direction, dst_ref, listed, acc, 512, lambda row: row, 12, 4)

    return kernel


def load_later_lists(mine_ref, count_y, first_ref, second_ref, val, direction):
    side_x, side_y = sides(mine_ref, count_y)
    for t, ref in enumerate((first_ref, second_ref)):
        for s in range(3):
            q = 3 * t + s
            for c in range(4):
                at = (s * 4 + c) * 8
                val[q, c] = ref[at : at + 8, :]
            direction[q] = 3 * (side_x * (s - 1) + 1) + side_y * (2 * t - 1) + 1


def corrected(acc, vel, c):
    return (1.0 - acc[:, 384:512]) * vel - acc[:, c * 128 : (c + 1) * 128]


def edge_rows(ref, c, columns):
    at = (lambda r: ref[r, columns]) if c is None else (lambda r: ref[c, r, columns])
    spare = [at(slice(0, 2))]
    low = [at(slice(x * 64, x * 64 + 1)) for x in range(1, 7)]
    high = [at(slice(x * 64 + 63, x * 64 + 64)) for x in range(1, 7)]
    return jnp.concatenate([at(slice(0, 64)), at(slice(448, 512))] + low + spare + high + spare, axis=0)


def edge_place(row):
    x, y = row >> 6, row & 63
    inside = jnp.where(y == 0, 127 + x, jnp.where(y == 63, 135 + x, 1024))
    return jnp.where(x == 0, y, jnp.where(x == 7, 64 + y, inside))


def make_edge_scatter(count_y):
    def kernel(
        mine_ref, base_ref, first_ref, second_ref, dst_ref, vel_ref,
        cor_ref, xa_ref, xb_ref, ya_ref, yb_ref, acc, val, listed, direction,
    ):
        load_later_lists(mine_ref, count_y, first_ref, second_ref, val, direction)
        acc[...] = edge_rows(base_ref, None, slice(None))
        scatter_lists(val, 6, direction, dst_ref, listed, acc, 144, edge_place, 12, 4)
        side_x, side_y = sides(mine_ref, count_y)
        for c in range(3):
            cor = corrected(acc, edge_rows(vel_ref, c, slice(None)), c)
            cor_ref[c] = cor[0:128]
            xa_ref[c] = jnp.where(side_x > 0, cor[64:128], cor[0:64])
            xb_ref[c] = jnp.where(side_x > 0, cor[0:64], cor[64:128])
            low = jnp.concatenate([cor[0:1], cor[128:134], cor[64:65]], axis=0)
            high = jnp.concatenate([cor[63:64], cor[136:142], cor[127:128]], axis=0)
            ya_ref[c] = jnp.where(side_y > 0, high, low)
            yb_ref[c] = jnp.where(side_y > 0, low, high)

    return kernel


def make_inner_scatter(count_y):
    def kernel(mine_ref, base_ref, first_ref, second_ref, dst_ref, vel_ref, cor_ref, acc, val, listed, direction):
        load_later_lists(mine_ref, count_y, first_ref, second_ref, val, direction)
        acc[...] = base_ref[64:448, :]
        scatter_lists(val, 6, direction, dst_ref, listed, acc, 384, lambda row: row - 64, 12, 4)
        for c in range(3):
            cor_ref[c] = corrected(acc, vel_ref[c, 64:448, :], c)

    return kernel


def add_forces(mine, tile_ref, cell_ref, coef_ref, pts_ref, rot_ref, out_ref, tlist):
    out_ref[...] = jnp.zeros_like(out_ref)
    n_turb = active_turbines(tile_ref, mine, tlist)
    points = tile_ref.shape[1]

    def turbine(i, carry):
        pair = [tlist[2 * i], tlist[2 * i + 1]]
        cell = jnp.concatenate([cell_ref[pl.ds(t, 1), :] for t in pair], axis=1)
        force = [[], [], []]
        for k, t in enumerate(pair):
            keep = jnp.where(2 * i + k < n_turb, 1.0 / points, 0.0)
            scale = -coef_ref[pl.ds(t, 1), :] * (rot_ref[pl.ds(t, 1), 0:1] * keep)
            for c in range(3):
                force[c].append(scale * pts_ref[c, pl.ds(t, 1), :])
        force = [jnp.concatenate(f, axis=1) for f in force]
        got = spread(512, (cell >> 7) & 511, cell & 127, force)
        for c in range(3):
            out_ref[c] += got[:, c * 128 : (c + 1) * 128]
        return carry

    lax.fori_loop(0, (n_turb + 1) >> 1, turbine, 0)


def make_stencil(count_y):
    def kernel(
        mine_ref, edge_ref, inner_ref, tile_ref, cell_ref, coef_ref, pts_ref, rot_ref, xa_ref, xb_ref, ya_ref, yb_ref,
        out_hbm, frc_hbm, out_ref, frc_ref, sem, tlist,
    ):
        add_forces(mine_ref[0], tile_ref, cell_ref, coef_ref, pts_ref, rot_ref, frc_ref, tlist)
        given = pltpu.make_async_copy(frc_ref, frc_hbm, sem.at[8])
        given.start()
        side_x, side_y = sides(mine_ref, count_y)
        lane = lax.broadcasted_iota(jnp.int32, (64, 128), 1)

        def slab(c, x):
            if x < 0:
                return jnp.where(side_x > 0, xb_ref[c * 64 : c * 64 + 64, :], xa_ref[c * 64 : c * 64 + 64, :])
            if x > 7:
                return jnp.where(side_x > 0, xa_ref[c * 64 : c * 64 + 64, :], xb_ref[c * 64 : c * 64 + 64, :])
            ref, at = (inner_ref, x - 1) if 1 <= x < 7 else (edge_ref, 0 if x == 0 else 1)
            return ref[c, at * 64 : at * 64 + 64, :]

        copies = []
        for x in range(8):
            now = [slab(c, x) for c in range(3)]
            for c in range(3):
                u = now[c]
                west, east = slab(c, x - 1), slab(c, x + 1)
                ya, yb = ya_ref[c, x : x + 1, :], yb_ref[c, x : x + 1, :]
                south = jnp.concatenate([jnp.where(side_y > 0, yb, ya), u[:-1]], axis=0)
                north = jnp.concatenate([u[1:], jnp.where(side_y > 0, ya, yb)], axis=0)
                upper = jnp.where(lane == 127, 0.0, pltpu.roll(u, 127, 1))
                lower = jnp.where(lane == 0, 0.0, pltpu.roll(u, 1, 1))
                laplace = east + west + north + south + upper + lower - 6.0 * u
                advect = (
                    now[0] * (east - west) * 0.5
                    + now[1] * (north - south) * 0.5
                    + now[2] * (upper - lower) * 0.5
                )
                out_ref[c, x] = u + 0.2 * (0.15 * laplace - advect + frc_ref[c, x * 64 : x * 64 + 64, :])
            copies.append(pltpu.make_async_copy(out_ref.at[:, x], out_hbm.at[:, x], sem.at[x]))
            copies[-1].start()
        for copy in copies:
            copy.wait()
        given.wait()

    return kernel


def swap(value, axis, step):
    count = lax.axis_size(axis)
    return lax.ppermute(value, axis, [(i, i ^ step) for i in range(count)])


def swap_next(value, axis):
    count = lax.axis_size(axis)
    return lax.ppermute(value, axis, [(i, (i - 1 if i % 2 == 0 else i + 1) % count) for i in range(count)])


def call(kernel, name, outs, ins, args, scratch=(), flops=10**9, limit=32):
    return pl.pallas_call(
        kernel,
        out_shape=tuple(jax.ShapeDtypeStruct(shape, dtype) for shape, dtype, _ in outs),
        in_specs=ins,
        out_specs=tuple(spec for _, _, spec in outs),
        scratch_shapes=list(scratch),
        compiler_params=pltpu.CompilerParams(vmem_limit_bytes=limit << 20),
        cost_estimate=pl.CostEstimate(flops=flops, bytes_accessed=10**5, transcendentals=0),
        name=name,
    )(*args)


def body(velocity, counts, src_cell, weights, dst_cell, blade_tile, blade_cell, blade_coef):
    vel = velocity.reshape(3, 512, 128)
    src = src_cell.reshape(72, 128)
    weight = weights.reshape(72, 128)
    dst = dst_cell.reshape(72, 128)
    turbines, points = blade_cell.shape
    count_x, count_y = lax.axis_size("gx"), lax.axis_size("gy")
    mine = (lax.axis_index("gx") * count_y + lax.axis_index("gy")).reshape(1).astype(jnp.int32)
    rows_t = turbines + -turbines % 8
    ints = lambda n: pltpu.SMEM((n,), jnp.int32)

    whole = ((72, 128), jnp.int32, VMEM)
    ints_t = (blade_tile.shape, jnp.int32, VMEM)
    given = (counts, vel, src, weight, dst, blade_tile, blade_cell, blade_coef)
    far, table, vel, src, weight, dst, tile, cell, coef, pts, rotor = call(
        make_far_gather(count_y, 12, 4),
        "far_gather",
        [((6, 4, 8, 128), F32, VMEM), ((3, 256, 512), BF16, VMEM), ((3, 512, 128), F32, VMEM), whole]
        + [((72, 128), F32, VMEM), whole, ints_t, ints_t, (blade_tile.shape, F32, VMEM)]
        + [((3, turbines, points), F32, VMEM), ((rows_t, 128), F32, VMEM)],
        [SMEM] + [HBM] * 8,
        (mine,) + tuple(pltpu.with_memory_space_constraint(v, pltpu.HBM) for v in given),
        [pltpu.SemaphoreType.DMA((10,)), pltpu.SMEM((1, 1, 9), jnp.int32), ints(72), ints(8), ints(32)],
        flops=5 * 10**9,
    )
    low = swap(jnp.concatenate([far[0:3].reshape(96, 128), rotor], axis=0), "gx", 1)
    high = swap_next(far[3:6].reshape(96, 128), "gx")
    (own,) = call(
        make_near_gather(count_y, 8, 4),
        "near_gather",
        [((3, 4, 8, 128), F32, VMEM)],
        [SMEM] + [VMEM] * 3,
        (mine, table, src, weight),
        [ints(48), ints(8)],
        flops=4 * 10**9,
    )
    rotor = rotor + low[96:]
    own = own.reshape(96, 128)

    def y_payload(t):
        return jnp.concatenate([part[t * 32 : t * 32 + 32] for part in (low, own, high)] + [rotor], axis=0)

    first = swap(y_payload(0), "gy", 1)
    rotor = rotor + first[96:]
    second = swap_next(y_payload(2), "gy")
    (acc,) = call(
        make_first_scatter(count_y),
        "first_scatter",
        [((512, 512), F32, VMEM)],
        [SMEM] + [VMEM] * 4,
        (mine, low, own, high, dst),
        [pltpu.VMEM((3, 4, 8, 128), F32), ints(48), ints(8)],
        flops=4 * 10**9,
    )
    rotor = rotor + second[96:]
    for axis, count in (("gx", count_x), ("gy", count_y)):
        step = 4
        while step < count:
            rotor = rotor + swap(rotor, axis, step)
            step *= 2
    lists = pltpu.VMEM((6, 4, 8, 128), F32)
    face_x, face_y = ((3, 64, 128), F32, VMEM), ((3, 8, 128), F32, VMEM)
    edge, xa, xb, ya, yb = call(
        make_edge_scatter(count_y),
        "edge_scatter",
        [((3, 128, 128), F32, VMEM), face_x, face_x, face_y, face_y],
        [SMEM] + [VMEM] * 5,
        (mine, acc, first, second, dst, vel),
        [pltpu.VMEM((144, 512), F32), lists, ints(72), ints(8)],
        flops=4 * 10**9,
    )
    rotor, xa, ya, yb = lax.optimization_barrier((rotor, xa, ya, yb))
    xb = swap_next(jnp.concatenate([xb.reshape(192, 128), rotor], axis=0), "gx")
    xa = swap(xa.reshape(192, 128), "gx", 1)
    ya = swap(ya, "gy", 1)
    yb = swap_next(yb, "gy")
    (inner,) = call(
        make_inner_scatter(count_y),
        "inner_scatter",
        [((3, 384, 128), F32, VMEM)],
        [SMEM] + [VMEM] * 5,
        (mine, acc, first, second, dst, vel),
        [pltpu.VMEM((384, 512), F32), lists, ints(72), ints(8)],
        flops=6 * 10**9,
    )
    rotor = rotor + xb[192:]
    updated, forcing = call(
        make_stencil(count_y),
        "stencil",
        [((3, 8, 64, 128), F32, HBM), ((3, 512, 128), F32, HBM)],
        [SMEM] + [VMEM] * 11,
        (mine, edge, inner, tile, cell, coef, pts, rotor, xa, xb, ya, yb),
        [pltpu.VMEM((3, 8, 64, 128), F32), pltpu.VMEM((3, 512, 128), F32), pltpu.SemaphoreType.DMA((9,)), ints(32)],
    )
    return updated, forcing.reshape(velocity.shape)


def solution(mesh):
    grid = P("gx", "gy", None)
    lists = P("gx", "gy", None, None)
    field = P(None, "gx", "gy", None)
    return jax.shard_map(
        body,
        mesh=mesh,
        in_specs=(field, grid, lists, lists, lists, P(), P(), P()),
        out_specs=(field, field),
        check_vma=False,
    )
```

```python
import jax
import jax.numpy as jnp
from jax import lax
from jax.experimental import pallas as pl
from jax.experimental.pallas import tpu as pltpu
from jax.sharding import PartitionSpec as P

F32 = jnp.float32
BF16 = jnp.bfloat16
VMEM = pl.BlockSpec(memory_space=pltpu.VMEM)
SMEM = pl.BlockSpec(memory_space=pltpu.SMEM)
HBM = pl.BlockSpec(memory_space=pltpu.HBM)


def halves(value):
    high = value.astype(BF16)
    low = (value - high.astype(F32)).astype(BF16)
    return high, low


def one_hot(extent, index):
    rows = lax.broadcasted_iota(jnp.int32, (extent, index.shape[1]), 0)
    return jnp.where(rows == index, 1.0, 0.0).astype(BF16)


def pick(table, cell):
    key = (cell & 127) | (((cell >> 15) & 1) << 7)
    place = (cell >> 7) & 255
    hot = one_hot(256, key)
    hot = jnp.concatenate([hot, hot], axis=0)
    here = lax.broadcasted_iota(jnp.int32, (256, cell.shape[1]), 0) == place
    out = []
    for c in range(3):
        found = jnp.dot(table[c], hot, preferred_element_type=F32)
        out.append(jnp.sum(jnp.where(here, found, 0.0), axis=0, keepdims=True))
    return out


def spread(extent, row, level, values):
    hot = one_hot(extent, row)
    at_level = lax.broadcasted_iota(jnp.int32, (128, level.shape[1]), 0) == level
    high, low = [], []
    for value in values:
        vh = value.astype(BF16).astype(F32)
        high.append(jnp.where(at_level, vh, 0.0).astype(BF16))
        low.append(jnp.where(at_level, value - vh, 0.0).astype(BF16))
    left = jnp.concatenate([hot, hot], axis=1)
    right = jnp.concatenate([jnp.concatenate(high, axis=0), jnp.concatenate(low, axis=0)], axis=1)
    return lax.dot_general(left, right, (((1,), (1,)), ((), ())), preferred_element_type=F32)


def sides(mine_ref, count_y):
    mine = mine_ref[0]
    return 1 - 2 * ((mine // count_y) & 1), 1 - 2 * (mine & 1)


def list_blocks(lists, listed):
    total = jnp.int32(0)
    for used, tag in lists:
        for j in range(8):
            listed[total + j] = tag * 8 + j
        total = total + ((used + 127) >> 7)
    return total


def run_chunks(total, large, small, chunk):
    many = (total + small - 1) // large

    def big(i, carry):
        chunk(i * large, large)
        return carry

    lax.fori_loop(0, many, big, 0)

    def rest(i, carry):
        chunk(many * large + i * small, small)
        return carry

    lax.fori_loop(0, jnp.maximum(total - many * large + small - 1, 0) // small, rest, 0)


def gather_lists(table, total, large, small, listed, direction, src_ref, w_ref, out_ref):
    for k in range(large):
        listed[total + k] = listed[total - 1]

    def chunk(first, width):
        blocks = [listed[first + k] for k in range(width)]
        rows = [direction[b >> 3] * 8 + (b & 7) for b in blocks]
        cell = jnp.concatenate([src_ref[pl.ds(r, 1), :] for r in rows], axis=1)
        found = pick(table, cell)
        for k, (b, r) in enumerate(zip(blocks, rows)):
            j = b & 7
            weight = w_ref[pl.ds(r, 1), :]
            for c in range(3):
                out_ref[b >> 3, c, pl.ds(j, 1), :] = found[c][:, k * 128 : (k + 1) * 128] * weight
            out_ref[b >> 3, 3, pl.ds(j, 1), :] = weight

    run_chunks(total, large, small, chunk)


def make_far_gather(count_y, large, small):
    def kernel(
        mine_ref, cnt_hbm, vel_hbm, src_hbm, w_hbm, dst_hbm, tile_hbm, cell_hbm, coef_hbm,
        out_ref, table, vel_ref, src_ref, w_ref, dst_ref, tile_ref, cell_ref, coef_ref, pts_ref, rot_ref,
        sem, cnt_ref, listed, direction, tlist,
    ):
        half = vel_ref.shape[1] // 2
        pairs = [(cnt_hbm, cnt_ref), (src_hbm, src_ref), (w_hbm, w_ref)]
        pairs += [(vel_hbm.at[c], vel_ref.at[c]) for c in range(3)]
        pairs += [(tile_hbm, tile_ref), (cell_hbm, cell_ref), (coef_hbm, coef_ref), (dst_hbm, dst_ref)]
        copies = [pltpu.make_async_copy(a, b, sem.at[k]) for k, (a, b) in enumerate(pairs)]
        for copy in copies:
            copy.start()
        out_ref[...] = jnp.zeros_like(out_ref)
        pts_ref[...] = jnp.zeros_like(pts_ref)
        rot_ref[...] = jnp.zeros_like(rot_ref)
        for copy in copies[:3]:
            copy.wait()
        slot = lax.broadcasted_iota(jnp.int32, (8, 128), 0) * 128 + lax.broadcasted_iota(jnp.int32, (8, 128), 1)
        for d in range(9):
            part = slice(d * 8, d * 8 + 8)
            w_ref[part, :] = jnp.where(slot < cnt_ref[0, 0, d], w_ref[part, :], 0.0)
        side_x, side_y = sides(mine_ref, count_y)
        lists = []
        for s in range(2):
            for t in range(3):
                d = 3 * (side_x * (1 - 2 * s) + 1) + side_y * (1 - t) + 1
                direction[3 * s + t] = d
                lists.append((cnt_ref[0, 0, d], 3 * s + t))
        total = list_blocks(lists, listed)
        for c in range(3):
            copies[3 + c].wait()
            for piece in range(2):
                high, low = halves(vel_ref[c, piece * half : (piece + 1) * half, :])
                table[c, :, piece * 128 : (piece + 1) * 128] = high
                table[c, :, 256 + piece * 128 : 256 + (piece + 1) * 128] = low
        for copy in copies[6:]:
            copy.wait()
        gather_lists(table, total, large, small, listed, direction, src_ref, w_ref, out_ref)
        gather_points(mine_ref[0], table, tile_ref, cell_ref, pts_ref, rot_ref, tlist)

    return kernel


def active_turbines(tile_ref, mine, listed):
    turbines = tile_ref.shape[0]
    owned = jnp.where(tile_ref[...] == mine, 1.0, 0.0)
    found = jnp.max(owned, axis=1, keepdims=True)
    total = jnp.int32(0)
    for t in range(turbines):
        listed[total] = t
        total = total + jnp.where(found[t, 0] > 0.5, 1, 0)
    listed[total] = 0
    return total


def gather_points(mine, table, tile_ref, cell_ref, pts_ref, rot_ref, tlist):
    turbines, points = tile_ref.shape
    n_turb = active_turbines(tile_ref, mine, tlist)

    def turbine(i, carry):
        pair = [tlist[2 * i], tlist[2 * i + 1]]
        cell = jnp.concatenate([cell_ref[pl.ds(t, 1), :] for t in pair], axis=1)
        found = pick(table, cell)
        for k, t in enumerate(pair):
            owned = tile_ref[pl.ds(t, 1), :] == mine
            for c in range(3):
                pts_ref[c, pl.ds(t, 1), :] = jnp.where(owned, found[c][:, k * points : (k + 1) * points], 0.0)
        return carry

    lax.fori_loop(0, (n_turb + 1) >> 1, turbine, 0)
    sums = jnp.sum(pts_ref[0], axis=1, keepdims=True)
    rot_ref[0:turbines, :] = jnp.broadcast_to(sums, (turbines, 128))


def used_slots(weight):
    return jnp.sum(jnp.where(weight != 0.0, 1.0, 0.0)).astype(jnp.int32)


def make_near_gather(count_y, large, small):
    def kernel(mine_ref, table, src_ref, w_ref, dst_ref, out_ref, acc, listed, direction):
        out_ref[...] = jnp.zeros_like(out_ref)
        acc[...] = jnp.zeros_like(acc)
        _, side_y = sides(mine_ref, count_y)
        used = [used_slots(w_ref[d * 8 : d * 8 + 8, :]) for d in (3, 4, 5)]
        last = jnp.where(side_y > 0, used[0], used[2])
        lists = [(jnp.where(side_y > 0, used[2], used[0]), 0), (used[1], 1), (last, 2)]
        for t in range(3):
            direction[t] = 3 + side_y * (1 - t) + 1
        total = list_blocks(lists, listed)
        gather_lists(table, total, large, small, listed, direction, src_ref, w_ref, out_ref)
        direction[0] = 4
        scatter_lists(out_ref.at[1:2], 1, direction, dst_ref, listed, acc, 512, lambda row: row, 8, 4)

    return kernel


def scatter_lists(val, n_lists, direction, dst_ref, listed, acc, extent, place, large, small):
    lists = []
    for q in range(n_lists):
        lists.append((used_slots(val[q, 3]), q))
    total = list_blocks(lists, listed)
    for k in range(large):
        listed[total + k] = 0

    def chunk(first, width):
        cells, vals = [], [[], [], [], []]
        for k in range(width):
            b = listed[first + k]
            q, j = b >> 3, b & 7
            keep = jnp.where(first + k < total, 1.0, 0.0)
            cells.append(dst_ref[pl.ds(direction[q] * 8 + j, 1), :])
            for c in range(4):
                vals[c].append(val[q, c, pl.ds(j, 1), :] * keep)
        cell = jnp.concatenate(cells, axis=1)
        vals = [jnp.concatenate(v, axis=1) for v in vals]
        acc[...] += spread(extent, place((cell >> 7) & 511), cell & 127, vals)

    run_chunks(total, large, small, chunk)


def make_first_scatter(count_y):
    def kernel(mine_ref, base_ref, low_ref, high_ref, first_ref, dst_ref, acc, edge, val, later, listed, direction):
        side_x, side_y = sides(mine_ref, count_y)
        for q, ref in enumerate((low_ref, high_ref)):
            for c in range(4):
                val[q, c] = ref[32 + c * 8 : 40 + c * 8, :]
            direction[q] = 3 * (side_x * (2 * q - 1) + 1) + 1
        acc[...] = base_ref[...]
        scatter_lists(val, 2, direction, dst_ref, listed, acc, 512, lambda row: row, 12, 4)
        edge[...] = edge_rows(acc, None, slice(None))
        load_later_lists(side_x, -side_y, first_ref, 0, later, direction)
        scatter_lists(later, 3, direction, dst_ref, listed, edge, 144, edge_place, 12, 4)

    return kernel


def load_later_lists(side_x, from_y, ref, start, val, direction):
    for s in range(3):
        for c in range(4):
            at = (s * 4 + c) * 8
            val[start + s, c] = ref[at : at + 8, :]
        direction[start + s] = 3 * (side_x * (s - 1) + 1) + from_y + 1


def corrected(acc, vel, c):
    return (1.0 - acc[:, 384:512]) * vel - acc[:, c * 128 : (c + 1) * 128]


def edge_rows(ref, c, columns):
    at = (lambda r: ref[r, columns]) if c is None else (lambda r: ref[c, r, columns])
    spare = [at(slice(0, 2))]
    low = [at(slice(x * 64, x * 64 + 1)) for x in range(1, 7)]
    high = [at(slice(x * 64 + 63, x * 64 + 64)) for x in range(1, 7)]
    return jnp.concatenate([at(slice(0, 64)), at(slice(448, 512))] + low + spare + high + spare, axis=0)


def edge_place(row):
    x, y = row >> 6, row & 63
    inside = jnp.where(y == 0, 127 + x, jnp.where(y == 63, 135 + x, 1024))
    return jnp.where(x == 0, y, jnp.where(x == 7, 64 + y, inside))


def make_edge_scatter(count_y):
    def kernel(
        mine_ref, base_ref, second_ref, dst_ref, vel_ref,
        cor_ref, xa_ref, xb_ref, ya_ref, yb_ref, acc, val, listed, direction,
    ):
        side_x, side_y = sides(mine_ref, count_y)
        load_later_lists(side_x, side_y, second_ref, 0, val, direction)
        acc[...] = base_ref[...]
        scatter_lists(val, 3, direction, dst_ref, listed, acc, 144, edge_place, 12, 4)
        for c in range(3):
            cor = corrected(acc, edge_rows(vel_ref, c, slice(None)), c)
            cor_ref[c] = cor[0:128]
            xa_ref[c] = jnp.where(side_x > 0, cor[64:128], cor[0:64])
            xb_ref[c] = jnp.where(side_x > 0, cor[0:64], cor[64:128])
            low = jnp.concatenate([cor[0:1], cor[128:134], cor[64:65]], axis=0)
            high = jnp.concatenate([cor[63:64], cor[136:142], cor[127:128]], axis=0)
            ya_ref[c] = jnp.where(side_y > 0, high, low)
            yb_ref[c] = jnp.where(side_y > 0, low, high)

    return kernel


def make_inner_scatter(count_y):
    def kernel(mine_ref, base_ref, first_ref, second_ref, dst_ref, vel_ref, cor_ref, acc, val, listed, direction):
        side_x, side_y = sides(mine_ref, count_y)
        load_later_lists(side_x, -side_y, first_ref, 0, val, direction)
        load_later_lists(side_x, side_y, second_ref, 3, val, direction)
        acc[...] = base_ref[64:448, :]
        scatter_lists(val, 6, direction, dst_ref, listed, acc, 384, lambda row: row - 64, 12, 4)
        for c in range(3):
            cor_ref[c] = corrected(acc, vel_ref[c, 64:448, :], c)

    return kernel


def add_forces(mine, tile_ref, cell_ref, coef_ref, pts_ref, rot_ref, out_ref, tlist):
    out_ref[...] = jnp.zeros_like(out_ref)
    n_turb = active_turbines(tile_ref, mine, tlist)
    points = tile_ref.shape[1]

    def turbine(i, carry):
        pair = [tlist[2 * i], tlist[2 * i + 1]]
        cell = jnp.concatenate([cell_ref[pl.ds(t, 1), :] for t in pair], axis=1)
        force = [[], [], []]
        for k, t in enumerate(pair):
            keep = jnp.where(2 * i + k < n_turb, 1.0 / points, 0.0)
            scale = -coef_ref[pl.ds(t, 1), :] * (rot_ref[pl.ds(t, 1), 0:1] * keep)
            for c in range(3):
                force[c].append(scale * pts_ref[c, pl.ds(t, 1), :])
        force = [jnp.concatenate(f, axis=1) for f in force]
        got = spread(512, (cell >> 7) & 511, cell & 127, force)
        for c in range(3):
            out_ref[c] += got[:, c * 128 : (c + 1) * 128]
        return carry

    lax.fori_loop(0, (n_turb + 1) >> 1, turbine, 0)


def make_stencil(count_y):
    def kernel(
        mine_ref, edge_ref, inner_ref, tile_ref, cell_ref, coef_ref, pts_ref, rot_ref, xa_ref, xb_ref, ya_ref, yb_ref,
        out_hbm, frc_hbm, out_ref, frc_ref, sem, tlist,
    ):
        add_forces(mine_ref[0], tile_ref, cell_ref, coef_ref, pts_ref, rot_ref, frc_ref, tlist)
        given = pltpu.make_async_copy(frc_ref, frc_hbm, sem.at[8])
        given.start()
        side_x, side_y = sides(mine_ref, count_y)
        lane = lax.broadcasted_iota(jnp.int32, (64, 128), 1)

        def slab(c, x):
            if x < 0:
                return jnp.where(side_x > 0, xb_ref[c * 64 : c * 64 + 64, :], xa_ref[c * 64 : c * 64 + 64, :])
            if x > 7:
                return jnp.where(side_x > 0, xa_ref[c * 64 : c * 64 + 64, :], xb_ref[c * 64 : c * 64 + 64, :])
            ref, at = (inner_ref, x - 1) if 1 <= x < 7 else (edge_ref, 0 if x == 0 else 1)
            return ref[c, at * 64 : at * 64 + 64, :]

        copies = []
        for x in range(8):
            now = [slab(c, x) for c in range(3)]
            up = [0.03 - 0.1 * v for v in now]
            down = [0.03 + 0.1 * v for v in now]
            up[2] = jnp.where(lane == 127, 0.0, up[2])
            down[2] = jnp.where(lane == 0, 0.0, down[2])
            for c in range(3):
                u = now[c]
                west, east = slab(c, x - 1), slab(c, x + 1)
                ya, yb = ya_ref[c, x : x + 1, :], yb_ref[c, x : x + 1, :]
                south = jnp.concatenate([jnp.where(side_y > 0, yb, ya), u[:-1]], axis=0)
                north = jnp.concatenate([u[1:], jnp.where(side_y > 0, ya, yb)], axis=0)
                upper, lower = pltpu.roll(u, 127, 1), pltpu.roll(u, 1, 1)
                moved = (up[0] * east + down[0] * west) + (up[1] * north + down[1] * south)
                moved = moved + (up[2] * upper + down[2] * lower)
                out_ref[c, x] = 0.82 * u + (moved + 0.2 * frc_ref[c, x * 64 : x * 64 + 64, :])
            copies.append(pltpu.make_async_copy(out_ref.at[:, x], out_hbm.at[:, x], sem.at[x]))
            copies[-1].start()
        for copy in copies:
            copy.wait()
        given.wait()

    return kernel


def swap(value, axis, step):
    count = lax.axis_size(axis)
    return lax.ppermute(value, axis, [(i, i ^ step) for i in range(count)])


def swap_next(value, axis):
    count = lax.axis_size(axis)
    return lax.ppermute(value, axis, [(i, (i - 1 if i % 2 == 0 else i + 1) % count) for i in range(count)])


def call(kernel, name, outs, ins, args, scratch=(), flops=10**9, limit=32):
    return pl.pallas_call(
        kernel,
        out_shape=tuple(jax.ShapeDtypeStruct(shape, dtype) for shape, dtype, _ in outs),
        in_specs=ins,
        out_specs=tuple(spec for _, _, spec in outs),
        scratch_shapes=list(scratch),
        compiler_params=pltpu.CompilerParams(vmem_limit_bytes=limit << 20),
        cost_estimate=pl.CostEstimate(flops=flops, bytes_accessed=10**5, transcendentals=0),
        name=name,
    )(*args)


def body(velocity, counts, src_cell, weights, dst_cell, blade_tile, blade_cell, blade_coef):
    vel = velocity.reshape(3, 512, 128)
    src = src_cell.reshape(72, 128)
    weight = weights.reshape(72, 128)
    dst = dst_cell.reshape(72, 128)
    turbines, points = blade_cell.shape
    count_x, count_y = lax.axis_size("gx"), lax.axis_size("gy")
    mine = (lax.axis_index("gx") * count_y + lax.axis_index("gy")).reshape(1).astype(jnp.int32)
    rows_t = turbines + -turbines % 8
    ints = lambda n: pltpu.SMEM((n,), jnp.int32)

    whole = ((72, 128), jnp.int32, VMEM)
    ints_t = (blade_tile.shape, jnp.int32, VMEM)
    given = (counts, vel, src, weight, dst, blade_tile, blade_cell, blade_coef)
    far, table, vel, src, weight, dst, tile, cell, coef, pts, rotor = call(
        make_far_gather(count_y, 12, 4),
        "far_gather",
        [((6, 4, 8, 128), F32, VMEM), ((3, 256, 512), BF16, VMEM), ((3, 512, 128), F32, VMEM), whole]
        + [((72, 128), F32, VMEM), whole, ints_t, ints_t, (blade_tile.shape, F32, VMEM)]
        + [((3, turbines, points), F32, VMEM), ((rows_t, 128), F32, VMEM)],
        [SMEM] + [HBM] * 8,
        (mine,) + tuple(pltpu.with_memory_space_constraint(v, pltpu.HBM) for v in given),
        [pltpu.SemaphoreType.DMA((10,)), pltpu.SMEM((1, 1, 9), jnp.int32), ints(72), ints(8), ints(32)],
        flops=5 * 10**9,
    )
    low = swap(jnp.concatenate([far[0:3].reshape(96, 128), rotor], axis=0), "gx", 1)
    high = swap_next(far[3:6].reshape(96, 128), "gx")
    own, acc = call(
        make_near_gather(count_y, 8, 4),
        "near_gather",
        [((3, 4, 8, 128), F32, VMEM), ((512, 512), F32, VMEM)],
        [SMEM] + [VMEM] * 4,
        (mine, table, src, weight, dst),
        [ints(48), ints(8)],
        flops=4 * 10**9,
    )
    rotor = rotor + low[96:]
    own = own.reshape(96, 128)

    def y_payload(t):
        return jnp.concatenate([part[t * 32 : t * 32 + 32] for part in (low, own, high)] + [rotor], axis=0)

    first = swap(y_payload(0), "gy", 1)
    rotor = rotor + first[96:]
    second = swap_next(y_payload(2), "gy")
    three = pltpu.VMEM((3, 4, 8, 128), F32)
    acc, edge = call(
        make_first_scatter(count_y),
        "first_scatter",
        [((512, 512), F32, VMEM), ((144, 512), F32, VMEM)],
        [SMEM] + [VMEM] * 5,
        (mine, acc, low, high, first, dst),
        [pltpu.VMEM((2, 4, 8, 128), F32), three, ints(48), ints(8)],
        flops=4 * 10**9,
    )
    rotor = rotor + second[96:]
    for axis, count in (("gx", count_x), ("gy", count_y)):
        step = 4
        while step < count:
            rotor = rotor + swap(rotor, axis, step)
            step *= 2
    lists = pltpu.VMEM((6, 4, 8, 128), F32)
    face_x, face_y = ((3, 64, 128), F32, VMEM), ((3, 8, 128), F32, VMEM)
    edge, xa, xb, ya, yb = call(
        make_edge_scatter(count_y),
        "edge_scatter",
        [((3, 128, 128), F32, VMEM), face_x, face_x, face_y, face_y],
        [SMEM] + [VMEM] * 4,
        (mine, edge, second, dst, vel),
        [pltpu.VMEM((144, 512), F32), three, ints(48), ints(8)],
        flops=4 * 10**9,
    )
    xb = swap_next(jnp.concatenate([xb.reshape(192, 128), rotor], axis=0), "gx")
    xa = swap(xa.reshape(192, 128), "gx", 1)
    ya = swap(ya, "gy", 1)
    yb = swap_next(yb, "gy")
    (inner,) = call(
        make_inner_scatter(count_y),
        "inner_scatter",
        [((3, 384, 128), F32, VMEM)],
        [SMEM] + [VMEM] * 5,
        (mine, acc, first, second, dst, vel),
        [pltpu.VMEM((384, 512), F32), lists, ints(72), ints(8)],
        flops=6 * 10**9,
    )
    rotor = rotor + xb[192:]
    updated, forcing = call(
        make_stencil(count_y),
        "stencil",
        [((3, 8, 64, 128), F32, HBM), ((3, 512, 128), F32, HBM)],
        [SMEM] + [VMEM] * 11,
        (mine, edge, inner, tile, cell, coef, pts, rotor, xa, xb, ya, yb),
        [pltpu.VMEM((3, 8, 64, 128), F32), pltpu.VMEM((3, 512, 128), F32), pltpu.SemaphoreType.DMA((9,)), ints(32)],
    )
    return updated, forcing.reshape(velocity.shape)


def solution(mesh):
    grid = P("gx", "gy", None)
    lists = P("gx", "gy", None, None)
    field = P(None, "gx", "gy", None)
    return jax.shard_map(
        body,
        mesh=mesh,
        in_specs=(field, grid, lists, lists, lists, P(), P(), P()),
        out_specs=(field, field),
        check_vma=False,
    )
```

```python
import jax
import jax.numpy as jnp
from jax import lax
from jax.experimental import pallas as pl
from jax.experimental.pallas import tpu as pltpu
from jax.sharding import PartitionSpec as P

F32 = jnp.float32
BF16 = jnp.bfloat16
VMEM = pl.BlockSpec(memory_space=pltpu.VMEM)
SMEM = pl.BlockSpec(memory_space=pltpu.SMEM)
HBM = pl.BlockSpec(memory_space=pltpu.HBM)


def halves(value):
    high = value.astype(BF16)
    low = (value - high.astype(F32)).astype(BF16)
    return high, low


def one_hot(extent, index):
    rows = lax.broadcasted_iota(jnp.int32, (extent, index.shape[1]), 0)
    return jnp.where(rows == index, 1.0, 0.0).astype(BF16)


def pick(table, cell):
    key = (cell & 127) | (((cell >> 15) & 1) << 7)
    place = (cell >> 7) & 255
    hot = one_hot(256, key)
    hot = jnp.concatenate([hot, hot], axis=0)
    here = lax.broadcasted_iota(jnp.int32, (256, cell.shape[1]), 0) == place
    out = []
    for c in range(3):
        found = jnp.dot(table[c], hot, preferred_element_type=F32)
        out.append(jnp.sum(jnp.where(here, found, 0.0), axis=0, keepdims=True))
    return out


def spread(extent, row, level, values):
    hot = one_hot(extent, row)
    at_level = lax.broadcasted_iota(jnp.int32, (128, level.shape[1]), 0) == level
    high, low = [], []
    for value in values:
        vh = value.astype(BF16).astype(F32)
        high.append(jnp.where(at_level, vh, 0.0).astype(BF16))
        low.append(jnp.where(at_level, value - vh, 0.0).astype(BF16))
    left = jnp.concatenate([hot, hot], axis=1)
    right = jnp.concatenate([jnp.concatenate(high, axis=0), jnp.concatenate(low, axis=0)], axis=1)
    return lax.dot_general(left, right, (((1,), (1,)), ((), ())), preferred_element_type=F32)


def sides(mine_ref, count_y):
    mine = mine_ref[0]
    return 1 - 2 * ((mine // count_y) & 1), 1 - 2 * (mine & 1)


def list_blocks(lists, listed):
    total = jnp.int32(0)
    for used, tag in lists:
        for j in range(8):
            listed[total + j] = tag * 8 + j
        total = total + ((used + 127) >> 7)
    return total


def run_chunks(total, large, small, chunk):
    many = (total + small - 1) // large

    def big(i, carry):
        chunk(i * large, large)
        return carry

    lax.fori_loop(0, many, big, 0)

    def rest(i, carry):
        chunk(many * large + i * small, small)
        return carry

    lax.fori_loop(0, jnp.maximum(total - many * large + small - 1, 0) // small, rest, 0)


def gather_lists(table, total, large, small, listed, direction, src_ref, w_ref, out_ref):
    for k in range(large):
        listed[total + k] = listed[total - 1]

    def chunk(first, width):
        blocks = [listed[first + k] for k in range(width)]
        rows = [direction[b >> 3] * 8 + (b & 7) for b in blocks]
        cell = jnp.concatenate([src_ref[pl.ds(r, 1), :] for r in rows], axis=1)
        found = pick(table, cell)
        for k, (b, r) in enumerate(zip(blocks, rows)):
            j = b & 7
            weight = w_ref[pl.ds(r, 1), :]
            for c in range(3):
                out_ref[b >> 3, c, pl.ds(j, 1), :] = found[c][:, k * 128 : (k + 1) * 128] * weight
            out_ref[b >> 3, 3, pl.ds(j, 1), :] = weight

    run_chunks(total, large, small, chunk)


def make_far_gather(count_y, large, small):
    def kernel(
        mine_ref, cnt_hbm, vel_hbm, src_hbm, w_hbm, dst_hbm, tile_hbm, cell_hbm, coef_hbm,
        out_ref, table, vel_ref, src_ref, w_ref, dst_ref, tile_ref, cell_ref, coef_ref, pts_ref, rot_ref,
        sem, cnt_ref, listed, direction, tlist,
    ):
        half = vel_ref.shape[1] // 2
        pairs = [(cnt_hbm, cnt_ref), (src_hbm, src_ref), (w_hbm, w_ref)]
        pairs += [(vel_hbm.at[c], vel_ref.at[c]) for c in range(3)]
        pairs += [(tile_hbm, tile_ref), (cell_hbm, cell_ref), (coef_hbm, coef_ref), (dst_hbm, dst_ref)]
        copies = [pltpu.make_async_copy(a, b, sem.at[k]) for k, (a, b) in enumerate(pairs)]
        for copy in copies:
            copy.start()
        out_ref[...] = jnp.zeros_like(out_ref)
        pts_ref[...] = jnp.zeros_like(pts_ref)
        for copy in copies[:3]:
            copy.wait()
        slot = lax.broadcasted_iota(jnp.int32, (8, 128), 0) * 128 + lax.broadcasted_iota(jnp.int32, (8, 128), 1)
        for d in range(9):
            part = slice(d * 8, d * 8 + 8)
            w_ref[part, :] = jnp.where(slot < cnt_ref[0, 0, d], w_ref[part, :], 0.0)
        side_x, side_y = sides(mine_ref, count_y)
        lists = []
        for s in range(2):
            for t in range(3):
                d = 3 * (side_x * (1 - 2 * s) + 1) + side_y * (1 - t) + 1
                direction[3 * s + t] = d
                lists.append((cnt_ref[0, 0, d], 3 * s + t))
        total = list_blocks(lists, listed)
        for c in range(3):
            copies[3 + c].wait()
            for piece in range(2):
                high, low = halves(vel_ref[c, piece * half : (piece + 1) * half, :])
                table[c, :, piece * 128 : (piece + 1) * 128] = high
                table[c, :, 256 + piece * 128 : 256 + (piece + 1) * 128] = low
        for copy in copies[6:]:
            copy.wait()
        gather_lists(table, total, large, small, listed, direction, src_ref, w_ref, out_ref)
        gather_points(mine_ref[0], table, tile_ref, cell_ref, pts_ref, rot_ref, tlist)

    return kernel


def active_turbines(tile_ref, mine, listed):
    turbines = tile_ref.shape[0]
    owned = jnp.where(tile_ref[...] == mine, 1.0, 0.0)
    found = jnp.max(owned, axis=1, keepdims=True)
    total = jnp.int32(0)
    for t in range(turbines):
        listed[total] = t
        total = total + jnp.where(found[t, 0] > 0.5, 1, 0)
    listed[total] = 0
    return total


def diagonal(turbines):
    shape = (turbines, 128)
    return lax.broadcasted_iota(jnp.int32, shape, 0) == lax.broadcasted_iota(jnp.int32, shape, 1)


def gather_points(mine, table, tile_ref, cell_ref, pts_ref, rot_ref, tlist):
    turbines, points = tile_ref.shape
    n_turb = active_turbines(tile_ref, mine, tlist)

    def turbine(i, carry):
        pair = [tlist[2 * i], tlist[2 * i + 1]]
        cell = jnp.concatenate([cell_ref[pl.ds(t, 1), :] for t in pair], axis=1)
        found = pick(table, cell)
        for k, t in enumerate(pair):
            owned = tile_ref[pl.ds(t, 1), :] == mine
            for c in range(3):
                pts_ref[c, pl.ds(t, 1), :] = jnp.where(owned, found[c][:, k * points : (k + 1) * points], 0.0)
        return carry

    lax.fori_loop(0, (n_turb + 1) >> 1, turbine, 0)
    sums = jnp.broadcast_to(jnp.sum(pts_ref[0], axis=1, keepdims=True), (turbines, 128))
    row = jnp.sum(jnp.where(diagonal(turbines), sums, 0.0), axis=0, keepdims=True)
    rot_ref[...] = jnp.broadcast_to(row, rot_ref.shape)


def used_slots(weight):
    return jnp.sum(jnp.where(weight != 0.0, 1.0, 0.0)).astype(jnp.int32)


def make_near_gather(count_y, large, small):
    def kernel(mine_ref, table, src_ref, w_ref, dst_ref, out_ref, acc, listed, direction):
        out_ref[...] = jnp.zeros_like(out_ref)
        acc[...] = jnp.zeros_like(acc)
        _, side_y = sides(mine_ref, count_y)
        used = [used_slots(w_ref[d * 8 : d * 8 + 8, :]) for d in (3, 4, 5)]
        last = jnp.where(side_y > 0, used[0], used[2])
        lists = [(jnp.where(side_y > 0, used[2], used[0]), 0), (used[1], 1), (last, 2)]
        for t in range(3):
            direction[t] = 3 + side_y * (1 - t) + 1
        total = list_blocks(lists, listed)
        gather_lists(table, total, large, small, listed, direction, src_ref, w_ref, out_ref)
        direction[0] = 4
        scatter_lists(out_ref.at[1:2], 1, direction, dst_ref, listed, acc, 512, lambda row: row, 8, 4)

    return kernel


def scatter_lists(val, n_lists, direction, dst_ref, listed, acc, extent, place, large, small):
    lists = []
    for q in range(n_lists):
        lists.append((used_slots(val[q, 3]), q))
    total = list_blocks(lists, listed)
    for k in range(large):
        listed[total + k] = 0

    def chunk(first, width):
        cells, vals = [], [[], [], [], []]
        for k in range(width):
            b = listed[first + k]
            q, j = b >> 3, b & 7
            keep = jnp.where(first + k < total, 1.0, 0.0)
            cells.append(dst_ref[pl.ds(direction[q] * 8 + j, 1), :])
            for c in range(4):
                vals[c].append(val[q, c, pl.ds(j, 1), :] * keep)
        cell = jnp.concatenate(cells, axis=1)
        vals = [jnp.concatenate(v, axis=1) for v in vals]
        acc[...] += spread(extent, place((cell >> 7) & 511), cell & 127, vals)

    run_chunks(total, large, small, chunk)


def load_level_lists(side_x, low_ref, high_ref, start, val, direction):
    for q, ref in enumerate((low_ref, high_ref)):
        for c in range(4):
            val[start + q, c] = ref[32 + c * 8 : 40 + c * 8, :]
        direction[start + q] = 3 * (side_x * (2 * q - 1) + 1) + 1


def make_first_scatter(count_y):
    def kernel(mine_ref, base_ref, low_ref, high_ref, first_ref, dst_ref, edge, val, listed, direction):
        side_x, side_y = sides(mine_ref, count_y)
        load_level_lists(side_x, low_ref, high_ref, 0, val, direction)
        load_later_lists(side_x, -side_y, first_ref, 2, val, direction)
        edge[...] = edge_rows(base_ref, None, slice(None))
        scatter_lists(val, 5, direction, dst_ref, listed, edge, 144, edge_place, 12, 4)

    return kernel


def load_later_lists(side_x, from_y, ref, start, val, direction):
    for s in range(3):
        for c in range(4):
            at = (s * 4 + c) * 8
            val[start + s, c] = ref[at : at + 8, :]
        direction[start + s] = 3 * (side_x * (s - 1) + 1) + from_y + 1


def corrected(acc, vel, c):
    return (1.0 - acc[:, 384:512]) * vel - acc[:, c * 128 : (c + 1) * 128]


def edge_rows(ref, c, columns):
    at = (lambda r: ref[r, columns]) if c is None else (lambda r: ref[c, r, columns])
    spare = [at(slice(0, 2))]
    low = [at(slice(x * 64, x * 64 + 1)) for x in range(1, 7)]
    high = [at(slice(x * 64 + 63, x * 64 + 64)) for x in range(1, 7)]
    return jnp.concatenate([at(slice(0, 64)), at(slice(448, 512))] + low + spare + high + spare, axis=0)


def edge_place(row):
    x, y = row >> 6, row & 63
    inside = jnp.where(y == 0, 127 + x, jnp.where(y == 63, 135 + x, 1024))
    return jnp.where(x == 0, y, jnp.where(x == 7, 64 + y, inside))


def make_edge_scatter(count_y):
    def kernel(
        mine_ref, base_ref, second_ref, dst_ref, vel_ref,
        cor_ref, xa_ref, xb_ref, ya_ref, yb_ref, acc, val, listed, direction,
    ):
        side_x, side_y = sides(mine_ref, count_y)
        load_later_lists(side_x, side_y, second_ref, 0, val, direction)
        acc[...] = base_ref[...]
        scatter_lists(val, 3, direction, dst_ref, listed, acc, 144, edge_place, 12, 4)
        for c in range(3):
            cor = corrected(acc, edge_rows(vel_ref, c, slice(None)), c)
            cor_ref[c] = cor[0:128]
            xa_ref[c] = jnp.where(side_x > 0, cor[64:128], cor[0:64])
            xb_ref[c] = jnp.where(side_x > 0, cor[0:64], cor[64:128])
            low = jnp.concatenate([cor[0:1], cor[128:134], cor[64:65]], axis=0)
            high = jnp.concatenate([cor[63:64], cor[136:142], cor[127:128]], axis=0)
            ya_ref[c] = jnp.where(side_y > 0, high, low)
            yb_ref[c] = jnp.where(side_y > 0, low, high)

    return kernel


def make_inner_scatter(count_y):
    def kernel(mine_ref, base_ref, low_ref, high_ref, first_ref, second_ref, dst_ref, vel_ref, cor_ref, acc, val, listed, direction):
        side_x, side_y = sides(mine_ref, count_y)
        load_later_lists(side_x, -side_y, first_ref, 0, val, direction)
        load_later_lists(side_x, side_y, second_ref, 3, val, direction)
        load_level_lists(side_x, low_ref, high_ref, 6, val, direction)
        acc[...] = base_ref[64:448, :]
        scatter_lists(val, 8, direction, dst_ref, listed, acc, 384, lambda row: row - 64, 12, 4)
        for c in range(3):
            cor_ref[c] = corrected(acc, vel_ref[c, 64:448, :], c)

    return kernel


def add_forces(mine, tile_ref, cell_ref, coef_ref, pts_ref, rot_ref, column, out_ref, tlist):
    out_ref[...] = jnp.zeros_like(out_ref)
    turbines = tile_ref.shape[0]
    sums = jnp.broadcast_to(rot_ref[0:1, :], (turbines, 128))
    sums = jnp.sum(jnp.where(diagonal(turbines), sums, 0.0), axis=1, keepdims=True)
    column[...] = jnp.broadcast_to(sums, (turbines, 128))
    n_turb = active_turbines(tile_ref, mine, tlist)
    points = tile_ref.shape[1]

    def turbine(i, carry):
        pair = [tlist[2 * i], tlist[2 * i + 1]]
        cell = jnp.concatenate([cell_ref[pl.ds(t, 1), :] for t in pair], axis=1)
        force = [[], [], []]
        for k, t in enumerate(pair):
            keep = jnp.where(2 * i + k < n_turb, 1.0 / points, 0.0)
            scale = -coef_ref[pl.ds(t, 1), :] * (column[pl.ds(t, 1), 0:1] * keep)
            for c in range(3):
                force[c].append(scale * pts_ref[c, pl.ds(t, 1), :])
        force = [jnp.concatenate(f, axis=1) for f in force]
        got = spread(512, (cell >> 7) & 511, cell & 127, force)
        for c in range(3):
            out_ref[c] += got[:, c * 128 : (c + 1) * 128]
        return carry

    lax.fori_loop(0, (n_turb + 1) >> 1, turbine, 0)


def make_stencil(count_y):
    def kernel(
        mine_ref, edge_ref, inner_ref, tile_ref, cell_ref, coef_ref, pts_ref, rot_ref, xa_ref, xb_ref, ya_ref, yb_ref,
        out_hbm, frc_hbm, out_ref, frc_ref, column, sem, tlist,
    ):
        add_forces(mine_ref[0], tile_ref, cell_ref, coef_ref, pts_ref, rot_ref, column, frc_ref, tlist)
        given = pltpu.make_async_copy(frc_ref, frc_hbm, sem.at[8])
        given.start()
        side_x, side_y = sides(mine_ref, count_y)
        lane = lax.broadcasted_iota(jnp.int32, (64, 128), 1)

        def slab(c, x):
            if x < 0:
                return jnp.where(side_x > 0, xb_ref[c * 64 : c * 64 + 64, :], xa_ref[c * 64 : c * 64 + 64, :])
            if x > 7:
                return jnp.where(side_x > 0, xa_ref[c * 64 : c * 64 + 64, :], xb_ref[c * 64 : c * 64 + 64, :])
            ref, at = (inner_ref, x - 1) if 1 <= x < 7 else (edge_ref, 0 if x == 0 else 1)
            return ref[c, at * 64 : at * 64 + 64, :]

        copies = []
        for x in range(8):
            now = [slab(c, x) for c in range(3)]
            up = [0.03 - 0.1 * v for v in now]
            down = [0.03 + 0.1 * v for v in now]
            up[2] = jnp.where(lane == 127, 0.0, up[2])
            down[2] = jnp.where(lane == 0, 0.0, down[2])
            for c in range(3):
                u = now[c]
                west, east = slab(c, x - 1), slab(c, x + 1)
                ya, yb = ya_ref[c, x : x + 1, :], yb_ref[c, x : x + 1, :]
                south = jnp.concatenate([jnp.where(side_y > 0, yb, ya), u[:-1]], axis=0)
                north = jnp.concatenate([u[1:], jnp.where(side_y > 0, ya, yb)], axis=0)
                upper, lower = pltpu.roll(u, 127, 1), pltpu.roll(u, 1, 1)
                moved = (up[0] * east + down[0] * west) + (up[1] * north + down[1] * south)
                moved = moved + (up[2] * upper + down[2] * lower)
                out_ref[c, x] = 0.82 * u + (moved + 0.2 * frc_ref[c, x * 64 : x * 64 + 64, :])
            copies.append(pltpu.make_async_copy(out_ref.at[:, x], out_hbm.at[:, x], sem.at[x]))
            copies[-1].start()
        for copy in copies:
            copy.wait()
        given.wait()

    return kernel


def swap(value, axis, step):
    count = lax.axis_size(axis)
    return lax.ppermute(value, axis, [(i, i ^ step) for i in range(count)])


def swap_next(value, axis):
    count = lax.axis_size(axis)
    return lax.ppermute(value, axis, [(i, (i - 1 if i % 2 == 0 else i + 1) % count) for i in range(count)])


def call(kernel, name, outs, ins, args, scratch=(), flops=10**9, limit=32):
    return pl.pallas_call(
        kernel,
        out_shape=tuple(jax.ShapeDtypeStruct(shape, dtype) for shape, dtype, _ in outs),
        in_specs=ins,
        out_specs=tuple(spec for _, _, spec in outs),
        scratch_shapes=list(scratch),
        compiler_params=pltpu.CompilerParams(vmem_limit_bytes=limit << 20),
        cost_estimate=pl.CostEstimate(flops=flops, bytes_accessed=10**5, transcendentals=0),
        name=name,
    )(*args)


def body(velocity, counts, src_cell, weights, dst_cell, blade_tile, blade_cell, blade_coef):
    vel = velocity.reshape(3, 512, 128)
    src = src_cell.reshape(72, 128)
    weight = weights.reshape(72, 128)
    dst = dst_cell.reshape(72, 128)
    turbines, points = blade_cell.shape
    count_x, count_y = lax.axis_size("gx"), lax.axis_size("gy")
    mine = (lax.axis_index("gx") * count_y + lax.axis_index("gy")).reshape(1).astype(jnp.int32)
    ints = lambda n: pltpu.SMEM((n,), jnp.int32)

    whole = ((72, 128), jnp.int32, VMEM)
    ints_t = (blade_tile.shape, jnp.int32, VMEM)
    given = (counts, vel, src, weight, dst, blade_tile, blade_cell, blade_coef)
    far, table, vel, src, weight, dst, tile, cell, coef, pts, rotor = call(
        make_far_gather(count_y, 12, 4),
        "far_gather",
        [((6, 4, 8, 128), F32, VMEM), ((3, 256, 512), BF16, VMEM), ((3, 512, 128), F32, VMEM), whole]
        + [((72, 128), F32, VMEM), whole, ints_t, ints_t, (blade_tile.shape, F32, VMEM)]
        + [((3, turbines, points), F32, VMEM), ((8, 128), F32, VMEM)],
        [SMEM] + [HBM] * 8,
        (mine,) + tuple(pltpu.with_memory_space_constraint(v, pltpu.HBM) for v in given),
        [pltpu.SemaphoreType.DMA((10,)), pltpu.SMEM((1, 1, 9), jnp.int32), ints(72), ints(8), ints(32)],
        flops=5 * 10**9,
    )
    low = swap(jnp.concatenate([far[0:3].reshape(96, 128), rotor], axis=0), "gx", 1)
    high = swap_next(far[3:6].reshape(96, 128), "gx")
    own, acc = call(
        make_near_gather(count_y, 8, 4),
        "near_gather",
        [((3, 4, 8, 128), F32, VMEM), ((512, 512), F32, VMEM)],
        [SMEM] + [VMEM] * 4,
        (mine, table, src, weight, dst),
        [ints(48), ints(8)],
        flops=4 * 10**9,
    )
    rotor = rotor + low[96:]
    own = own.reshape(96, 128)

    def y_payload(t):
        return jnp.concatenate([part[t * 32 : t * 32 + 32] for part in (low, own, high)] + [rotor], axis=0)

    first = swap(y_payload(0), "gy", 1)
    rotor = rotor + first[96:]
    second = swap_next(y_payload(2), "gy")
    (edge,) = call(
        make_first_scatter(count_y),
        "first_scatter",
        [((144, 512), F32, VMEM)],
        [SMEM] + [VMEM] * 5,
        (mine, acc, low, high, first, dst),
        [pltpu.VMEM((5, 4, 8, 128), F32), ints(72), ints(8)],
        flops=4 * 10**9,
    )
    rotor = rotor + second[96:]
    for axis, count in (("gx", count_x), ("gy", count_y)):
        step = 4
        while step < count:
            rotor = rotor + swap(rotor, axis, step)
            step *= 2
    lists = pltpu.VMEM((8, 4, 8, 128), F32)
    face_x, face_y = ((3, 64, 128), F32, VMEM), ((3, 8, 128), F32, VMEM)
    edge, xa, xb, ya, yb = call(
        make_edge_scatter(count_y),
        "edge_scatter",
        [((3, 128, 128), F32, VMEM), face_x, face_x, face_y, face_y],
        [SMEM] + [VMEM] * 4,
        (mine, edge, second, dst, vel),
        [pltpu.VMEM((144, 512), F32), pltpu.VMEM((3, 4, 8, 128), F32), ints(48), ints(8)],
        flops=4 * 10**9,
    )
    xb = swap_next(jnp.concatenate([xb.reshape(192, 128), rotor], axis=0), "gx")
    xa = swap(xa.reshape(192, 128), "gx", 1)
    ya = swap(ya, "gy", 1)
    yb = swap_next(yb, "gy")
    (inner,) = call(
        make_inner_scatter(count_y),
        "inner_scatter",
        [((3, 384, 128), F32, VMEM)],
        [SMEM] + [VMEM] * 7,
        (mine, acc, low, high, first, second, dst, vel),
        [pltpu.VMEM((384, 512), F32), lists, ints(96), ints(8)],
        flops=6 * 10**9,
    )
    rotor = rotor + xb[192:]
    updated, forcing = call(
        make_stencil(count_y),
        "stencil",
        [((3, 8, 64, 128), F32, HBM), ((3, 512, 128), F32, HBM)],
        [SMEM] + [VMEM] * 11,
        (mine, edge, inner, tile, cell, coef, pts, rotor, xa, xb, ya, yb),
        [pltpu.VMEM((3, 8, 64, 128), F32), pltpu.VMEM((3, 512, 128), F32), pltpu.VMEM((turbines, 128), F32)]
        + [pltpu.SemaphoreType.DMA((9,)), ints(32)],
    )
    return updated, forcing.reshape(velocity.shape)


def solution(mesh):
    grid = P("gx", "gy", None)
    lists = P("gx", "gy", None, None)
    field = P(None, "gx", "gy", None)
    return jax.shard_map(
        body,
        mesh=mesh,
        in_specs=(field, grid, lists, lists, lists, P(), P(), P()),
        out_specs=(field, field),
        check_vma=False,
    )
```

```python
import jax
import jax.numpy as jnp
from jax import lax
from jax.experimental import pallas as pl
from jax.experimental.pallas import tpu as pltpu
from jax.sharding import PartitionSpec as P

F32 = jnp.float32
BF16 = jnp.bfloat16
VMEM = pl.BlockSpec(memory_space=pltpu.VMEM)
SMEM = pl.BlockSpec(memory_space=pltpu.SMEM)
HBM = pl.BlockSpec(memory_space=pltpu.HBM)


def halves(value):
    high = value.astype(BF16)
    low = (value - high.astype(F32)).astype(BF16)
    return high, low


def one_hot(extent, index):
    rows = lax.broadcasted_iota(jnp.int32, (extent, index.shape[1]), 0)
    return jnp.where(rows == index, 1.0, 0.0).astype(BF16)


def pick(table, cell):
    key = (cell & 127) | (((cell >> 15) & 1) << 7)
    place = (cell >> 7) & 255
    hot = one_hot(256, key)
    hot = jnp.concatenate([hot, hot], axis=0)
    here = lax.broadcasted_iota(jnp.int32, (256, cell.shape[1]), 0) == place
    out = []
    for c in range(3):
        found = jnp.dot(table[c], hot, preferred_element_type=F32)
        out.append(jnp.sum(jnp.where(here, found, 0.0), axis=0, keepdims=True))
    return out


def spread(extent, row, level, values):
    hot = one_hot(extent, row)
    at_level = lax.broadcasted_iota(jnp.int32, (128, level.shape[1]), 0) == level
    high, low = [], []
    for value in values:
        vh = value.astype(BF16).astype(F32)
        high.append(jnp.where(at_level, vh, 0.0).astype(BF16))
        low.append(jnp.where(at_level, value - vh, 0.0).astype(BF16))
    left = jnp.concatenate([hot, hot], axis=1)
    right = jnp.concatenate([jnp.concatenate(high, axis=0), jnp.concatenate(low, axis=0)], axis=1)
    return lax.dot_general(left, right, (((1,), (1,)), ((), ())), preferred_element_type=F32)


def sides(mine_ref, count_y):
    mine = mine_ref[0]
    return 1 - 2 * ((mine // count_y) & 1), 1 - 2 * (mine & 1)


def list_blocks(lists, listed):
    total = jnp.int32(0)
    for used, tag in lists:
        for j in range(8):
            listed[total + j] = tag * 8 + j
        total = total + ((used + 127) >> 7)
    return total


def run_chunks(total, large, small, chunk):
    many = (total + small - 1) // large

    def big(i, carry):
        chunk(i * large, large)
        return carry

    lax.fori_loop(0, many, big, 0)

    def rest(i, carry):
        chunk(many * large + i * small, small)
        return carry

    lax.fori_loop(0, jnp.maximum(total - many * large + small - 1, 0) // small, rest, 0)


def gather_lists(table, total, large, small, listed, direction, src_ref, w_ref, out_ref):
    for k in range(large):
        listed[total + k] = listed[total - 1]

    def chunk(first, width):
        blocks = [listed[first + k] for k in range(width)]
        rows = [direction[b >> 3] * 8 + (b & 7) for b in blocks]
        cell = jnp.concatenate([src_ref[pl.ds(r, 1), :] for r in rows], axis=1)
        found = pick(table, cell)
        for k, (b, r) in enumerate(zip(blocks, rows)):
            j = b & 7
            weight = w_ref[pl.ds(r, 1), :]
            for c in range(3):
                out_ref[b >> 3, c, pl.ds(j, 1), :] = found[c][:, k * 128 : (k + 1) * 128] * weight
            out_ref[b >> 3, 3, pl.ds(j, 1), :] = weight

    run_chunks(total, large, small, chunk)


def make_far_gather(count_y, large, small):
    def kernel(
        mine_ref, cnt_hbm, vel_hbm, src_hbm, w_hbm, dst_hbm, tile_hbm, cell_hbm, coef_hbm,
        out_ref, table, vel_ref, src_ref, w_ref, dst_ref, tile_ref, cell_ref, coef_ref, pts_ref, rot_ref,
        sem, cnt_ref, listed, direction, tlist,
    ):
        half = vel_ref.shape[1] // 2
        pairs = [(cnt_hbm, cnt_ref), (src_hbm, src_ref), (w_hbm, w_ref), (tile_hbm, tile_ref)]
        pairs += [(vel_hbm.at[c], vel_ref.at[c]) for c in range(3)]
        pairs += [(cell_hbm, cell_ref), (coef_hbm, coef_ref), (dst_hbm, dst_ref)]
        copies = [pltpu.make_async_copy(a, b, sem.at[k]) for k, (a, b) in enumerate(pairs)]
        for copy in copies:
            copy.start()
        out_ref[...] = jnp.zeros_like(out_ref)
        pts_ref[...] = jnp.zeros_like(pts_ref)
        for copy in copies[:4]:
            copy.wait()
        n_turb = active_turbines(tile_ref, mine_ref[0], tlist)
        slot = lax.broadcasted_iota(jnp.int32, (8, 128), 0) * 128 + lax.broadcasted_iota(jnp.int32, (8, 128), 1)
        for d in range(9):
            part = slice(d * 8, d * 8 + 8)
            w_ref[part, :] = jnp.where(slot < cnt_ref[0, 0, d], w_ref[part, :], 0.0)
        side_x, side_y = sides(mine_ref, count_y)
        lists = []
        for s in range(2):
            for t in range(3):
                d = 3 * (side_x * (1 - 2 * s) + 1) + side_y * (1 - t) + 1
                direction[3 * s + t] = d
                lists.append((cnt_ref[0, 0, d], 3 * s + t))
        total = list_blocks(lists, listed)
        for c in range(3):
            copies[4 + c].wait()
            for piece in range(2):
                high, low = halves(vel_ref[c, piece * half : (piece + 1) * half, :])
                table[c, :, piece * 128 : (piece + 1) * 128] = high
                table[c, :, 256 + piece * 128 : 256 + (piece + 1) * 128] = low
        for copy in copies[7:]:
            copy.wait()
        gather_lists(table, total, large, small, listed, direction, src_ref, w_ref, out_ref)
        gather_points(mine_ref[0], n_turb, table, tile_ref, cell_ref, pts_ref, rot_ref, tlist)

    return kernel


def active_turbines(tile_ref, mine, listed):
    turbines = tile_ref.shape[0]
    owned = jnp.where(tile_ref[...] == mine, 1.0, 0.0)
    found = jnp.max(owned, axis=1, keepdims=True)
    total = jnp.int32(0)
    for t in range(turbines):
        listed[total] = t
        total = total + jnp.where(found[t, 0] > 0.5, 1, 0)
    listed[total] = 0
    return total


def diagonal(turbines):
    shape = (turbines, 128)
    return lax.broadcasted_iota(jnp.int32, shape, 0) == lax.broadcasted_iota(jnp.int32, shape, 1)


def gather_points(mine, n_turb, table, tile_ref, cell_ref, pts_ref, rot_ref, tlist):
    turbines, points = tile_ref.shape

    def turbine(i, carry):
        pair = [tlist[2 * i], tlist[2 * i + 1]]
        cell = jnp.concatenate([cell_ref[pl.ds(t, 1), :] for t in pair], axis=1)
        found = pick(table, cell)
        for k, t in enumerate(pair):
            owned = tile_ref[pl.ds(t, 1), :] == mine
            for c in range(3):
                pts_ref[c, pl.ds(t, 1), :] = jnp.where(owned, found[c][:, k * points : (k + 1) * points], 0.0)
        return carry

    lax.fori_loop(0, (n_turb + 1) >> 1, turbine, 0)
    sums = jnp.broadcast_to(jnp.sum(pts_ref[0], axis=1, keepdims=True), (turbines, 128))
    row = jnp.sum(jnp.where(diagonal(turbines), sums, 0.0), axis=0, keepdims=True)
    rot_ref[...] = jnp.broadcast_to(row, rot_ref.shape)


def used_slots(weight):
    return jnp.sum(jnp.where(weight != 0.0, 1.0, 0.0)).astype(jnp.int32)


def make_near_gather(count_y, large, small):
    def kernel(mine_ref, table, src_ref, w_ref, dst_ref, out_ref, acc, listed, direction):
        out_ref[...] = jnp.zeros_like(out_ref)
        acc[...] = jnp.zeros_like(acc)
        _, side_y = sides(mine_ref, count_y)
        used = [used_slots(w_ref[d * 8 : d * 8 + 8, :]) for d in (3, 4, 5)]
        last = jnp.where(side_y > 0, used[0], used[2])
        lists = [(jnp.where(side_y > 0, used[2], used[0]), 0), (used[1], 1), (last, 2)]
        for t in range(3):
            direction[t] = 3 + side_y * (1 - t) + 1
        total = list_blocks(lists, listed)
        gather_lists(table, total, large, small, listed, direction, src_ref, w_ref, out_ref)
        direction[0] = 4
        scatter_lists(out_ref.at[1:2], 1, direction, dst_ref, listed, acc, 512, lambda row: row, 8, 4)

    return kernel


def scatter_lists(val, n_lists, direction, dst_ref, listed, acc, extent, place, large, small):
    lists = []
    for q in range(n_lists):
        lists.append((used_slots(val[q, 3]), q))
    total = list_blocks(lists, listed)
    for k in range(large):
        listed[total + k] = 0

    def chunk(first, width):
        cells, vals = [], [[], [], [], []]
        for k in range(width):
            b = listed[first + k]
            q, j = b >> 3, b & 7
            keep = jnp.where(first + k < total, 1.0, 0.0)
            cells.append(dst_ref[pl.ds(direction[q] * 8 + j, 1), :])
            for c in range(4):
                vals[c].append(val[q, c, pl.ds(j, 1), :] * keep)
        cell = jnp.concatenate(cells, axis=1)
        vals = [jnp.concatenate(v, axis=1) for v in vals]
        acc[...] += spread(extent, place((cell >> 7) & 511), cell & 127, vals)

    run_chunks(total, large, small, chunk)


def load_level_lists(side_x, low_ref, high_ref, start, val, direction):
    for q, ref in enumerate((low_ref, high_ref)):
        for c in range(4):
            val[start + q, c] = ref[32 + c * 8 : 40 + c * 8, :]
        direction[start + q] = 3 * (side_x * (2 * q - 1) + 1) + 1


def make_level_edges(count_y):
    def kernel(mine_ref, base_ref, low_ref, high_ref, dst_ref, edge, val, listed, direction):
        side_x, _ = sides(mine_ref, count_y)
        load_level_lists(side_x, low_ref, high_ref, 0, val, direction)
        edge[...] = edge_rows(base_ref, None, slice(None))
        scatter_lists(val, 2, direction, dst_ref, listed, edge, 144, edge_place, 12, 4)

    return kernel


def make_core_edges(count_y):
    def kernel(mine_ref, base_ref, first_ref, dst_ref, edge, val, listed, direction):
        side_x, side_y = sides(mine_ref, count_y)
        load_later_lists(side_x, -side_y, first_ref, 0, val, direction)
        edge[...] = base_ref[...]
        scatter_lists(val, 3, direction, dst_ref, listed, edge, 144, edge_place, 12, 4)

    return kernel


def load_later_lists(side_x, from_y, ref, start, val, direction):
    for s in range(3):
        for c in range(4):
            at = (s * 4 + c) * 8
            val[start + s, c] = ref[at : at + 8, :]
        direction[start + s] = 3 * (side_x * (s - 1) + 1) + from_y + 1


def corrected(acc, vel, c):
    return (1.0 - acc[:, 384:512]) * vel - acc[:, c * 128 : (c + 1) * 128]


def edge_rows(ref, c, columns):
    at = (lambda r: ref[r, columns]) if c is None else (lambda r: ref[c, r, columns])
    spare = [at(slice(0, 2))]
    low = [at(slice(x * 64, x * 64 + 1)) for x in range(1, 7)]
    high = [at(slice(x * 64 + 63, x * 64 + 64)) for x in range(1, 7)]
    return jnp.concatenate([at(slice(0, 64)), at(slice(448, 512))] + low + spare + high + spare, axis=0)


def edge_place(row):
    x, y = row >> 6, row & 63
    inside = jnp.where(y == 0, 127 + x, jnp.where(y == 63, 135 + x, 1024))
    return jnp.where(x == 0, y, jnp.where(x == 7, 64 + y, inside))


def make_edge_scatter(count_y):
    def kernel(
        mine_ref, base_ref, second_ref, dst_ref, vel_ref,
        cor_ref, xa_ref, xb_ref, ya_ref, yb_ref, acc, val, listed, direction,
    ):
        side_x, side_y = sides(mine_ref, count_y)
        load_later_lists(side_x, side_y, second_ref, 0, val, direction)
        acc[...] = base_ref[...]
        scatter_lists(val, 3, direction, dst_ref, listed, acc, 144, edge_place, 12, 4)
        for c in range(3):
            cor = corrected(acc, edge_rows(vel_ref, c, slice(None)), c)
            cor_ref[c] = cor[0:128]
            xa_ref[c] = jnp.where(side_x > 0, cor[64:128], cor[0:64])
            xb_ref[c] = jnp.where(side_x > 0, cor[0:64], cor[64:128])
            low = jnp.concatenate([cor[0:1], cor[128:134], cor[64:65]], axis=0)
            high = jnp.concatenate([cor[63:64], cor[136:142], cor[127:128]], axis=0)
            ya_ref[c] = jnp.where(side_y > 0, high, low)
            yb_ref[c] = jnp.where(side_y > 0, low, high)

    return kernel


def make_inner_scatter(count_y):
    def kernel(mine_ref, base_ref, low_ref, high_ref, first_ref, second_ref, dst_ref, vel_ref, cor_ref, acc, val, listed, direction):
        side_x, side_y = sides(mine_ref, count_y)
        load_later_lists(side_x, -side_y, first_ref, 0, val, direction)
        load_later_lists(side_x, side_y, second_ref, 3, val, direction)
        load_level_lists(side_x, low_ref, high_ref, 6, val, direction)
        acc[...] = base_ref[64:448, :]
        scatter_lists(val, 8, direction, dst_ref, listed, acc, 384, lambda row: row - 64, 12, 4)
        for c in range(3):
            cor_ref[c] = corrected(acc, vel_ref[c, 64:448, :], c)

    return kernel


def add_forces(mine, tile_ref, cell_ref, coef_ref, pts_ref, rot_ref, column, out_ref, tlist):
    out_ref[...] = jnp.zeros_like(out_ref)
    turbines = tile_ref.shape[0]
    sums = jnp.broadcast_to(rot_ref[0:1, :], (turbines, 128))
    sums = jnp.sum(jnp.where(diagonal(turbines), sums, 0.0), axis=1, keepdims=True)
    column[...] = jnp.broadcast_to(sums, (turbines, 128))
    n_turb = active_turbines(tile_ref, mine, tlist)
    points = tile_ref.shape[1]

    def turbine(i, carry):
        pair = [tlist[2 * i], tlist[2 * i + 1]]
        cell = jnp.concatenate([cell_ref[pl.ds(t, 1), :] for t in pair], axis=1)
        force = [[], [], []]
        for k, t in enumerate(pair):
            keep = jnp.where(2 * i + k < n_turb, 1.0 / points, 0.0)
            scale = -coef_ref[pl.ds(t, 1), :] * (column[pl.ds(t, 1), 0:1] * keep)
            for c in range(3):
                force[c].append(scale * pts_ref[c, pl.ds(t, 1), :])
        force = [jnp.concatenate(f, axis=1) for f in force]
        got = spread(512, (cell >> 7) & 511, cell & 127, force)
        for c in range(3):
            out_ref[c] += got[:, c * 128 : (c + 1) * 128]
        return carry

    lax.fori_loop(0, (n_turb + 1) >> 1, turbine, 0)


def make_stencil(count_y):
    def kernel(
        mine_ref, edge_ref, inner_ref, tile_ref, cell_ref, coef_ref, pts_ref, rot_ref, xa_ref, xb_ref, ya_ref, yb_ref,
        out_hbm, frc_hbm, out_ref, frc_ref, column, sem, tlist,
    ):
        add_forces(mine_ref[0], tile_ref, cell_ref, coef_ref, pts_ref, rot_ref, column, frc_ref, tlist)
        given = pltpu.make_async_copy(frc_ref, frc_hbm, sem.at[8])
        given.start()
        side_x, side_y = sides(mine_ref, count_y)
        lane = lax.broadcasted_iota(jnp.int32, (64, 128), 1)

        def slab(c, x):
            if x < 0:
                return jnp.where(side_x > 0, xb_ref[c * 64 : c * 64 + 64, :], xa_ref[c * 64 : c * 64 + 64, :])
            if x > 7:
                return jnp.where(side_x > 0, xa_ref[c * 64 : c * 64 + 64, :], xb_ref[c * 64 : c * 64 + 64, :])
            ref, at = (inner_ref, x - 1) if 1 <= x < 7 else (edge_ref, 0 if x == 0 else 1)
            return ref[c, at * 64 : at * 64 + 64, :]

        copies = []
        for x in range(8):
            now = [slab(c, x) for c in range(3)]
            up = [0.03 - 0.1 * v for v in now]
            down = [0.03 + 0.1 * v for v in now]
            up[2] = jnp.where(lane == 127, 0.0, up[2])
            down[2] = jnp.where(lane == 0, 0.0, down[2])
            for c in range(3):
                u = now[c]
                west, east = slab(c, x - 1), slab(c, x + 1)
                ya, yb = ya_ref[c, x : x + 1, :], yb_ref[c, x : x + 1, :]
                south = jnp.concatenate([jnp.where(side_y > 0, yb, ya), u[:-1]], axis=0)
                north = jnp.concatenate([u[1:], jnp.where(side_y > 0, ya, yb)], axis=0)
                upper, lower = pltpu.roll(u, 127, 1), pltpu.roll(u, 1, 1)
                moved = (up[0] * east + down[0] * west) + (up[1] * north + down[1] * south)
                moved = moved + (up[2] * upper + down[2] * lower)
                out_ref[c, x] = 0.82 * u + (moved + 0.2 * frc_ref[c, x * 64 : x * 64 + 64, :])
            copies.append(pltpu.make_async_copy(out_ref.at[:, x], out_hbm.at[:, x], sem.at[x]))
            copies[-1].start()
        for copy in copies:
            copy.wait()
        given.wait()

    return kernel


def swap(value, axis, step):
    count = lax.axis_size(axis)
    return lax.ppermute(value, axis, [(i, i ^ step) for i in range(count)])


def swap_next(value, axis):
    count = lax.axis_size(axis)
    return lax.ppermute(value, axis, [(i, (i - 1 if i % 2 == 0 else i + 1) % count) for i in range(count)])


def call(kernel, name, outs, ins, args, scratch=(), flops=10**9, limit=32):
    return pl.pallas_call(
        kernel,
        out_shape=tuple(jax.ShapeDtypeStruct(shape, dtype) for shape, dtype, _ in outs),
        in_specs=ins,
        out_specs=tuple(spec for _, _, spec in outs),
        scratch_shapes=list(scratch),
        compiler_params=pltpu.CompilerParams(vmem_limit_bytes=limit << 20),
        cost_estimate=pl.CostEstimate(flops=flops, bytes_accessed=10**5, transcendentals=0),
        name=name,
    )(*args)


def body(velocity, counts, src_cell, weights, dst_cell, blade_tile, blade_cell, blade_coef):
    vel = velocity.reshape(3, 512, 128)
    src = src_cell.reshape(72, 128)
    weight = weights.reshape(72, 128)
    dst = dst_cell.reshape(72, 128)
    turbines, points = blade_cell.shape
    count_x, count_y = lax.axis_size("gx"), lax.axis_size("gy")
    mine = (lax.axis_index("gx") * count_y + lax.axis_index("gy")).reshape(1).astype(jnp.int32)
    ints = lambda n: pltpu.SMEM((n,), jnp.int32)

    whole = ((72, 128), jnp.int32, VMEM)
    ints_t = (blade_tile.shape, jnp.int32, VMEM)
    given = (counts, vel, src, weight, dst, blade_tile, blade_cell, blade_coef)
    far, table, vel, src, weight, dst, tile, cell, coef, pts, rotor = call(
        make_far_gather(count_y, 12, 4),
        "far_gather",
        [((6, 4, 8, 128), F32, VMEM), ((3, 256, 512), BF16, VMEM), ((3, 512, 128), F32, VMEM), whole]
        + [((72, 128), F32, VMEM), whole, ints_t, ints_t, (blade_tile.shape, F32, VMEM)]
        + [((3, turbines, points), F32, VMEM), ((8, 128), F32, VMEM)],
        [SMEM] + [HBM] * 8,
        (mine,) + tuple(pltpu.with_memory_space_constraint(v, pltpu.HBM) for v in given),
        [pltpu.SemaphoreType.DMA((10,)), pltpu.SMEM((1, 1, 9), jnp.int32), ints(72), ints(8), ints(32)],
        flops=5 * 10**9,
    )
    low = swap(jnp.concatenate([far[0:3].reshape(96, 128), rotor], axis=0), "gx", 1)
    high = swap_next(far[3:6].reshape(96, 128), "gx")
    own, acc = call(
        make_near_gather(count_y, 8, 4),
        "near_gather",
        [((3, 4, 8, 128), F32, VMEM), ((512, 512), F32, VMEM)],
        [SMEM] + [VMEM] * 4,
        (mine, table, src, weight, dst),
        [ints(48), ints(8)],
        flops=4 * 10**9,
    )
    rotor = rotor + low[96:]
    own = own.reshape(96, 128)

    def y_payload(t):
        return jnp.concatenate([part[t * 32 : t * 32 + 32] for part in (low, own, high)] + [rotor], axis=0)

    first = swap(y_payload(0), "gy", 1)
    rotor = rotor + first[96:]
    second = swap_next(y_payload(2), "gy")
    (edge,) = call(
        make_level_edges(count_y),
        "level_edges",
        [((144, 512), F32, VMEM)],
        [SMEM] + [VMEM] * 4,
        (mine, acc, low, high, dst),
        [pltpu.VMEM((2, 4, 8, 128), F32), ints(48), ints(8)],
        flops=4 * 10**9,
    )
    (edge,) = call(
        make_core_edges(count_y),
        "core_edges",
        [((144, 512), F32, VMEM)],
        [SMEM] + [VMEM] * 3,
        (mine, edge, first, dst),
        [pltpu.VMEM((3, 4, 8, 128), F32), ints(48), ints(8)],
        flops=4 * 10**9,
    )
    rotor = rotor + second[96:]
    for axis, count in (("gx", count_x), ("gy", count_y)):
        step = 4
        while step < count:
            rotor = rotor + swap(rotor, axis, step)
            step *= 2
    lists = pltpu.VMEM((8, 4, 8, 128), F32)
    face_x, face_y = ((3, 64, 128), F32, VMEM), ((3, 8, 128), F32, VMEM)
    edge, xa, xb, ya, yb = call(
        make_edge_scatter(count_y),
        "edge_scatter",
        [((3, 128, 128), F32, VMEM), face_x, face_x, face_y, face_y],
        [SMEM] + [VMEM] * 4,
        (mine, edge, second, dst, vel),
        [pltpu.VMEM((144, 512), F32), pltpu.VMEM((3, 4, 8, 128), F32), ints(48), ints(8)],
        flops=4 * 10**9,
    )
    xb = swap_next(jnp.concatenate([xb.reshape(192, 128), rotor], axis=0), "gx")
    xa = swap(xa.reshape(192, 128), "gx", 1)
    ya = swap(ya, "gy", 1)
    yb = swap_next(yb, "gy")
    (inner,) = call(
        make_inner_scatter(count_y),
        "inner_scatter",
        [((3, 384, 128), F32, VMEM)],
        [SMEM] + [VMEM] * 7,
        (mine, acc, low, high, first, second, dst, vel),
        [pltpu.VMEM((384, 512), F32), lists, ints(96), ints(8)],
        flops=6 * 10**9,
    )
    rotor = rotor + xb[192:]
    updated, forcing = call(
        make_stencil(count_y),
        "stencil",
        [((3, 8, 64, 128), F32, HBM), ((3, 512, 128), F32, HBM)],
        [SMEM] + [VMEM] * 11,
        (mine, edge, inner, tile, cell, coef, pts, rotor, xa, xb, ya, yb),
        [pltpu.VMEM((3, 8, 64, 128), F32), pltpu.VMEM((3, 512, 128), F32), pltpu.VMEM((turbines, 128), F32)]
        + [pltpu.SemaphoreType.DMA((9,)), ints(32)],
    )
    return updated, forcing.reshape(velocity.shape)


def solution(mesh):
    grid = P("gx", "gy", None)
    lists = P("gx", "gy", None, None)
    field = P(None, "gx", "gy", None)
    return jax.shard_map(
        body,
        mesh=mesh,
        in_specs=(field, grid, lists, lists, lists, P(), P(), P()),
        out_specs=(field, field),
        check_vma=False,
    )
```

```python
import jax
import jax.numpy as jnp
from jax import lax
from jax.experimental import pallas as pl
from jax.experimental.pallas import tpu as pltpu
from jax.sharding import PartitionSpec as P

F32 = jnp.float32
BF16 = jnp.bfloat16
VMEM = pl.BlockSpec(memory_space=pltpu.VMEM)
SMEM = pl.BlockSpec(memory_space=pltpu.SMEM)
HBM = pl.BlockSpec(memory_space=pltpu.HBM)


def halves(value):
    high = value.astype(BF16)
    low = (value - high.astype(F32)).astype(BF16)
    return high, low


def one_hot(extent, index):
    rows = lax.broadcasted_iota(jnp.int32, (extent, index.shape[1]), 0)
    return jnp.where(rows == index, 1.0, 0.0).astype(BF16)


def pick(table, cell):
    key = (cell & 127) | (((cell >> 15) & 1) << 7)
    place = (cell >> 7) & 255
    hot = one_hot(256, key)
    hot = jnp.concatenate([hot, hot], axis=0)
    here = lax.broadcasted_iota(jnp.int32, (256, cell.shape[1]), 0) == place
    out = []
    for c in range(3):
        found = jnp.dot(table[c], hot, preferred_element_type=F32)
        out.append(jnp.sum(jnp.where(here, found, 0.0), axis=0, keepdims=True))
    return out


def spread(extent, row, level, values):
    hot = one_hot(extent, row)
    at_level = lax.broadcasted_iota(jnp.int32, (128, level.shape[1]), 0) == level
    high, low = [], []
    for value in values:
        vh = value.astype(BF16).astype(F32)
        high.append(jnp.where(at_level, vh, 0.0).astype(BF16))
        low.append(jnp.where(at_level, value - vh, 0.0).astype(BF16))
    left = jnp.concatenate([hot, hot], axis=1)
    right = jnp.concatenate([jnp.concatenate(high, axis=0), jnp.concatenate(low, axis=0)], axis=1)
    return lax.dot_general(left, right, (((1,), (1,)), ((), ())), preferred_element_type=F32)


def sides(mine_ref, count_y):
    mine = mine_ref[0]
    return 1 - 2 * ((mine // count_y) & 1), 1 - 2 * (mine & 1)


def list_blocks(lists, listed):
    total = jnp.int32(0)
    for used, tag in lists:
        for j in range(8):
            listed[total + j] = tag * 8 + j
        total = total + ((used + 127) >> 7)
    return total


def run_chunks(total, large, small, chunk):
    many = (total + small - 1) // large

    def big(i, carry):
        chunk(i * large, large)
        return carry

    lax.fori_loop(0, many, big, 0)

    def rest(i, carry):
        chunk(many * large + i * small, small)
        return carry

    lax.fori_loop(0, jnp.maximum(total - many * large + small - 1, 0) // small, rest, 0)


def gather_lists(table, total, large, small, listed, direction, src_ref, w_ref, out_ref):
    for k in range(large):
        listed[total + k] = listed[total - 1]

    def chunk(first, width):
        blocks = [listed[first + k] for k in range(width)]
        rows = [direction[b >> 3] * 8 + (b & 7) for b in blocks]
        cell = jnp.concatenate([src_ref[pl.ds(r, 1), :] for r in rows], axis=1)
        found = pick(table, cell)
        for k, (b, r) in enumerate(zip(blocks, rows)):
            j = b & 7
            weight = w_ref[pl.ds(r, 1), :]
            for c in range(3):
                out_ref[b >> 3, c, pl.ds(j, 1), :] = found[c][:, k * 128 : (k + 1) * 128] * weight
            out_ref[b >> 3, 3, pl.ds(j, 1), :] = weight

    run_chunks(total, large, small, chunk)


def make_far_gather(count_y, large, small):
    def kernel(
        mine_ref, cnt_hbm, vel_hbm, src_hbm, w_hbm, dst_hbm, tile_hbm, cell_hbm, coef_hbm,
        out_ref, table, vel_ref, src_ref, w_ref, dst_ref, tile_ref, cell_ref, coef_ref, pts_ref, rot_ref,
        sem, cnt_ref, listed, direction, tlist,
    ):
        half = vel_ref.shape[1] // 2
        pairs = [(cnt_hbm, cnt_ref), (src_hbm, src_ref), (w_hbm, w_ref), (tile_hbm, tile_ref)]
        pairs += [(vel_hbm.at[c], vel_ref.at[c]) for c in range(3)]
        pairs += [(cell_hbm, cell_ref), (coef_hbm, coef_ref), (dst_hbm, dst_ref)]
        copies = [pltpu.make_async_copy(a, b, sem.at[k]) for k, (a, b) in enumerate(pairs)]
        for copy in copies:
            copy.start()
        out_ref[...] = jnp.zeros_like(out_ref)
        pts_ref[...] = jnp.zeros_like(pts_ref)
        for copy in copies[:4]:
            copy.wait()
        n_turb = active_turbines(tile_ref, mine_ref[0], tlist)
        slot = lax.broadcasted_iota(jnp.int32, (8, 128), 0) * 128 + lax.broadcasted_iota(jnp.int32, (8, 128), 1)
        for d in range(9):
            part = slice(d * 8, d * 8 + 8)
            w_ref[part, :] = jnp.where(slot < cnt_ref[0, 0, d], w_ref[part, :], 0.0)
        side_x, side_y = sides(mine_ref, count_y)
        lists = []
        for s in range(2):
            for t in range(3):
                d = 3 * (side_x * (1 - 2 * s) + 1) + side_y * (1 - t) + 1
                direction[3 * s + t] = d
                lists.append((cnt_ref[0, 0, d], 3 * s + t))
        total = list_blocks(lists, listed)
        for c in range(3):
            copies[4 + c].wait()
            for piece in range(2):
                high, low = halves(vel_ref[c, piece * half : (piece + 1) * half, :])
                table[c, :, piece * 128 : (piece + 1) * 128] = high
                table[c, :, 256 + piece * 128 : 256 + (piece + 1) * 128] = low
        for copy in copies[7:]:
            copy.wait()
        gather_lists(table, total, large, small, listed, direction, src_ref, w_ref, out_ref)
        gather_points(mine_ref[0], n_turb, table, tile_ref, cell_ref, pts_ref, rot_ref, tlist)

    return kernel


def active_turbines(tile_ref, mine, listed):
    turbines = tile_ref.shape[0]
    owned = jnp.where(tile_ref[...] == mine, 1.0, 0.0)
    found = jnp.max(owned, axis=1, keepdims=True)
    total = jnp.int32(0)
    for t in range(turbines):
        listed[total] = t
        total = total + jnp.where(found[t, 0] > 0.5, 1, 0)
    listed[total] = 0
    return total


def diagonal(turbines):
    shape = (turbines, 128)
    return lax.broadcasted_iota(jnp.int32, shape, 0) == lax.broadcasted_iota(jnp.int32, shape, 1)


def gather_points(mine, n_turb, table, tile_ref, cell_ref, pts_ref, rot_ref, tlist):
    turbines, points = tile_ref.shape

    def turbine(i, carry):
        pair = [tlist[2 * i], tlist[2 * i + 1]]
        cell = jnp.concatenate([cell_ref[pl.ds(t, 1), :] for t in pair], axis=1)
        found = pick(table, cell)
        for k, t in enumerate(pair):
            owned = tile_ref[pl.ds(t, 1), :] == mine
            for c in range(3):
                pts_ref[c, pl.ds(t, 1), :] = jnp.where(owned, found[c][:, k * points : (k + 1) * points], 0.0)
        return carry

    lax.fori_loop(0, (n_turb + 1) >> 1, turbine, 0)
    sums = jnp.broadcast_to(jnp.sum(pts_ref[0], axis=1, keepdims=True), (turbines, 128))
    row = jnp.sum(jnp.where(diagonal(turbines), sums, 0.0), axis=0, keepdims=True)
    rot_ref[...] = jnp.broadcast_to(row, rot_ref.shape)


def used_slots(weight):
    return jnp.sum(jnp.where(weight != 0.0, 1.0, 0.0)).astype(jnp.int32)


def make_near_gather(count_y, large, small):
    def kernel(mine_ref, table, src_ref, w_ref, dst_ref, out_ref, acc, listed, direction):
        out_ref[...] = jnp.zeros_like(out_ref)
        acc[...] = jnp.zeros_like(acc)
        _, side_y = sides(mine_ref, count_y)
        used = [used_slots(w_ref[d * 8 : d * 8 + 8, :]) for d in (3, 4, 5)]
        last = jnp.where(side_y > 0, used[0], used[2])
        lists = [(jnp.where(side_y > 0, used[2], used[0]), 0), (used[1], 1), (last, 2)]
        for t in range(3):
            direction[t] = 3 + side_y * (1 - t) + 1
        total = list_blocks(lists, listed)
        gather_lists(table, total, large, small, listed, direction, src_ref, w_ref, out_ref)
        direction[0] = 4
        scatter_lists(out_ref.at[1:2], 1, direction, dst_ref, listed, acc, 512, lambda row: row, 8, 4)

    return kernel


def scatter_lists(val, n_lists, direction, dst_ref, listed, acc, extent, place, large, small):
    lists = []
    for q in range(n_lists):
        lists.append((used_slots(val[q, 3]), q))
    total = list_blocks(lists, listed)
    for k in range(large):
        listed[total + k] = 0

    def chunk(first, width):
        cells, vals = [], [[], [], [], []]
        for k in range(width):
            b = listed[first + k]
            q, j = b >> 3, b & 7
            keep = jnp.where(first + k < total, 1.0, 0.0)
            cells.append(dst_ref[pl.ds(direction[q] * 8 + j, 1), :])
            for c in range(4):
                vals[c].append(val[q, c, pl.ds(j, 1), :] * keep)
        cell = jnp.concatenate(cells, axis=1)
        vals = [jnp.concatenate(v, axis=1) for v in vals]
        acc[...] += spread(extent, place((cell >> 7) & 511), cell & 127, vals)

    run_chunks(total, large, small, chunk)


def load_level_lists(side_x, low_ref, high_ref, start, val, direction):
    for q, ref in enumerate((low_ref, high_ref)):
        for c in range(4):
            val[start + q, c] = ref[32 + c * 8 : 40 + c * 8, :]
        direction[start + q] = 3 * (side_x * (2 * q - 1) + 1) + 1


def make_level_edges(count_y):
    def kernel(mine_ref, base_ref, low_ref, high_ref, dst_ref, edge, val, listed, direction):
        side_x, _ = sides(mine_ref, count_y)
        load_level_lists(side_x, low_ref, high_ref, 0, val, direction)
        edge[...] = edge_rows(base_ref, None, slice(None))
        scatter_lists(val, 2, direction, dst_ref, listed, edge, 144, edge_place, 12, 4)

    return kernel


def make_core_edges(count_y):
    def kernel(mine_ref, base_ref, first_ref, dst_ref, edge, val, listed, direction):
        side_x, side_y = sides(mine_ref, count_y)
        load_later_lists(side_x, -side_y, first_ref, 0, val, direction)
        edge[...] = base_ref[...]
        scatter_lists(val, 3, direction, dst_ref, listed, edge, 144, edge_place, 12, 4)

    return kernel


def load_later_lists(side_x, from_y, ref, start, val, direction):
    for s in range(3):
        for c in range(4):
            at = (s * 4 + c) * 8
            val[start + s, c] = ref[at : at + 8, :]
        direction[start + s] = 3 * (side_x * (s - 1) + 1) + from_y + 1


def corrected(acc, vel, c):
    return (1.0 - acc[:, 384:512]) * vel - acc[:, c * 128 : (c + 1) * 128]


def edge_rows(ref, c, columns):
    at = (lambda r: ref[r, columns]) if c is None else (lambda r: ref[c, r, columns])
    spare = [at(slice(0, 2))]
    low = [at(slice(x * 64, x * 64 + 1)) for x in range(1, 7)]
    high = [at(slice(x * 64 + 63, x * 64 + 64)) for x in range(1, 7)]
    return jnp.concatenate([at(slice(0, 64)), at(slice(448, 512))] + low + spare + high + spare, axis=0)


def edge_place(row):
    x, y = row >> 6, row & 63
    inside = jnp.where(y == 0, 127 + x, jnp.where(y == 63, 135 + x, 1024))
    return jnp.where(x == 0, y, jnp.where(x == 7, 64 + y, inside))


def make_edge_scatter(count_y):
    def kernel(
        mine_ref, base_ref, second_ref, dst_ref, vel_ref,
        cor_ref, xa_ref, xb_ref, ya_ref, yb_ref, acc, val, listed, direction,
    ):
        side_x, side_y = sides(mine_ref, count_y)
        load_later_lists(side_x, side_y, second_ref, 0, val, direction)
        acc[...] = base_ref[...]
        scatter_lists(val, 3, direction, dst_ref, listed, acc, 144, edge_place, 12, 4)
        for c in range(3):
            cor = corrected(acc, edge_rows(vel_ref, c, slice(None)), c)
            cor_ref[c] = cor[0:128]
            xa_ref[c] = jnp.where(side_x > 0, cor[64:128], cor[0:64])
            xb_ref[c] = jnp.where(side_x > 0, cor[0:64], cor[64:128])
            low = jnp.concatenate([cor[0:1], cor[128:134], cor[64:65]], axis=0)
            high = jnp.concatenate([cor[63:64], cor[136:142], cor[127:128]], axis=0)
            ya_ref[c] = jnp.where(side_y > 0, high, low)
            yb_ref[c] = jnp.where(side_y > 0, low, high)

    return kernel


def make_inner_scatter(count_y):
    def kernel(mine_ref, base_ref, low_ref, high_ref, first_ref, second_ref, dst_ref, vel_ref, cor_ref, acc, val, listed, direction):
        side_x, side_y = sides(mine_ref, count_y)
        load_later_lists(side_x, -side_y, first_ref, 0, val, direction)
        load_later_lists(side_x, side_y, second_ref, 3, val, direction)
        load_level_lists(side_x, low_ref, high_ref, 6, val, direction)
        acc[...] = base_ref[64:448, :]
        scatter_lists(val, 8, direction, dst_ref, listed, acc, 384, lambda row: row - 64, 12, 4)
        for c in range(3):
            cor_ref[c] = corrected(acc, vel_ref[c, 64:448, :], c)

    return kernel


def add_forces(mine, tile_ref, cell_ref, coef_ref, pts_ref, rot_ref, column, out_ref, tlist):
    out_ref[...] = jnp.zeros_like(out_ref)
    turbines = tile_ref.shape[0]
    sums = jnp.broadcast_to(rot_ref[0:1, :], (turbines, 128))
    sums = jnp.sum(jnp.where(diagonal(turbines), sums, 0.0), axis=1, keepdims=True)
    column[...] = jnp.broadcast_to(sums, (turbines, 128))
    n_turb = active_turbines(tile_ref, mine, tlist)
    points = tile_ref.shape[1]

    def turbine(i, carry):
        pair = [tlist[2 * i], tlist[2 * i + 1]]
        cell = jnp.concatenate([cell_ref[pl.ds(t, 1), :] for t in pair], axis=1)
        force = [[], [], []]
        for k, t in enumerate(pair):
            keep = jnp.where(2 * i + k < n_turb, 1.0 / points, 0.0)
            scale = -coef_ref[pl.ds(t, 1), :] * (column[pl.ds(t, 1), 0:1] * keep)
            for c in range(3):
                force[c].append(scale * pts_ref[c, pl.ds(t, 1), :])
        force = [jnp.concatenate(f, axis=1) for f in force]
        got = spread(512, (cell >> 7) & 511, cell & 127, force)
        for c in range(3):
            out_ref[c] += got[:, c * 128 : (c + 1) * 128]
        return carry

    lax.fori_loop(0, (n_turb + 1) >> 1, turbine, 0)


def make_stencil(count_y):
    def kernel(
        mine_ref, edge_ref, inner_ref, tile_ref, cell_ref, coef_ref, pts_ref, rot_ref, xa_ref, xb_ref, ya_ref, yb_ref,
        out_hbm, frc_hbm, out_ref, frc_ref, column, sem, tlist,
    ):
        add_forces(mine_ref[0], tile_ref, cell_ref, coef_ref, pts_ref, rot_ref, column, frc_ref, tlist)
        given = pltpu.make_async_copy(frc_ref, frc_hbm, sem.at[8])
        given.start()
        side_x, side_y = sides(mine_ref, count_y)
        lane = lax.broadcasted_iota(jnp.int32, (64, 128), 1)

        def slab(c, x):
            if x < 0:
                return jnp.where(side_x > 0, xb_ref[c * 64 : c * 64 + 64, :], xa_ref[c * 64 : c * 64 + 64, :])
            if x > 7:
                return jnp.where(side_x > 0, xa_ref[c * 64 : c * 64 + 64, :], xb_ref[c * 64 : c * 64 + 64, :])
            ref, at = (inner_ref, x - 1) if 1 <= x < 7 else (edge_ref, 0 if x == 0 else 1)
            return ref[c, at * 64 : at * 64 + 64, :]

        copies = []
        for x in range(8):
            now = [slab(c, x) for c in range(3)]
            up = [0.03 - 0.1 * v for v in now]
            down = [0.03 + 0.1 * v for v in now]
            up[2] = jnp.where(lane == 127, 0.0, up[2])
            down[2] = jnp.where(lane == 0, 0.0, down[2])
            for c in range(3):
                u = now[c]
                west, east = slab(c, x - 1), slab(c, x + 1)
                ya, yb = ya_ref[c, x : x + 1, :], yb_ref[c, x : x + 1, :]
                south = jnp.concatenate([jnp.where(side_y > 0, yb, ya), u[:-1]], axis=0)
                north = jnp.concatenate([u[1:], jnp.where(side_y > 0, ya, yb)], axis=0)
                upper, lower = pltpu.roll(u, 127, 1), pltpu.roll(u, 1, 1)
                moved = (up[0] * east + down[0] * west) + (up[1] * north + down[1] * south)
                moved = moved + (up[2] * upper + down[2] * lower)
                out_ref[c, x] = 0.82 * u + (moved + 0.2 * frc_ref[c, x * 64 : x * 64 + 64, :])
            copies.append(pltpu.make_async_copy(out_ref.at[:, x], out_hbm.at[:, x], sem.at[x]))
            copies[-1].start()
        for copy in copies:
            copy.wait()
        given.wait()

    return kernel


def swap(value, axis, step):
    count = lax.axis_size(axis)
    return lax.ppermute(value, axis, [(i, i ^ step) for i in range(count)])


def swap_next(value, axis):
    count = lax.axis_size(axis)
    return lax.ppermute(value, axis, [(i, (i - 1 if i % 2 == 0 else i + 1) % count) for i in range(count)])


def call(kernel, name, outs, ins, args, scratch=(), flops=10**9, limit=32):
    return pl.pallas_call(
        kernel,
        out_shape=tuple(jax.ShapeDtypeStruct(shape, dtype) for shape, dtype, _ in outs),
        in_specs=ins,
        out_specs=tuple(spec for _, _, spec in outs),
        scratch_shapes=list(scratch),
        compiler_params=pltpu.CompilerParams(vmem_limit_bytes=limit << 20),
        cost_estimate=pl.CostEstimate(flops=flops, bytes_accessed=10**5, transcendentals=0),
        name=name,
    )(*args)


def body(velocity, counts, src_cell, weights, dst_cell, blade_tile, blade_cell, blade_coef):
    vel = velocity.reshape(3, 512, 128)
    src = src_cell.reshape(72, 128)
    weight = weights.reshape(72, 128)
    dst = dst_cell.reshape(72, 128)
    turbines, points = blade_cell.shape
    count_x, count_y = lax.axis_size("gx"), lax.axis_size("gy")
    mine = (lax.axis_index("gx") * count_y + lax.axis_index("gy")).reshape(1).astype(jnp.int32)
    ints = lambda n: pltpu.SMEM((n,), jnp.int32)

    whole = ((72, 128), jnp.int32, VMEM)
    ints_t = (blade_tile.shape, jnp.int32, VMEM)
    given = (counts, vel, src, weight, dst, blade_tile, blade_cell, blade_coef)
    far, table, vel, src, weight, dst, tile, cell, coef, pts, rotor = call(
        make_far_gather(count_y, 12, 4),
        "far_gather",
        [((6, 4, 8, 128), F32, VMEM), ((3, 256, 512), BF16, VMEM), ((3, 512, 128), F32, VMEM), whole]
        + [((72, 128), F32, VMEM), whole, ints_t, ints_t, (blade_tile.shape, F32, VMEM)]
        + [((3, turbines, points), F32, VMEM), ((8, 128), F32, VMEM)],
        [SMEM] + [HBM] * 8,
        (mine,) + tuple(pltpu.with_memory_space_constraint(v, pltpu.HBM) for v in given),
        [pltpu.SemaphoreType.DMA((10,)), pltpu.SMEM((1, 1, 9), jnp.int32), ints(72), ints(8), ints(32)],
        flops=5 * 10**9,
    )
    low = swap(far[0:3].reshape(96, 128), "gx", 1)
    high = swap_next(jnp.concatenate([far[3:6].reshape(96, 128), rotor], axis=0), "gx")
    own, acc = call(
        make_near_gather(count_y, 8, 4),
        "near_gather",
        [((3, 4, 8, 128), F32, VMEM), ((512, 512), F32, VMEM)],
        [SMEM] + [VMEM] * 4,
        (mine, table, src, weight, dst),
        [ints(48), ints(8)],
        flops=4 * 10**9,
    )
    rotor = rotor + high[96:]
    own = own.reshape(96, 128)

    def y_payload(t):
        return jnp.concatenate([part[t * 32 : t * 32 + 32] for part in (low, own, high)] + [rotor], axis=0)

    first = swap(y_payload(0), "gy", 1)
    rotor = rotor + first[96:]
    second = swap_next(y_payload(2), "gy")
    (edge,) = call(
        make_level_edges(count_y),
        "level_edges",
        [((144, 512), F32, VMEM)],
        [SMEM] + [VMEM] * 4,
        (mine, acc, low, high, dst),
        [pltpu.VMEM((2, 4, 8, 128), F32), ints(48), ints(8)],
        flops=4 * 10**9,
    )
    (edge,) = call(
        make_core_edges(count_y),
        "core_edges",
        [((144, 512), F32, VMEM)],
        [SMEM] + [VMEM] * 3,
        (mine, edge, first, dst),
        [pltpu.VMEM((3, 4, 8, 128), F32), ints(48), ints(8)],
        flops=4 * 10**9,
    )
    rotor = rotor + second[96:]
    for axis, count in (("gx", count_x), ("gy", count_y)):
        step = 4
        while step < count:
            rotor = rotor + swap(rotor, axis, step)
            step *= 2
    lists = pltpu.VMEM((8, 4, 8, 128), F32)
    face_x, face_y = ((3, 64, 128), F32, VMEM), ((3, 8, 128), F32, VMEM)
    edge, xa, xb, ya, yb = call(
        make_edge_scatter(count_y),
        "edge_scatter",
        [((3, 128, 128), F32, VMEM), face_x, face_x, face_y, face_y],
        [SMEM] + [VMEM] * 4,
        (mine, edge, second, dst, vel),
        [pltpu.VMEM((144, 512), F32), pltpu.VMEM((3, 4, 8, 128), F32), ints(48), ints(8)],
        flops=4 * 10**9,
    )
    xb = swap_next(xb.reshape(192, 128), "gx")
    rotor, ya, yb = lax.optimization_barrier((rotor, ya, yb))
    xa = swap(jnp.concatenate([xa.reshape(192, 128), rotor], axis=0), "gx", 1)
    ya = swap(ya, "gy", 1)
    yb = swap_next(yb, "gy")
    (inner,) = call(
        make_inner_scatter(count_y),
        "inner_scatter",
        [((3, 384, 128), F32, VMEM)],
        [SMEM] + [VMEM] * 7,
        (mine, acc, low, high, first, second, dst, vel),
        [pltpu.VMEM((384, 512), F32), lists, ints(96), ints(8)],
        flops=6 * 10**9,
    )
    xa, xb, ya, yb = lax.optimization_barrier((xa, xb, ya, yb))
    rotor = rotor + xa[192:]
    updated, forcing = call(
        make_stencil(count_y),
        "stencil",
        [((3, 8, 64, 128), F32, HBM), ((3, 512, 128), F32, HBM)],
        [SMEM] + [VMEM] * 11,
        (mine, edge, inner, tile, cell, coef, pts, rotor, xa, xb, ya, yb),
        [pltpu.VMEM((3, 8, 64, 128), F32), pltpu.VMEM((3, 512, 128), F32), pltpu.VMEM((turbines, 128), F32)]
        + [pltpu.SemaphoreType.DMA((9,)), ints(32)],
    )
    return updated, forcing.reshape(velocity.shape)


def solution(mesh):
    grid = P("gx", "gy", None)
    lists = P("gx", "gy", None, None)
    field = P(None, "gx", "gy", None)
    return jax.shard_map(
        body,
        mesh=mesh,
        in_specs=(field, grid, lists, lists, lists, P(), P(), P()),
        out_specs=(field, field),
        check_vma=False,
    )
```

```python
import jax
import jax.numpy as jnp
from jax import lax
from jax.experimental import pallas as pl
from jax.experimental.pallas import tpu as pltpu
from jax.sharding import PartitionSpec as P

F32 = jnp.float32
BF16 = jnp.bfloat16
VMEM = pl.BlockSpec(memory_space=pltpu.VMEM)
SMEM = pl.BlockSpec(memory_space=pltpu.SMEM)
HBM = pl.BlockSpec(memory_space=pltpu.HBM)


def halves(value):
    high = value.astype(BF16)
    low = (value - high.astype(F32)).astype(BF16)
    return high, low


def one_hot(extent, index):
    rows = lax.broadcasted_iota(jnp.int32, (extent, index.shape[1]), 0)
    return jnp.where(rows == index, 1.0, 0.0).astype(BF16)


def pick(table, cell):
    key = (cell & 127) | (((cell >> 15) & 1) << 7)
    place = (cell >> 7) & 255
    hot = one_hot(256, key)
    hot = jnp.concatenate([hot, hot], axis=0)
    here = lax.broadcasted_iota(jnp.int32, (256, cell.shape[1]), 0) == place
    out = []
    for c in range(3):
        found = jnp.dot(table[c], hot, preferred_element_type=F32)
        out.append(jnp.sum(jnp.where(here, found, 0.0), axis=0, keepdims=True))
    return out


def spread(extent, row, level, values):
    hot = one_hot(extent, row)
    at_level = lax.broadcasted_iota(jnp.int32, (128, level.shape[1]), 0) == level
    high, low = [], []
    for value in values:
        vh = value.astype(BF16).astype(F32)
        high.append(jnp.where(at_level, vh, 0.0).astype(BF16))
        low.append(jnp.where(at_level, value - vh, 0.0).astype(BF16))
    left = jnp.concatenate([hot, hot], axis=1)
    right = jnp.concatenate([jnp.concatenate(high, axis=0), jnp.concatenate(low, axis=0)], axis=1)
    return lax.dot_general(left, right, (((1,), (1,)), ((), ())), preferred_element_type=F32)


def sides(mine_ref, count_y):
    mine = mine_ref[0]
    return 1 - 2 * ((mine // count_y) & 1), 1 - 2 * (mine & 1)


def list_blocks(lists, listed):
    total = jnp.int32(0)
    for used, tag in lists:
        for j in range(8):
            listed[total + j] = tag * 8 + j
        total = total + ((used + 127) >> 7)
    return total


def run_chunks(total, large, small, chunk):
    many = (total + small - 1) // large

    def big(i, carry):
        chunk(i * large, large)
        return carry

    lax.fori_loop(0, many, big, 0)

    def rest(i, carry):
        chunk(many * large + i * small, small)
        return carry

    lax.fori_loop(0, jnp.maximum(total - many * large + small - 1, 0) // small, rest, 0)


def gather_lists(table, total, large, small, listed, direction, src_ref, w_ref, out_ref):
    for k in range(large):
        listed[total + k] = listed[total - 1]

    def chunk(first, width):
        blocks = [listed[first + k] for k in range(width)]
        rows = [direction[b >> 3] * 8 + (b & 7) for b in blocks]
        cell = jnp.concatenate([src_ref[pl.ds(r, 1), :] for r in rows], axis=1)
        found = pick(table, cell)
        for k, (b, r) in enumerate(zip(blocks, rows)):
            j = b & 7
            weight = w_ref[pl.ds(r, 1), :]
            for c in range(3):
                out_ref[b >> 3, c, pl.ds(j, 1), :] = found[c][:, k * 128 : (k + 1) * 128] * weight
            out_ref[b >> 3, 3, pl.ds(j, 1), :] = weight

    run_chunks(total, large, small, chunk)


def make_far_gather(count_y, large, small):
    def kernel(
        mine_ref, cnt_hbm, vel_hbm, src_hbm, w_hbm, dst_hbm, tile_hbm, cell_hbm, coef_hbm,
        out_ref, table, vel_ref, src_ref, w_ref, dst_ref, tile_ref, cell_ref, coef_ref, pts_ref, rot_ref,
        sem, cnt_ref, listed, direction, tlist,
    ):
        half = vel_ref.shape[1] // 2
        pairs = [(cnt_hbm, cnt_ref), (src_hbm, src_ref), (w_hbm, w_ref), (tile_hbm, tile_ref)]
        pairs += [(vel_hbm.at[c], vel_ref.at[c]) for c in range(3)]
        pairs += [(cell_hbm, cell_ref), (coef_hbm, coef_ref), (dst_hbm, dst_ref)]
        copies = [pltpu.make_async_copy(a, b, sem.at[k]) for k, (a, b) in enumerate(pairs)]
        for copy in copies:
            copy.start()
        out_ref[...] = jnp.zeros_like(out_ref)
        pts_ref[...] = jnp.zeros_like(pts_ref)
        for copy in copies[:4]:
            copy.wait()
        n_turb = active_turbines(tile_ref, mine_ref[0], tlist)
        slot = lax.broadcasted_iota(jnp.int32, (8, 128), 0) * 128 + lax.broadcasted_iota(jnp.int32, (8, 128), 1)
        for d in range(9):
            part = slice(d * 8, d * 8 + 8)
            w_ref[part, :] = jnp.where(slot < cnt_ref[0, 0, d], w_ref[part, :], 0.0)
        side_x, side_y = sides(mine_ref, count_y)
        lists = []
        for s in range(2):
            for t in range(3):
                d = 3 * (side_x * (1 - 2 * s) + 1) + side_y * (1 - t) + 1
                direction[3 * s + t] = d
                lists.append((cnt_ref[0, 0, d], 3 * s + t))
        total = list_blocks(lists, listed)
        for c in range(3):
            copies[4 + c].wait()
            for piece in range(2):
                high, low = halves(vel_ref[c, piece * half : (piece + 1) * half, :])
                table[c, :, piece * 128 : (piece + 1) * 128] = high
                table[c, :, 256 + piece * 128 : 256 + (piece + 1) * 128] = low
        for copy in copies[7:]:
            copy.wait()
        gather_lists(table, total, large, small, listed, direction, src_ref, w_ref, out_ref)
        gather_points(mine_ref[0], n_turb, table, tile_ref, cell_ref, pts_ref, rot_ref, tlist)

    return kernel


def active_turbines(tile_ref, mine, listed):
    turbines = tile_ref.shape[0]
    owned = jnp.where(tile_ref[...] == mine, 1.0, 0.0)
    found = jnp.max(owned, axis=1, keepdims=True)
    total = jnp.int32(0)
    for t in range(turbines):
        listed[total] = t
        total = total + jnp.where(found[t, 0] > 0.5, 1, 0)
    listed[total] = 0
    return total


def diagonal(turbines):
    shape = (turbines, 128)
    return lax.broadcasted_iota(jnp.int32, shape, 0) == lax.broadcasted_iota(jnp.int32, shape, 1)


def gather_points(mine, n_turb, table, tile_ref, cell_ref, pts_ref, rot_ref, tlist):
    turbines, points = tile_ref.shape

    def turbine(i, carry):
        pair = [tlist[2 * i], tlist[2 * i + 1]]
        cell = jnp.concatenate([cell_ref[pl.ds(t, 1), :] for t in pair], axis=1)
        found = pick(table, cell)
        for k, t in enumerate(pair):
            owned = tile_ref[pl.ds(t, 1), :] == mine
            for c in range(3):
                pts_ref[c, pl.ds(t, 1), :] = jnp.where(owned, found[c][:, k * points : (k + 1) * points], 0.0)
        return carry

    lax.fori_loop(0, (n_turb + 1) >> 1, turbine, 0)
    sums = jnp.broadcast_to(jnp.sum(pts_ref[0], axis=1, keepdims=True), (turbines, 128))
    row = jnp.sum(jnp.where(diagonal(turbines), sums, 0.0), axis=0, keepdims=True)
    rot_ref[...] = jnp.broadcast_to(row, rot_ref.shape)


def used_slots(weight):
    return jnp.sum(jnp.where(weight != 0.0, 1.0, 0.0)).astype(jnp.int32)


def make_near_gather(count_y, large, small):
    def kernel(mine_ref, table, src_ref, w_ref, dst_ref, out_ref, acc, listed, direction):
        out_ref[...] = jnp.zeros_like(out_ref)
        acc[...] = jnp.zeros_like(acc)
        _, side_y = sides(mine_ref, count_y)
        used = [used_slots(w_ref[d * 8 : d * 8 + 8, :]) for d in (3, 4, 5)]
        last = jnp.where(side_y > 0, used[0], used[2])
        lists = [(jnp.where(side_y > 0, used[2], used[0]), 0), (used[1], 1), (last, 2)]
        for t in range(3):
            direction[t] = 3 + side_y * (1 - t) + 1
        total = list_blocks(lists, listed)
        gather_lists(table, total, large, small, listed, direction, src_ref, w_ref, out_ref)
        direction[0] = 4
        scatter_lists(out_ref.at[1:2], 1, direction, dst_ref, listed, acc, 512, lambda row: row, 8, 4)

    return kernel


def scatter_lists(val, n_lists, direction, dst_ref, listed, acc, extent, place, large, small):
    lists = []
    for q in range(n_lists):
        lists.append((used_slots(val[q, 3]), q))
    total = list_blocks(lists, listed)
    for k in range(large):
        listed[total + k] = 0

    def chunk(first, width):
        cells, vals = [], [[], [], [], []]
        for k in range(width):
            b = listed[first + k]
            q, j = b >> 3, b & 7
            keep = jnp.where(first + k < total, 1.0, 0.0)
            cells.append(dst_ref[pl.ds(direction[q] * 8 + j, 1), :])
            for c in range(4):
                vals[c].append(val[q, c, pl.ds(j, 1), :] * keep)
        cell = jnp.concatenate(cells, axis=1)
        vals = [jnp.concatenate(v, axis=1) for v in vals]
        acc[...] += spread(extent, place((cell >> 7) & 511), cell & 127, vals)

    run_chunks(total, large, small, chunk)


def load_level_lists(side_x, low_ref, high_ref, start, val, direction):
    for q, ref in enumerate((low_ref, high_ref)):
        for c in range(4):
            val[start + q, c] = ref[32 + c * 8 : 40 + c * 8, :]
        direction[start + q] = 3 * (side_x * (2 * q - 1) + 1) + 1


def make_level_edges(count_y):
    def kernel(mine_ref, base_ref, low_ref, high_ref, dst_ref, edge, val, listed, direction):
        side_x, _ = sides(mine_ref, count_y)
        load_level_lists(side_x, low_ref, high_ref, 0, val, direction)
        edge[...] = edge_rows(base_ref, None, slice(None))
        scatter_lists(val, 2, direction, dst_ref, listed, edge, 144, edge_place, 12, 4)

    return kernel


def make_core_edges(count_y):
    def kernel(mine_ref, base_ref, first_ref, dst_ref, edge, val, listed, direction):
        side_x, side_y = sides(mine_ref, count_y)
        load_later_lists(side_x, -side_y, first_ref, 0, val, direction)
        edge[...] = base_ref[...]
        scatter_lists(val, 3, direction, dst_ref, listed, edge, 144, edge_place, 12, 4)

    return kernel


def load_later_lists(side_x, from_y, ref, start, val, direction):
    for s in range(3):
        for c in range(4):
            at = (s * 4 + c) * 8
            val[start + s, c] = ref[at : at + 8, :]
        direction[start + s] = 3 * (side_x * (s - 1) + 1) + from_y + 1


def corrected(acc, vel, c):
    return (1.0 - acc[:, 384:512]) * vel - acc[:, c * 128 : (c + 1) * 128]


def edge_rows(ref, c, columns):
    at = (lambda r: ref[r, columns]) if c is None else (lambda r: ref[c, r, columns])
    spare = [at(slice(0, 2))]
    low = [at(slice(x * 64, x * 64 + 1)) for x in range(1, 7)]
    high = [at(slice(x * 64 + 63, x * 64 + 64)) for x in range(1, 7)]
    return jnp.concatenate([at(slice(0, 64)), at(slice(448, 512))] + low + spare + high + spare, axis=0)


def edge_place(row):
    x, y = row >> 6, row & 63
    inside = jnp.where(y == 0, 127 + x, jnp.where(y == 63, 135 + x, 1024))
    return jnp.where(x == 0, y, jnp.where(x == 7, 64 + y, inside))


def make_edge_scatter(count_y):
    def kernel(
        mine_ref, base_ref, second_ref, dst_ref, vel_ref,
        cor_ref, xa_ref, xb_ref, ya_ref, yb_ref, acc, val, listed, direction,
    ):
        side_x, side_y = sides(mine_ref, count_y)
        load_later_lists(side_x, side_y, second_ref, 0, val, direction)
        acc[...] = base_ref[...]
        scatter_lists(val, 3, direction, dst_ref, listed, acc, 144, edge_place, 12, 4)
        for c in range(3):
            cor = corrected(acc, edge_rows(vel_ref, c, slice(None)), c)
            cor_ref[c] = cor[0:128]
            xa_ref[c] = jnp.where(side_x > 0, cor[64:128], cor[0:64])
            xb_ref[c] = jnp.where(side_x > 0, cor[0:64], cor[64:128])
            low = jnp.concatenate([cor[0:1], cor[128:134], cor[64:65]], axis=0)
            high = jnp.concatenate([cor[63:64], cor[136:142], cor[127:128]], axis=0)
            ya_ref[c] = jnp.where(side_y > 0, high, low)
            yb_ref[c] = jnp.where(side_y > 0, low, high)

    return kernel


def make_inner_scatter(count_y):
    def kernel(mine_ref, base_ref, low_ref, high_ref, first_ref, second_ref, dst_ref, vel_ref, cor_ref, acc, val, listed, direction):
        side_x, side_y = sides(mine_ref, count_y)
        load_later_lists(side_x, -side_y, first_ref, 0, val, direction)
        load_later_lists(side_x, side_y, second_ref, 3, val, direction)
        load_level_lists(side_x, low_ref, high_ref, 6, val, direction)
        acc[...] = base_ref[64:448, :]
        scatter_lists(val, 8, direction, dst_ref, listed, acc, 384, lambda row: row - 64, 12, 4)
        for c in range(3):
            cor_ref[c] = corrected(acc, vel_ref[c, 64:448, :], c)

    return kernel


def add_forces(mine, tile_ref, cell_ref, coef_ref, pts_ref, rot_ref, column, out_ref, tlist):
    out_ref[...] = jnp.zeros_like(out_ref)
    turbines = tile_ref.shape[0]
    sums = jnp.broadcast_to(rot_ref[0:1, :], (turbines, 128))
    sums = jnp.sum(jnp.where(diagonal(turbines), sums, 0.0), axis=1, keepdims=True)
    column[...] = jnp.broadcast_to(sums, (turbines, 128))
    n_turb = active_turbines(tile_ref, mine, tlist)
    points = tile_ref.shape[1]

    def turbine(i, carry):
        pair = [tlist[2 * i], tlist[2 * i + 1]]
        cell = jnp.concatenate([cell_ref[pl.ds(t, 1), :] for t in pair], axis=1)
        force = [[], [], []]
        for k, t in enumerate(pair):
            keep = jnp.where(2 * i + k < n_turb, 1.0 / points, 0.0)
            scale = -coef_ref[pl.ds(t, 1), :] * (column[pl.ds(t, 1), 0:1] * keep)
            for c in range(3):
                force[c].append(scale * pts_ref[c, pl.ds(t, 1), :])
        force = [jnp.concatenate(f, axis=1) for f in force]
        got = spread(512, (cell >> 7) & 511, cell & 127, force)
        for c in range(3):
            out_ref[c] += got[:, c * 128 : (c + 1) * 128]
        return carry

    lax.fori_loop(0, (n_turb + 1) >> 1, turbine, 0)


def make_stencil(count_y):
    def kernel(
        mine_ref, edge_ref, inner_ref, tile_ref, cell_ref, coef_ref, pts_ref, rot_ref, xa_ref, xb_ref, ya_ref, yb_ref,
        out_hbm, frc_hbm, out_ref, frc_ref, column, sem, tlist,
    ):
        add_forces(mine_ref[0], tile_ref, cell_ref, coef_ref, pts_ref, rot_ref, column, frc_ref, tlist)
        given = pltpu.make_async_copy(frc_ref, frc_hbm, sem.at[8])
        given.start()
        side_x, side_y = sides(mine_ref, count_y)
        lane = lax.broadcasted_iota(jnp.int32, (64, 128), 1)

        def slab(c, x):
            if x < 0:
                return jnp.where(side_x > 0, xb_ref[c * 64 : c * 64 + 64, :], xa_ref[c * 64 : c * 64 + 64, :])
            if x > 7:
                return jnp.where(side_x > 0, xa_ref[c * 64 : c * 64 + 64, :], xb_ref[c * 64 : c * 64 + 64, :])
            ref, at = (inner_ref, x - 1) if 1 <= x < 7 else (edge_ref, 0 if x == 0 else 1)
            return ref[c, at * 64 : at * 64 + 64, :]

        copies = []
        for x in range(8):
            now = [slab(c, x) for c in range(3)]
            up = [0.03 - 0.1 * v for v in now]
            down = [0.03 + 0.1 * v for v in now]
            up[2] = jnp.where(lane == 127, 0.0, up[2])
            down[2] = jnp.where(lane == 0, 0.0, down[2])
            for c in range(3):
                u = now[c]
                west, east = slab(c, x - 1), slab(c, x + 1)
                ya, yb = ya_ref[c, x : x + 1, :], yb_ref[c, x : x + 1, :]
                south = jnp.concatenate([jnp.where(side_y > 0, yb, ya), u[:-1]], axis=0)
                north = jnp.concatenate([u[1:], jnp.where(side_y > 0, ya, yb)], axis=0)
                upper, lower = pltpu.roll(u, 127, 1), pltpu.roll(u, 1, 1)
                moved = (up[0] * east + down[0] * west) + (up[1] * north + down[1] * south)
                moved = moved + (up[2] * upper + down[2] * lower)
                out_ref[c, x] = 0.82 * u + (moved + 0.2 * frc_ref[c, x * 64 : x * 64 + 64, :])
            copies.append(pltpu.make_async_copy(out_ref.at[:, x], out_hbm.at[:, x], sem.at[x]))
            copies[-1].start()
        for copy in copies:
            copy.wait()
        given.wait()

    return kernel


def swap(value, axis, step):
    count = lax.axis_size(axis)
    return lax.ppermute(value, axis, [(i, i ^ step) for i in range(count)])


def swap_next(value, axis):
    count = lax.axis_size(axis)
    return lax.ppermute(value, axis, [(i, (i - 1 if i % 2 == 0 else i + 1) % count) for i in range(count)])


def call(kernel, name, outs, ins, args, scratch=(), flops=10**9, limit=32):
    return pl.pallas_call(
        kernel,
        out_shape=tuple(jax.ShapeDtypeStruct(shape, dtype) for shape, dtype, _ in outs),
        in_specs=ins,
        out_specs=tuple(spec for _, _, spec in outs),
        scratch_shapes=list(scratch),
        compiler_params=pltpu.CompilerParams(vmem_limit_bytes=limit << 20),
        cost_estimate=pl.CostEstimate(flops=flops, bytes_accessed=10**5, transcendentals=0),
        name=name,
    )(*args)


def body(velocity, counts, src_cell, weights, dst_cell, blade_tile, blade_cell, blade_coef):
    vel = velocity.reshape(3, 512, 128)
    src = src_cell.reshape(72, 128)
    weight = weights.reshape(72, 128)
    dst = dst_cell.reshape(72, 128)
    turbines, points = blade_cell.shape
    count_x, count_y = lax.axis_size("gx"), lax.axis_size("gy")
    mine = (lax.axis_index("gx") * count_y + lax.axis_index("gy")).reshape(1).astype(jnp.int32)
    ints = lambda n: pltpu.SMEM((n,), jnp.int32)

    whole = ((72, 128), jnp.int32, VMEM)
    ints_t = (blade_tile.shape, jnp.int32, VMEM)
    given = (counts, vel, src, weight, dst, blade_tile, blade_cell, blade_coef)
    far, table, vel, src, weight, dst, tile, cell, coef, pts, rotor = call(
        make_far_gather(count_y, 12, 4),
        "far_gather",
        [((6, 4, 8, 128), F32, VMEM), ((3, 256, 512), BF16, VMEM), ((3, 512, 128), F32, VMEM), whole]
        + [((72, 128), F32, VMEM), whole, ints_t, ints_t, (blade_tile.shape, F32, VMEM)]
        + [((3, turbines, points), F32, VMEM), ((8, 128), F32, VMEM)],
        [SMEM] + [HBM] * 8,
        (mine,) + tuple(pltpu.with_memory_space_constraint(v, pltpu.HBM) for v in given),
        [pltpu.SemaphoreType.DMA((10,)), pltpu.SMEM((1, 1, 9), jnp.int32), ints(72), ints(8), ints(32)],
        flops=5 * 10**9,
    )
    low = swap(jnp.concatenate([far[0:3].reshape(96, 128), rotor, rotor], axis=0), "gx", 1)
    high = swap_next(jnp.concatenate([far[3:6].reshape(96, 128), rotor], axis=0), "gx")
    own, acc = call(
        make_near_gather(count_y, 8, 4),
        "near_gather",
        [((3, 4, 8, 128), F32, VMEM), ((512, 512), F32, VMEM)],
        [SMEM] + [VMEM] * 4,
        (mine, table, src, weight, dst),
        [ints(48), ints(8)],
        flops=4 * 10**9,
    )
    rotor = rotor + high[96:]
    own = own.reshape(96, 128)

    def y_payload(t):
        return jnp.concatenate([part[t * 32 : t * 32 + 32] for part in (low, own, high)] + [rotor], axis=0)

    first = swap(y_payload(0), "gy", 1)
    rotor = rotor + first[96:]
    second = swap_next(y_payload(2), "gy")
    (edge,) = call(
        make_level_edges(count_y),
        "level_edges",
        [((144, 512), F32, VMEM)],
        [SMEM] + [VMEM] * 4,
        (mine, acc, low, high, dst),
        [pltpu.VMEM((2, 4, 8, 128), F32), ints(48), ints(8)],
        flops=4 * 10**9,
    )
    (edge,) = call(
        make_core_edges(count_y),
        "core_edges",
        [((144, 512), F32, VMEM)],
        [SMEM] + [VMEM] * 3,
        (mine, edge, first, dst),
        [pltpu.VMEM((3, 4, 8, 128), F32), ints(48), ints(8)],
        flops=4 * 10**9,
    )
    rotor = rotor + second[96:]
    for axis, count in (("gx", count_x), ("gy", count_y)):
        step = 4
        while step < count:
            rotor = rotor + swap(rotor, axis, step)
            step *= 2
    lists = pltpu.VMEM((8, 4, 8, 128), F32)
    face_x, face_y = ((3, 64, 128), F32, VMEM), ((3, 8, 128), F32, VMEM)
    edge, xa, xb, ya, yb = call(
        make_edge_scatter(count_y),
        "edge_scatter",
        [((3, 128, 128), F32, VMEM), face_x, face_x, face_y, face_y],
        [SMEM] + [VMEM] * 4,
        (mine, edge, second, dst, vel),
        [pltpu.VMEM((144, 512), F32), pltpu.VMEM((3, 4, 8, 128), F32), ints(48), ints(8)],
        flops=4 * 10**9,
    )
    xb = swap_next(xb.reshape(192, 128), "gx")
    rotor, ya, yb = lax.optimization_barrier((rotor, ya, yb))
    xa = swap(jnp.concatenate([xa.reshape(192, 128), rotor], axis=0), "gx", 1)
    ya = swap(ya, "gy", 1)
    yb = swap_next(yb, "gy")
    (inner,) = call(
        make_inner_scatter(count_y),
        "inner_scatter",
        [((3, 384, 128), F32, VMEM)],
        [SMEM] + [VMEM] * 7,
        (mine, acc, low, high, first, second, dst, vel),
        [pltpu.VMEM((384, 512), F32), lists, ints(96), ints(8)],
        flops=6 * 10**9,
    )
    xa, xb, ya, yb = lax.optimization_barrier((xa, xb, ya, yb))
    rotor = rotor + xa[192:]
    updated, forcing = call(
        make_stencil(count_y),
        "stencil",
        [((3, 8, 64, 128), F32, HBM), ((3, 512, 128), F32, HBM)],
        [SMEM] + [VMEM] * 11,
        (mine, edge, inner, tile, cell, coef, pts, rotor, xa, xb, ya, yb),
        [pltpu.VMEM((3, 8, 64, 128), F32), pltpu.VMEM((3, 512, 128), F32), pltpu.VMEM((turbines, 128), F32)]
        + [pltpu.SemaphoreType.DMA((9,)), ints(32)],
    )
    return updated, forcing.reshape(velocity.shape)


def solution(mesh):
    grid = P("gx", "gy", None)
    lists = P("gx", "gy", None, None)
    field = P(None, "gx", "gy", None)
    return jax.shard_map(
        body,
        mesh=mesh,
        in_specs=(field, grid, lists, lists, lists, P(), P(), P()),
        out_specs=(field, field),
        check_vma=False,
    )
```

```python
import jax
import jax.numpy as jnp
from jax import lax
from jax.experimental import pallas as pl
from jax.experimental.pallas import tpu as pltpu
from jax.sharding import PartitionSpec as P

F32 = jnp.float32
BF16 = jnp.bfloat16
VMEM = pl.BlockSpec(memory_space=pltpu.VMEM)
SMEM = pl.BlockSpec(memory_space=pltpu.SMEM)
HBM = pl.BlockSpec(memory_space=pltpu.HBM)


def halves(value):
    high = value.astype(BF16)
    low = (value - high.astype(F32)).astype(BF16)
    return high, low


def one_hot(extent, index):
    rows = lax.broadcasted_iota(jnp.int32, (extent, index.shape[1]), 0)
    return jnp.where(rows == index, 1.0, 0.0).astype(BF16)


def pick(table, cell):
    key = (cell & 127) | (((cell >> 15) & 1) << 7)
    place = (cell >> 7) & 255
    hot = one_hot(256, key)
    hot = jnp.concatenate([hot, hot], axis=0)
    here = lax.broadcasted_iota(jnp.int32, (256, cell.shape[1]), 0) == place
    out = []
    for c in range(3):
        found = jnp.dot(table[c], hot, preferred_element_type=F32)
        out.append(jnp.sum(jnp.where(here, found, 0.0), axis=0, keepdims=True))
    return out


def spread(extent, row, level, values):
    hot = one_hot(extent, row)
    at_level = lax.broadcasted_iota(jnp.int32, (128, level.shape[1]), 0) == level
    high, low = [], []
    for value in values:
        vh = value.astype(BF16).astype(F32)
        high.append(jnp.where(at_level, vh, 0.0).astype(BF16))
        low.append(jnp.where(at_level, value - vh, 0.0).astype(BF16))
    left = jnp.concatenate([hot, hot], axis=1)
    right = jnp.concatenate([jnp.concatenate(high, axis=0), jnp.concatenate(low, axis=0)], axis=1)
    return lax.dot_general(left, right, (((1,), (1,)), ((), ())), preferred_element_type=F32)


def sides(mine_ref, count_y):
    mine = mine_ref[0]
    return 1 - 2 * ((mine // count_y) & 1), 1 - 2 * (mine & 1)


def list_blocks(lists, listed):
    total = jnp.int32(0)
    for used, tag in lists:
        for j in range(8):
            listed[total + j] = tag * 8 + j
        total = total + ((used + 127) >> 7)
    return total


def run_chunks(total, large, small, chunk):
    many = (total + small - 1) // large

    def big(i, carry):
        chunk(i * large, large)
        return carry

    lax.fori_loop(0, many, big, 0)

    def rest(i, carry):
        chunk(many * large + i * small, small)
        return carry

    lax.fori_loop(0, jnp.maximum(total - many * large + small - 1, 0) // small, rest, 0)


def gather_lists(table, total, large, small, listed, direction, src_ref, w_ref, out_ref):
    for k in range(large):
        listed[total + k] = listed[total - 1]

    def chunk(first, width):
        blocks = [listed[first + k] for k in range(width)]
        rows = [direction[b >> 3] * 8 + (b & 7) for b in blocks]
        cell = jnp.concatenate([src_ref[pl.ds(r, 1), :] for r in rows], axis=1)
        found = pick(table, cell)
        for k, (b, r) in enumerate(zip(blocks, rows)):
            j = b & 7
            weight = w_ref[pl.ds(r, 1), :]
            for c in range(3):
                out_ref[b >> 3, c, pl.ds(j, 1), :] = found[c][:, k * 128 : (k + 1) * 128] * weight
            out_ref[b >> 3, 3, pl.ds(j, 1), :] = weight

    run_chunks(total, large, small, chunk)


def make_far_gather(count_y, large, small):
    def kernel(
        mine_ref, cnt_hbm, vel_hbm, src_hbm, w_hbm, dst_hbm, tile_hbm, cell_hbm, coef_hbm,
        out_ref, table, vel_ref, src_ref, w_ref, dst_ref, tile_ref, cell_ref, coef_ref, pts_ref, rot_ref,
        sem, cnt_ref, listed, direction, tlist,
    ):
        half = vel_ref.shape[1] // 2
        pairs = [(cnt_hbm, cnt_ref), (src_hbm, src_ref), (w_hbm, w_ref), (tile_hbm, tile_ref)]
        pairs += [(vel_hbm.at[c], vel_ref.at[c]) for c in range(3)]
        pairs += [(cell_hbm, cell_ref), (coef_hbm, coef_ref), (dst_hbm, dst_ref)]
        copies = [pltpu.make_async_copy(a, b, sem.at[k]) for k, (a, b) in enumerate(pairs)]
        for copy in copies:
            copy.start()
        out_ref[...] = jnp.zeros_like(out_ref)
        pts_ref[...] = jnp.zeros_like(pts_ref)
        for copy in copies[:4]:
            copy.wait()
        n_turb = active_turbines(tile_ref, mine_ref[0], tlist)
        slot = lax.broadcasted_iota(jnp.int32, (8, 128), 0) * 128 + lax.broadcasted_iota(jnp.int32, (8, 128), 1)
        for d in range(9):
            part = slice(d * 8, d * 8 + 8)
            w_ref[part, :] = jnp.where(slot < cnt_ref[0, 0, d], w_ref[part, :], 0.0)
        side_x, side_y = sides(mine_ref, count_y)
        lists = []
        for s in range(2):
            for t in range(3):
                d = 3 * (side_x * (1 - 2 * s) + 1) + side_y * (1 - t) + 1
                direction[3 * s + t] = d
                lists.append((cnt_ref[0, 0, d], 3 * s + t))
        total = list_blocks(lists, listed)
        for c in range(3):
            copies[4 + c].wait()
            for piece in range(2):
                high, low = halves(vel_ref[c, piece * half : (piece + 1) * half, :])
                table[c, :, piece * 128 : (piece + 1) * 128] = high
                table[c, :, 256 + piece * 128 : 256 + (piece + 1) * 128] = low
        for copy in copies[7:]:
            copy.wait()
        gather_lists(table, total, large, small, listed, direction, src_ref, w_ref, out_ref)
        gather_points(mine_ref[0], n_turb, table, tile_ref, cell_ref, pts_ref, rot_ref, tlist)

    return kernel


def active_turbines(tile_ref, mine, listed):
    turbines = tile_ref.shape[0]
    owned = jnp.where(tile_ref[...] == mine, 1.0, 0.0)
    found = jnp.max(owned, axis=1, keepdims=True)
    total = jnp.int32(0)
    for t in range(turbines):
        listed[total] = t
        total = total + jnp.where(found[t, 0] > 0.5, 1, 0)
    listed[total] = 0
    return total


def diagonal(turbines):
    shape = (turbines, 128)
    return lax.broadcasted_iota(jnp.int32, shape, 0) == lax.broadcasted_iota(jnp.int32, shape, 1)


def gather_points(mine, n_turb, table, tile_ref, cell_ref, pts_ref, rot_ref, tlist):
    turbines, points = tile_ref.shape

    def turbine(i, carry):
        pair = [tlist[2 * i], tlist[2 * i + 1]]
        cell = jnp.concatenate([cell_ref[pl.ds(t, 1), :] for t in pair], axis=1)
        found = pick(table, cell)
        for k, t in enumerate(pair):
            owned = tile_ref[pl.ds(t, 1), :] == mine
            for c in range(3):
                pts_ref[c, pl.ds(t, 1), :] = jnp.where(owned, found[c][:, k * points : (k + 1) * points], 0.0)
        return carry

    lax.fori_loop(0, (n_turb + 1) >> 1, turbine, 0)
    sums = jnp.broadcast_to(jnp.sum(pts_ref[0], axis=1, keepdims=True), (turbines, 128))
    row = jnp.sum(jnp.where(diagonal(turbines), sums, 0.0), axis=0, keepdims=True)
    rot_ref[...] = jnp.broadcast_to(row, rot_ref.shape)


def used_slots(weight):
    return jnp.sum(jnp.where(weight != 0.0, 1.0, 0.0)).astype(jnp.int32)


def make_near_gather(count_y, large, small):
    def kernel(mine_ref, table, src_ref, w_ref, dst_ref, out_ref, acc, listed, direction):
        out_ref[...] = jnp.zeros_like(out_ref)
        acc[...] = jnp.zeros_like(acc)
        _, side_y = sides(mine_ref, count_y)
        used = [used_slots(w_ref[d * 8 : d * 8 + 8, :]) for d in (3, 4, 5)]
        last = jnp.where(side_y > 0, used[0], used[2])
        lists = [(jnp.where(side_y > 0, used[2], used[0]), 0), (used[1], 1), (last, 2)]
        for t in range(3):
            direction[t] = 3 + side_y * (1 - t) + 1
        total = list_blocks(lists, listed)
        gather_lists(table, total, large, small, listed, direction, src_ref, w_ref, out_ref)
        direction[0] = 4
        scatter_lists(out_ref.at[1:2], 1, direction, dst_ref, listed, acc, 512, lambda row: row, 8, 4)

    return kernel


def scatter_lists(val, n_lists, direction, dst_ref, listed, acc, extent, place, large, small):
    lists = []
    for q in range(n_lists):
        lists.append((used_slots(val[q, 3]), q))
    total = list_blocks(lists, listed)
    for k in range(large):
        listed[total + k] = 0

    def chunk(first, width):
        cells, vals = [], [[], [], [], []]
        for k in range(width):
            b = listed[first + k]
            q, j = b >> 3, b & 7
            keep = jnp.where(first + k < total, 1.0, 0.0)
            cells.append(dst_ref[pl.ds(direction[q] * 8 + j, 1), :])
            for c in range(4):
                vals[c].append(val[q, c, pl.ds(j, 1), :] * keep)
        cell = jnp.concatenate(cells, axis=1)
        vals = [jnp.concatenate(v, axis=1) for v in vals]
        acc[...] += spread(extent, place((cell >> 7) & 511), cell & 127, vals)

    run_chunks(total, large, small, chunk)


def load_level_lists(side_x, low_ref, high_ref, start, val, direction):
    for q, ref in enumerate((low_ref, high_ref)):
        for c in range(4):
            val[start + q, c] = ref[32 + c * 8 : 40 + c * 8, :]
        direction[start + q] = 3 * (side_x * (2 * q - 1) + 1) + 1


def make_level_edges(count_y):
    def kernel(mine_ref, base_ref, low_ref, high_ref, dst_ref, edge, val, listed, direction):
        side_x, _ = sides(mine_ref, count_y)
        load_level_lists(side_x, low_ref, high_ref, 0, val, direction)
        edge[...] = edge_rows(base_ref, None, slice(None))
        scatter_lists(val, 2, direction, dst_ref, listed, edge, 144, edge_place, 12, 4)

    return kernel


def make_core_edges(count_y):
    def kernel(mine_ref, base_ref, first_ref, dst_ref, edge, val, listed, direction):
        side_x, side_y = sides(mine_ref, count_y)
        load_later_lists(side_x, -side_y, first_ref, 0, val, direction)
        edge[...] = base_ref[...]
        scatter_lists(val, 3, direction, dst_ref, listed, edge, 144, edge_place, 12, 4)

    return kernel


def load_later_lists(side_x, from_y, ref, start, val, direction):
    for s in range(3):
        for c in range(4):
            at = (s * 4 + c) * 8
            val[start + s, c] = ref[at : at + 8, :]
        direction[start + s] = 3 * (side_x * (s - 1) + 1) + from_y + 1


def corrected(acc, vel, c):
    return (1.0 - acc[:, 384:512]) * vel - acc[:, c * 128 : (c + 1) * 128]


def edge_rows(ref, c, columns):
    at = (lambda r: ref[r, columns]) if c is None else (lambda r: ref[c, r, columns])
    spare = [at(slice(0, 2))]
    low = [at(slice(x * 64, x * 64 + 1)) for x in range(1, 7)]
    high = [at(slice(x * 64 + 63, x * 64 + 64)) for x in range(1, 7)]
    return jnp.concatenate([at(slice(0, 64)), at(slice(448, 512))] + low + spare + high + spare, axis=0)


def edge_place(row):
    x, y = row >> 6, row & 63
    inside = jnp.where(y == 0, 127 + x, jnp.where(y == 63, 135 + x, 1024))
    return jnp.where(x == 0, y, jnp.where(x == 7, 64 + y, inside))


def make_edge_scatter(count_y):
    def kernel(
        mine_ref, base_ref, second_ref, dst_ref, vel_ref,
        cor_ref, xa_ref, xb_ref, ya_ref, yb_ref, acc, val, listed, direction,
    ):
        side_x, side_y = sides(mine_ref, count_y)
        load_later_lists(side_x, side_y, second_ref, 0, val, direction)
        acc[...] = base_ref[...]
        scatter_lists(val, 3, direction, dst_ref, listed, acc, 144, edge_place, 12, 4)
        for c in range(3):
            cor = corrected(acc, edge_rows(vel_ref, c, slice(None)), c)
            cor_ref[c] = cor[0:128]
            xa_ref[c] = jnp.where(side_x > 0, cor[64:128], cor[0:64])
            xb_ref[c] = jnp.where(side_x > 0, cor[0:64], cor[64:128])
            low = jnp.concatenate([cor[0:1], cor[128:134], cor[64:65]], axis=0)
            high = jnp.concatenate([cor[63:64], cor[136:142], cor[127:128]], axis=0)
            ya_ref[c] = jnp.where(side_y > 0, high, low)
            yb_ref[c] = jnp.where(side_y > 0, low, high)

    return kernel


def make_inner_scatter(count_y):
    def kernel(mine_ref, base_ref, low_ref, high_ref, first_ref, second_ref, dst_ref, vel_ref, cor_ref, acc, val, listed, direction):
        side_x, side_y = sides(mine_ref, count_y)
        load_later_lists(side_x, -side_y, first_ref, 0, val, direction)
        load_later_lists(side_x, side_y, second_ref, 3, val, direction)
        load_level_lists(side_x, low_ref, high_ref, 6, val, direction)
        acc[...] = base_ref[64:448, :]
        scatter_lists(val, 8, direction, dst_ref, listed, acc, 384, lambda row: row - 64, 12, 4)
        for c in range(3):
            cor_ref[c] = corrected(acc, vel_ref[c, 64:448, :], c)

    return kernel


def add_forces(mine, tile_ref, cell_ref, coef_ref, pts_ref, rot_ref, column, out_ref, tlist):
    out_ref[...] = jnp.zeros_like(out_ref)
    turbines = tile_ref.shape[0]
    sums = jnp.broadcast_to(rot_ref[0:1, :], (turbines, 128))
    sums = jnp.sum(jnp.where(diagonal(turbines), sums, 0.0), axis=1, keepdims=True)
    column[...] = jnp.broadcast_to(sums, (turbines, 128))
    n_turb = active_turbines(tile_ref, mine, tlist)
    points = tile_ref.shape[1]

    def turbine(i, carry):
        pair = [tlist[2 * i], tlist[2 * i + 1]]
        cell = jnp.concatenate([cell_ref[pl.ds(t, 1), :] for t in pair], axis=1)
        force = [[], [], []]
        for k, t in enumerate(pair):
            keep = jnp.where(2 * i + k < n_turb, 1.0 / points, 0.0)
            scale = -coef_ref[pl.ds(t, 1), :] * (column[pl.ds(t, 1), 0:1] * keep)
            for c in range(3):
                force[c].append(scale * pts_ref[c, pl.ds(t, 1), :])
        force = [jnp.concatenate(f, axis=1) for f in force]
        got = spread(512, (cell >> 7) & 511, cell & 127, force)
        for c in range(3):
            out_ref[c] += got[:, c * 128 : (c + 1) * 128]
        return carry

    lax.fori_loop(0, (n_turb + 1) >> 1, turbine, 0)


def make_stencil(count_y):
    def kernel(
        mine_ref, edge_ref, inner_ref, tile_ref, cell_ref, coef_ref, pts_ref, rot_ref, xa_ref, xb_ref, ya_ref, yb_ref,
        out_hbm, frc_hbm, out_ref, frc_ref, column, sem, tlist,
    ):
        add_forces(mine_ref[0], tile_ref, cell_ref, coef_ref, pts_ref, rot_ref, column, frc_ref, tlist)
        given = pltpu.make_async_copy(frc_ref, frc_hbm, sem.at[8])
        given.start()
        side_x, side_y = sides(mine_ref, count_y)
        lane = lax.broadcasted_iota(jnp.int32, (64, 128), 1)

        def slab(c, x):
            if x < 0:
                return jnp.where(side_x > 0, xb_ref[c * 64 : c * 64 + 64, :], xa_ref[c * 64 : c * 64 + 64, :])
            if x > 7:
                return jnp.where(side_x > 0, xa_ref[c * 64 : c * 64 + 64, :], xb_ref[c * 64 : c * 64 + 64, :])
            ref, at = (inner_ref, x - 1) if 1 <= x < 7 else (edge_ref, 0 if x == 0 else 1)
            return ref[c, at * 64 : at * 64 + 64, :]

        copies = []
        for x in range(8):
            now = [slab(c, x) for c in range(3)]
            up = [0.03 - 0.1 * v for v in now]
            down = [0.03 + 0.1 * v for v in now]
            up[2] = jnp.where(lane == 127, 0.0, up[2])
            down[2] = jnp.where(lane == 0, 0.0, down[2])
            for c in range(3):
                u = now[c]
                west, east = slab(c, x - 1), slab(c, x + 1)
                ya, yb = ya_ref[c, x : x + 1, :], yb_ref[c, x : x + 1, :]
                south = jnp.concatenate([jnp.where(side_y > 0, yb, ya), u[:-1]], axis=0)
                north = jnp.concatenate([u[1:], jnp.where(side_y > 0, ya, yb)], axis=0)
                upper, lower = pltpu.roll(u, 127, 1), pltpu.roll(u, 1, 1)
                moved = (up[0] * east + down[0] * west) + (up[1] * north + down[1] * south)
                moved = moved + (up[2] * upper + down[2] * lower)
                out_ref[c, x] = 0.82 * u + (moved + 0.2 * frc_ref[c, x * 64 : x * 64 + 64, :])
            copies.append(pltpu.make_async_copy(out_ref.at[:, x], out_hbm.at[:, x], sem.at[x]))
            copies[-1].start()
        for copy in copies:
            copy.wait()
        given.wait()

    return kernel


def swap(value, axis, step):
    count = lax.axis_size(axis)
    return lax.ppermute(value, axis, [(i, i ^ step) for i in range(count)])


def swap_next(value, axis):
    count = lax.axis_size(axis)
    return lax.ppermute(value, axis, [(i, (i - 1 if i % 2 == 0 else i + 1) % count) for i in range(count)])


def call(kernel, name, outs, ins, args, scratch=(), flops=10**9, limit=32):
    return pl.pallas_call(
        kernel,
        out_shape=tuple(jax.ShapeDtypeStruct(shape, dtype) for shape, dtype, _ in outs),
        in_specs=ins,
        out_specs=tuple(spec for _, _, spec in outs),
        scratch_shapes=list(scratch),
        compiler_params=pltpu.CompilerParams(vmem_limit_bytes=limit << 20),
        cost_estimate=pl.CostEstimate(flops=flops, bytes_accessed=10**5, transcendentals=0),
        name=name,
    )(*args)


def body(velocity, counts, src_cell, weights, dst_cell, blade_tile, blade_cell, blade_coef):
    vel = velocity.reshape(3, 512, 128)
    src = src_cell.reshape(72, 128)
    weight = weights.reshape(72, 128)
    dst = dst_cell.reshape(72, 128)
    turbines, points = blade_cell.shape
    count_x, count_y = lax.axis_size("gx"), lax.axis_size("gy")
    mine = (lax.axis_index("gx") * count_y + lax.axis_index("gy")).reshape(1).astype(jnp.int32)
    ints = lambda n: pltpu.SMEM((n,), jnp.int32)

    whole = ((72, 128), jnp.int32, VMEM)
    ints_t = (blade_tile.shape, jnp.int32, VMEM)
    given = (counts, vel, src, weight, dst, blade_tile, blade_cell, blade_coef)
    far, table, vel, src, weight, dst, tile, cell, coef, pts, rotor = call(
        make_far_gather(count_y, 12, 4),
        "far_gather",
        [((6, 4, 8, 128), F32, VMEM), ((3, 256, 512), BF16, VMEM), ((3, 512, 128), F32, VMEM), whole]
        + [((72, 128), F32, VMEM), whole, ints_t, ints_t, (blade_tile.shape, F32, VMEM)]
        + [((3, turbines, points), F32, VMEM), ((8, 128), F32, VMEM)],
        [SMEM] + [HBM] * 8,
        (mine,) + tuple(pltpu.with_memory_space_constraint(v, pltpu.HBM) for v in given),
        [pltpu.SemaphoreType.DMA((10,)), pltpu.SMEM((1, 1, 9), jnp.int32), ints(72), ints(8), ints(32)],
        flops=5 * 10**9,
    )
    low = swap(jnp.concatenate([far[0:3].reshape(96, 128), rotor, rotor], axis=0), "gx", 1)
    high = swap_next(jnp.concatenate([far[3:6].reshape(96, 128), rotor], axis=0), "gx")
    own, acc = call(
        make_near_gather(count_y, 12, 4),
        "near_gather",
        [((3, 4, 8, 128), F32, VMEM), ((512, 512), F32, VMEM)],
        [SMEM] + [VMEM] * 4,
        (mine, table, src, weight, dst),
        [ints(48), ints(8)],
        flops=4 * 10**9,
    )
    rotor = rotor + high[96:]
    own = own.reshape(96, 128)

    def y_payload(t):
        return jnp.concatenate([part[t * 32 : t * 32 + 32] for part in (low, own, high)] + [rotor], axis=0)

    first = swap(y_payload(0), "gy", 1)
    rotor = rotor + first[96:]
    second = swap_next(y_payload(2), "gy")
    (edge,) = call(
        make_level_edges(count_y),
        "level_edges",
        [((144, 512), F32, VMEM)],
        [SMEM] + [VMEM] * 4,
        (mine, acc, low, high, dst),
        [pltpu.VMEM((2, 4, 8, 128), F32), ints(48), ints(8)],
        flops=4 * 10**9,
    )
    (edge,) = call(
        make_core_edges(count_y),
        "core_edges",
        [((144, 512), F32, VMEM)],
        [SMEM] + [VMEM] * 3,
        (mine, edge, first, dst),
        [pltpu.VMEM((3, 4, 8, 128), F32), ints(48), ints(8)],
        flops=4 * 10**9,
    )
    rotor = rotor + second[96:]
    for axis, count in (("gx", count_x), ("gy", count_y)):
        step = 4
        while step < count:
            rotor = rotor + swap(rotor, axis, step)
            step *= 2
    lists = pltpu.VMEM((8, 4, 8, 128), F32)
    face_x, face_y = ((3, 64, 128), F32, VMEM), ((3, 8, 128), F32, VMEM)
    edge, xa, xb, ya, yb = call(
        make_edge_scatter(count_y),
        "edge_scatter",
        [((3, 128, 128), F32, VMEM), face_x, face_x, face_y, face_y],
        [SMEM] + [VMEM] * 4,
        (mine, edge, second, dst, vel),
        [pltpu.VMEM((144, 512), F32), pltpu.VMEM((3, 4, 8, 128), F32), ints(48), ints(8)],
        flops=4 * 10**9,
    )
    xb = swap_next(xb.reshape(192, 128), "gx")
    rotor, ya, yb = lax.optimization_barrier((rotor, ya, yb))
    xa = swap(jnp.concatenate([xa.reshape(192, 128), rotor], axis=0), "gx", 1)
    ya = swap(ya, "gy", 1)
    yb = swap_next(yb, "gy")
    (inner,) = call(
        make_inner_scatter(count_y),
        "inner_scatter",
        [((3, 384, 128), F32, VMEM)],
        [SMEM] + [VMEM] * 7,
        (mine, acc, low, high, first, second, dst, vel),
        [pltpu.VMEM((384, 512), F32), lists, ints(96), ints(8)],
        flops=6 * 10**9,
    )
    xa, xb, ya, yb = lax.optimization_barrier((xa, xb, ya, yb))
    rotor = rotor + xa[192:]
    updated, forcing = call(
        make_stencil(count_y),
        "stencil",
        [((3, 8, 64, 128), F32, HBM), ((3, 512, 128), F32, HBM)],
        [SMEM] + [VMEM] * 11,
        (mine, edge, inner, tile, cell, coef, pts, rotor, xa, xb, ya, yb),
        [pltpu.VMEM((3, 8, 64, 128), F32), pltpu.VMEM((3, 512, 128), F32), pltpu.VMEM((turbines, 128), F32)]
        + [pltpu.SemaphoreType.DMA((9,)), ints(32)],
    )
    return updated, forcing.reshape(velocity.shape)


def solution(mesh):
    grid = P("gx", "gy", None)
    lists = P("gx", "gy", None, None)
    field = P(None, "gx", "gy", None)
    return jax.shard_map(
        body,
        mesh=mesh,
        in_specs=(field, grid, lists, lists, lists, P(), P(), P()),
        out_specs=(field, field),
        check_vma=False,
    )
```
